256 devices in a mesh: dp: 32 (over z, x), mp: 8 (over y, core).
Axes of the slice: x: 4, y: 4, z: 8, core: 2. Of those that a mesh axis runs over, the one named last changes fastest.
Arguments:
- input_steps: bfloat16 [4, 3072, 8192], P(None, 'dp', 'mp'), may hold values from -6 to 6
- gate_steps: bfloat16 [4, 3072, 8192], P(None, 'dp', 'mp'), may hold values from -6 to 6
- conv_state: bfloat16 [3072, 3, 8192], P('dp', None, 'mp'), may hold values from -6 to 6
- ssm_state: bfloat16 [3072, 16, 8192], P('dp', None, 'mp'), may hold values from -6 to 6
- new_slot: int32 [3072], replicated, may hold values from 0 to 3071, as said below
- remaining: int32 [3072], replicated, may hold values from 1 to 4
- conv_weight: float32 [4, 8192], P(None, 'mp'), may hold values from -3 to 3
- conv_bias: float32 [8192], P('mp'), may hold values from -3 to 3
- coef_proj: bfloat16 [8192, 544], P('mp', 'dp'), may hold values from -0.0625 to 0.0625
- delta_proj: bfloat16 [512, 8192], P('dp', 'mp'), may hold values from -0.25 to 0.25
- delta_bias: float32 [8192], P('mp'), may hold values from -4 to -1
- decay_log: float32 [16, 8192], P(None, 'mp'), may hold values from -1 to 2
- skip_gain: float32 [8192], P('mp'), may hold values from 0.5 to 1.5
- out_proj: bfloat16 [8192, 4096], P('mp', 'dp'), may hold values from -0.0625 to 0.0625
Outputs:
- layer_out: bfloat16 [4, 3072, 4096], P(None, 'dp', 'mp')
- conv_final: bfloat16 [3072, 3, 8192], P('dp', None, 'mp')
- ssm_final: bfloat16 [3072, 16, 8192], P('dp', None, 'mp')
The draws below stay inside these ranges and needn't reach their ends.
Inputs may be any that keep to these rules, and one draw needn't show every extreme that they name: new_slot is a permutation of the rollouts. Each group hands to every group 0, 3 or 6 of its rollouts: 6 to exactly one group and 0 to exactly one group; each group receives 6 from exactly one group and 0 from exactly one group.
All inputs are finite; a program needn't handle non-finite values.
Results may differ from the reference program's by a relative error of at most 0.03.
Values may be sent and summed in bfloat16 or wider, within the bound.
No kernel may reach another device: no remote copies, remote signals or barrier semaphores. Data moves between devices by JAX's collectives and lax.ppermute only.
A program may use at most 128 MiB of HBM per device.

```python
import jax
import jax.numpy as jnp
from jax import lax

E_WIN = 8192
D_OUT = 4096
DT_RANK = 512
STATE = 16
TAPS = 4
STEPS = 4
ROWS = 96
TOTAL = 3072
N_DP = 32
N_MP = 8


def draw_new_slot(key, part):
    groups = N_DP
    base = ROWS // N_DP
    base_key = jax.random.fold_in(key, 7)
    key_sigma, key_order, key_within = jax.random.split(base_key, 3)
    sigma = jax.random.permutation(key_sigma, groups).astype(jnp.int32)
    tau = jnp.roll(sigma, -1)
    column = jnp.arange(groups, dtype=jnp.int32)
    counts = base + base * (column[None, :] == sigma[:, None]).astype(jnp.int32) - base * (column[None, :] == tau[:, None]).astype(jnp.int32)
    cumulative = jnp.cumsum(counts, axis=1)
    position = jnp.arange(ROWS, dtype=jnp.int32)
    target = jnp.sum((cumulative[:, None, :] <= position[None, :, None]).astype(jnp.int32), axis=2)
    start_source = cumulative - counts
    before = jnp.cumsum(counts, axis=0) - counts
    offset = jnp.take_along_axis(before, target, axis=1) + position[None, :] - jnp.take_along_axis(start_source, target, axis=1)
    within_keys = jax.random.split(key_within, groups)
    shuffles = jax.vmap(lambda sub_key: jax.random.permutation(sub_key, ROWS).astype(jnp.int32))(within_keys)
    final_slot = shuffles[target.reshape(-1), offset.reshape(-1)].reshape(groups, ROWS)
    values = target * ROWS + final_slot
    order_keys = jax.random.split(key_order, groups)
    orders = jax.vmap(lambda sub_key: jax.random.permutation(sub_key, ROWS).astype(jnp.int32))(order_keys)
    group_index = jnp.broadcast_to(column[:, None], (groups, ROWS))
    result = jnp.zeros((groups, ROWS), jnp.int32).at[group_index, orders].set(values)
    return result.reshape(groups * ROWS)


def set_ends(values, own_key, least, high):
    longest = values.shape.index(max(values.shape))
    spots = []
    for shift in (0, 1):
        where = [jax.random.randint(jax.random.fold_in(own_key, axis), (), 0, length) for axis, length in enumerate(values.shape)]
        where[longest] = (where[longest] + shift) % values.shape[longest]
        spots.append(tuple(where))
    return values.at[spots[0]].set(least).at[spots[1]].set(high)


def levels(own_key, extent, shards, least, high):
    level = 1.0
    for dim, shards_of in shards:
        steps = jax.random.uniform(jax.random.fold_in(jax.random.fold_in(own_key, 6), dim), (shards_of,), jnp.float32, least / len(shards), high / len(shards))
        level = level * jnp.repeat(jnp.exp(steps), extent[dim] // shards_of).reshape((-1,) + (1,) * (len(extent) - 1 - dim))
    return level


def scatter_about(own_key, shape, scale, most, cuts=(), kind=jnp.bfloat16):
    array = scale * jax.random.normal(own_key, shape, jnp.float32)
    if cuts:
        array = array * levels(own_key, shape, cuts, -0.22, 0.18)
    return jnp.clip(array, -most, most).astype(kind)


def setup_inputs(seed: int = 0) -> dict:
    key_list = jax.random.split(jax.random.key(seed), 15)
    return {
        "input_steps": scatter_about(key_list[0], (STEPS, TOTAL, E_WIN), 1.0, 6.0, ((1, 32), (2, 8))),
        "gate_steps": scatter_about(key_list[1], (STEPS, TOTAL, E_WIN), 1.0, 6.0, ((1, 32), (2, 8))),
        "conv_state": scatter_about(key_list[2], (TOTAL, TAPS - 1, E_WIN), 1.0, 6.0, ((0, 32), (2, 8))),
        "ssm_state": scatter_about(key_list[3], (TOTAL, STATE, E_WIN), 1.0, 6.0, ((0, 32), (2, 8))),
        "new_slot": draw_new_slot(jax.random.fold_in(key_list[14], 71), 0),
        "remaining": set_ends(jax.random.randint(key_list[5], (TOTAL,), 1, STEPS + 1), jax.random.fold_in(key_list[5], 1), 1, STEPS).astype(jnp.int32),
        "conv_weight": scatter_about(key_list[6], (TAPS, E_WIN), 0.5, 3.0, ((1, 8),), jnp.float32),
        "conv_bias": scatter_about(key_list[7], (E_WIN,), 0.5, 3.0, ((0, 8),), jnp.float32),
        "coef_proj": scatter_about(key_list[8], (E_WIN, DT_RANK + 2 * STATE), E_WIN ** -0.5, 0.0625, ((0, 8), (1, 32))),
        "delta_proj": scatter_about(key_list[9], (DT_RANK, E_WIN), DT_RANK ** -0.5, 0.25, ((0, 32), (1, 8))),
        "delta_bias": jnp.clip(-4.0 + 3.0 * jax.random.uniform(key_list[10], (E_WIN,), jnp.float32) ** levels(key_list[10], (E_WIN,), ((0, 8),), -0.2, 0.2), -4.0, -1.0),
        "decay_log": jnp.clip(-1.0 + 3.0 * jax.random.uniform(key_list[11], (STATE, E_WIN), jnp.float32) ** levels(key_list[11], (STATE, E_WIN), ((1, 8),), -0.2, 0.2), -1.0, 2.0),
        "skip_gain": jnp.clip(0.5 + 1.0 * jax.random.uniform(key_list[12], (E_WIN,), jnp.float32) ** levels(key_list[12], (E_WIN,), ((0, 8),), -0.2, 0.2), 0.5, 1.5),
        "out_proj": scatter_about(key_list[13], (E_WIN, D_OUT), E_WIN ** -0.5, 0.0625, ((0, 8), (1, 32))),
    }


def reference(input_steps, gate_steps, conv_state, ssm_state, new_slot, remaining, conv_weight, conv_bias, coef_proj, delta_proj, delta_bias, decay_log, skip_gain, out_proj):
    total_rows = new_slot.shape[0]
    channels = input_steps.shape[2]
    inverse = jnp.zeros((total_rows,), jnp.int32).at[new_slot].set(jnp.arange(total_rows, dtype=jnp.int32))
    conv_moved = conv_state[inverse]
    ssm_moved = ssm_state[inverse]
    remain_moved = remaining[inverse]
    decay_rate = -jnp.exp(decay_log)
    inputs = (
        input_steps.reshape(STEPS, N_DP, ROWS, channels).transpose(1, 0, 2, 3),
        gate_steps.reshape(STEPS, N_DP, ROWS, channels).transpose(1, 0, 2, 3),
        conv_moved.reshape(N_DP, ROWS, TAPS - 1, channels),
        ssm_moved.reshape(N_DP, ROWS, STATE, channels),
        remain_moved.reshape(N_DP, ROWS),
    )

    def advance(group_rows):
        input_group, gate_group, window_in, state_in, remain_group = group_rows
        window = window_in.astype(jnp.float32)
        hidden = state_in.astype(jnp.float32)
        results = []
        for position in range(STEPS):
            active = (remain_group > position)[:, None]
            current = input_group[position].astype(jnp.float32)
            full_window = jnp.concatenate([window, current[:, None, :]], axis=1)
            conv_out = jnp.sum(full_window * conv_weight[None], axis=1) + conv_bias
            activated = jax.nn.silu(conv_out)
            low_rank = jnp.dot(activated.astype(jnp.bfloat16), coef_proj, preferred_element_type=jnp.float32)
            step_in = low_rank[:, :DT_RANK].astype(jnp.bfloat16)
            input_coef = low_rank[:, DT_RANK:DT_RANK + STATE]
            output_coef = low_rank[:, DT_RANK + STATE:]
            step_size = jax.nn.softplus(jnp.dot(step_in, delta_proj, preferred_element_type=jnp.float32) + delta_bias)
            decay_factor = jnp.exp(step_size[:, None, :] * decay_rate[None])
            updated = decay_factor * hidden + (step_size * activated)[:, None, :] * input_coef[:, :, None]
            mixer = (jnp.sum(updated * output_coef[:, :, None], axis=1) + skip_gain * activated) * jax.nn.silu(gate_group[position].astype(jnp.float32))
            hidden = jnp.where(active[:, :, None], updated, hidden)
            window = jnp.where(active[:, :, None], full_window[:, 1:], window)
            results.append(jnp.where(active, mixer, 0.0).astype(jnp.bfloat16))
        stacked = jnp.stack(results).reshape(STEPS * ROWS, channels)
        pieces = jnp.einsum(
            "rge,ged->grd",
            stacked.reshape(STEPS * ROWS, N_MP, channels // N_MP).astype(jnp.float32),
            out_proj.reshape(N_MP, channels // N_MP, D_OUT).astype(jnp.float32),
        )
        rounded = lax.optimization_barrier(pieces.astype(jnp.bfloat16))
        layer_block = jnp.sum(rounded.astype(jnp.float32), axis=0).astype(jnp.bfloat16)
        return layer_block.reshape(STEPS, ROWS, D_OUT), window.astype(jnp.bfloat16), hidden.astype(jnp.bfloat16)

    layer_out, conv_final, ssm_final = lax.map(advance, inputs)
    layer_out = layer_out.transpose(1, 0, 2, 3).reshape(STEPS, total_rows, D_OUT)
    return layer_out, conv_final.reshape(total_rows, TAPS - 1, channels), ssm_final.reshape(total_rows, STATE, channels)
```

```python
import functools

import jax
import jax.numpy as jnp
from jax import lax
from jax.experimental import pallas as pl
from jax.experimental.pallas import tpu as pltpu
from jax.sharding import Mesh
from jax.sharding import PartitionSpec as P

BF = jnp.bfloat16
F32 = jnp.float32
I32 = jnp.int32
NZ, NX, NY, NC = 8, 4, 4, 2
GROUPS = NZ * NX
ROWS = 96
CH = 1024
STATE = 16
RANK = 512
STEPS = 4
LOW = RANK + 2 * STATE
COEF = LOW // GROUPS
DELTA = RANK // GROUPS
BASE = ROWS // GROUPS
SLOT = 16
SEC = 32
GATH = SEC + DELTA
LOG2E = 1.4426950408889634
VMEM = pl.BlockSpec(memory_space=pltpu.VMEM)
SMEM = pl.BlockSpec(memory_space=pltpu.SMEM)
ANY = pl.BlockSpec(memory_space=pl.ANY)


def iota(shape, dim):
    return lax.broadcasted_iota(I32, shape, dim)


def bdot(a, b):
    return jnp.dot(a, b, preferred_element_type=F32)


def bdot_t(a, b):
    return lax.dot_general(a, b, (((1,), (1,)), ((), ())), preferred_element_type=F32)


def onehot(cond):
    return cond.astype(F32).astype(BF)


def plan_kernel(
    me_ref, slots_ref, remaining_ref, mine_ref, conv_ref, coef_ref,
    pack_ref, gather_ref, rem_ref, col_ref, ext_ref, buf_ref, sec_ref,
):
    me = me_ref[0]
    match = (slots_ref[...] == me * ROWS + iota((ROWS, GROUPS * ROWS), 0)).astype(I32)
    inv = jnp.sum(match * iota(match.shape, 1), axis=1, keepdims=True)
    rem_ref[...] = jnp.sum(match * remaining_ref[...], axis=1, keepdims=True)
    square = (ROWS, ROWS)
    eye = iota(square, 0) == iota(square, 1)
    inv_row = jnp.sum(jnp.where(eye, inv, 0), axis=0, keepdims=True)
    src = inv // ROWS
    src_row = inv_row // ROWS
    rank = jnp.sum(
        ((src == src_row) & (inv_row < inv)).astype(I32), axis=1, keepdims=True
    )
    rank_row = jnp.sum(
        ((src == src_row) & (inv < inv_row)).astype(I32), axis=0, keepdims=True
    )
    base_row = src_row * BASE + rank_row
    where_row = jnp.where(rank_row < BASE, base_row, ROWS + base_row - BASE)
    gather_ref[...] = jnp.broadcast_to(where_row, gather_ref.shape)
    for tap in range(3):
        at = pl.ds(tap * ROWS, ROWS)
        col_ref[at, :] = jnp.where(rank < BASE, src * SLOT + rank * 3 + tap, -1)
        ext_ref[at, :] = jnp.where(
            rank < BASE, -1, src * GATH + COEF + (rank - BASE) * 3 + tap
        )
    to_row = mine_ref[...] // ROWS
    to = jnp.sum(jnp.where(eye, to_row, 0), axis=1, keepdims=True)
    same = to == to_row
    order_row = jnp.sum((same & (iota(square, 0) < iota(square, 1))).astype(I32), axis=0, keepdims=True)
    order = jnp.sum((same & (iota(square, 1) < iota(square, 0))).astype(I32), axis=1, keepdims=True)
    place = jnp.where(order < BASE, to * BASE + order, ROWS + order - BASE)
    lanes = (ROWS, 128)
    picked = jnp.sum(jnp.where(place == iota(lanes, 1), iota(lanes, 0), 0), axis=0, keepdims=True)
    pack_ref[...] = jnp.broadcast_to(picked, pack_ref.shape)
    buf = jnp.zeros((GROUPS * SLOT, CH), F32)
    sec = bdot(onehot(iota((SEC, COEF), 0) == iota((SEC, COEF), 1)), coef_ref[...])
    for tap in range(3):
        dest = jnp.where(order_row < BASE, to_row * SLOT + order_row * 3 + tap, -1)
        buf += bdot(onehot(iota((GROUPS * SLOT, ROWS), 0) == dest), conv_ref[tap])
        dest = jnp.where(order_row < BASE, -1, COEF + (order_row - BASE) * 3 + tap)
        sec += bdot(onehot(iota((SEC, ROWS), 0) == dest), conv_ref[tap])
    buf_ref[...] = buf.astype(BF)
    sec_ref[...] = sec.astype(BF)


def plan(me, slots, remaining, mine, conv, coef):
    shape = jax.ShapeDtypeStruct
    return pl.pallas_call(
        plan_kernel,
        name="plan",
        out_shape=(
            shape((8, 128), I32),
            shape((8, ROWS), I32),
            shape((ROWS, 1), I32),
            shape((3 * ROWS, 1), I32),
            shape((3 * ROWS, 1), I32),
            shape((GROUPS * SLOT, CH), BF),
            shape((SEC, CH), BF),
        ),
        in_specs=[SMEM] + [VMEM] * 5,
        out_specs=(VMEM,) * 7,
        compiler_params=pltpu.CompilerParams(vmem_limit_bytes=40 << 20),
    )(me, slots, remaining, mine, conv, coef)


def pack_kernel(pick_ref, ssm_ref, main_ref, extra_ref, sems):
    def send(p, carry):
        pltpu.make_async_copy(ssm_ref.at[pick_ref[0, p]], main_ref.at[p], sems.at[0]).start()
        return carry

    lax.fori_loop(0, ROWS, send, 0)
    for p in range(BASE):
        pltpu.make_async_copy(ssm_ref.at[pick_ref[0, ROWS + p]], extra_ref.at[p], sems.at[1]).start()
    pltpu.make_async_copy(ssm_ref, main_ref, sems.at[0]).wait()
    pltpu.make_async_copy(ssm_ref.at[pl.ds(0, BASE)], extra_ref, sems.at[1]).wait()


def pack(pick, ssm):
    shape = jax.ShapeDtypeStruct
    return pl.pallas_call(
        pack_kernel,
        name="pack",
        out_shape=(shape((ROWS, STATE, CH), BF), shape((BASE, STATE, CH), BF)),
        in_specs=[SMEM, ANY],
        out_specs=(ANY, ANY),
        scratch_shapes=[pltpu.SemaphoreType.DMA((2,))],
        compiler_params=pltpu.CompilerParams(vmem_limit_bytes=8 << 20),
    )(pick, ssm)


def conv_kernel(
    me_ref, moved_ref, g0, g1, g2, g3, col_ref, ext_ref, rem_ref, inputs_ref, weight_ref, bias_ref,
    act_ref, low_ref, final_ref,
):
    x = me_ref[1]
    parts = (g0, g1, g2, g3)
    span = NZ * GATH
    window = bdot(onehot(col_ref[...] == iota((3 * ROWS, GROUPS * SLOT), 1)), moved_ref[...])
    coef = jnp.zeros((LOW, CH), F32)
    for k, part in enumerate(parts):
        at = iota((1, span), 1)
        z, q = at // GATH, at % GATH
        group = z * NX + lax.rem(x - k + NX, NX)
        ext = onehot(ext_ref[...] == group * GATH + q)
        window += bdot(ext, part[...])
        row = jnp.where(q < COEF, group * COEF + q, -1)
        coef += bdot(onehot(iota((LOW, span), 0) == row), part[...])
    coef = coef.astype(BF)
    taps = [window[tap * ROWS : (tap + 1) * ROWS] for tap in range(3)]
    taps += [inputs_ref[t].astype(F32) for t in range(STEPS)]
    weight = weight_ref[...]
    for t in range(STEPS):
        out = bias_ref[...] + sum(taps[t + k] * weight[k : k + 1] for k in range(4))
        act = out / (1.0 + jnp.exp(-out))
        act_ref[t] = act
        low_ref[pl.ds(t * ROWS, ROWS), :] = bdot_t(act.astype(BF), coef).astype(BF)
    rem = rem_ref[...]
    for k in range(3):
        kept = taps[k]
        for t in range(1, STEPS + 1):
            kept = jnp.where(rem >= t, taps[t + k], kept)
        final_ref[k] = kept.astype(BF)


def conv_stage(me, moved, parts, col, ext, rem, inputs, weight, bias):
    shape = jax.ShapeDtypeStruct
    return pl.pallas_call(
        conv_kernel,
        name="conv",
        out_shape=(
            shape((STEPS, ROWS, CH), F32),
            shape((STEPS * ROWS, LOW), BF),
            shape((3, ROWS, CH), BF),
        ),
        in_specs=[SMEM] + [VMEM] * 11,
        out_specs=(VMEM,) * 3,
        compiler_params=pltpu.CompilerParams(vmem_limit_bytes=56 << 20),
    )(me, moved, *parts, col, ext, rem, inputs, weight, bias)


def step_kernel(
    me_ref, own_ref, other_ref, g0, g1, g2, g3, bias_ref, act_ref, gate_ref, skip_ref, rem_ref, log_ref,
    dt_ref, dx_ref, sk_ref, sg_ref, bc_ref, rate_ref, low_ref,
):
    x, y, c = me_ref[1], me_ref[2], me_ref[3]
    rate_ref[...] = -jnp.exp(log_ref[...]) * LOG2E
    chunk = STEPS * ROWS // (NY * NC)
    for half, piece in ((c, own_ref), (1 - c, other_ref)):
        for m in range(NY):
            at = half * NY + lax.rem(y + m, NY)
            low_ref[pl.ds(pl.multiple_of(at * chunk, 16), chunk), :] = piece[m]
    span = NZ * GATH
    delta = jnp.zeros((RANK, CH), F32)
    for k, part in enumerate((g0, g1, g2, g3)):
        at = iota((1, span), 1)
        z, q = at // GATH, at % GATH
        group = z * NX + lax.rem(x - k + NX, NX)
        row = jnp.where(q >= SEC, group * DELTA + q - SEC, -1)
        delta += bdot(onehot(iota((RANK, span), 0) == row), part[...])
    delta = delta.astype(BF)
    rem = rem_ref[...]
    for t in range(STEPS):
        low = low_ref[pl.ds(t * ROWS, ROWS), :]
        raw = bdot(low[:, :RANK], delta) + bias_ref[...]
        size = jnp.maximum(raw, 0.0) + jnp.log1p(jnp.exp(-jnp.abs(raw)))
        active = rem > t
        size = jnp.where(active, size, 0.0)
        act = act_ref[t]
        gate = gate_ref[t].astype(F32)
        dt_ref[t] = size
        dx_ref[t] = size * act
        sk_ref[t] = skip_ref[...] * act
        sg_ref[t] = jnp.where(active, gate / (1.0 + jnp.exp(-gate)), 0.0)
        coefs = low[:, RANK:].astype(F32)
        for n in range(2 * STATE):
            bc_ref[t, n] = jnp.broadcast_to(coefs[:, n : n + 1], (ROWS, 128))


def step_stage(me, own, other, parts, bias, act, gate, skip, rem, log):
    shape = jax.ShapeDtypeStruct
    rows = shape((STEPS, ROWS, CH), F32)
    return pl.pallas_call(
        step_kernel,
        name="sizes",
        out_shape=(rows, rows, rows, rows, shape((STEPS, 2 * STATE, ROWS, 128), F32), shape((STATE, CH), F32)),
        in_specs=[SMEM] + [VMEM] * 12,
        out_specs=(VMEM,) * 6,
        scratch_shapes=[pltpu.VMEM((STEPS * ROWS, LOW), BF)],
        compiler_params=pltpu.CompilerParams(vmem_limit_bytes=56 << 20),
    )(me, own, other, *parts, bias, act, gate, skip, rem, log)


BLOCK = 8
BLOCKS = ROWS // BLOCK


def scan_kernel(
    at_ref, main_ref, extra_ref, dt_ref, dx_ref, sk_ref, sg_ref, bc_ref, rate_ref,
    out_ref, final_ref, held, wide, sems,
):
    b = pl.program_id(0)

    def fetch(block):
        for i in range(BLOCK):
            at = at_ref[0, block * BLOCK + i]

            @pl.when(at < ROWS)
            def _():
                pltpu.make_async_copy(main_ref.at[at], held.at[block, i], sems.at[block]).start()

            @pl.when(at >= ROWS)
            def _():
                pltpu.make_async_copy(extra_ref.at[at - ROWS], held.at[block, i], sems.at[block]).start()

    @pl.when(b == 0)
    def _():
        for block in range(3):
            fetch(block)

    @pl.when(b + 3 < BLOCKS)
    def _():
        fetch(b + 3)

    pltpu.make_async_copy(main_ref.at[pl.ds(0, BLOCK)], held.at[b], sems.at[b]).wait()
    for i in range(BLOCK):
        for l in range(CH // 128):
            wide[l, pl.ds(i * STATE, STATE), :] = held[b, i, :, pl.ds(l * 128, 128)].astype(F32)

    def lanes(l, carry):
        cols = pl.ds(pl.multiple_of(l * 128, 128), 128)
        dts = [dt_ref[t, :, cols] for t in range(STEPS)]
        dxs = [dx_ref[t, :, cols] for t in range(STEPS)]
        sums = [sk_ref[t, :, cols] for t in range(STEPS)]
        for n in range(STATE):
            here = pl.ds(n, BLOCK, stride=STATE)
            h = wide[l, here, :]
            rate = jnp.broadcast_to(rate_ref[pl.ds(n, 1), cols], (BLOCK, 128))
            for t in range(STEPS):
                h = jnp.exp2(dts[t] * rate) * h + dxs[t] * bc_ref[t, n]
                sums[t] += h * bc_ref[t, STATE + n]
            wide[l, here, :] = h
        for t in range(STEPS):
            out_ref[t, :, cols] = (sums[t] * sg_ref[t, :, cols]).astype(BF)
        return carry

    lax.fori_loop(0, CH // 128, lanes, 0)
    for i in range(BLOCK):
        for l in range(CH // 128):
            final_ref[i, :, pl.ds(l * 128, 128)] = wide[l, pl.ds(i * STATE, STATE), :].astype(BF)


def scan_stage(at, main, extra, dt, dx, sk, sg, bc, rate):
    shape = jax.ShapeDtypeStruct
    rows = pl.BlockSpec((STEPS, BLOCK, CH), lambda b, at: (0, b, 0))
    return pl.pallas_call(
        scan_kernel,
        name="scan",
        out_shape=(shape((STEPS, ROWS, CH), BF), shape((ROWS, STATE, CH), BF)),
        grid_spec=pltpu.PrefetchScalarGridSpec(
            num_scalar_prefetch=1,
            grid=(BLOCKS,),
            in_specs=[
                ANY,
                ANY,
                rows,
                rows,
                rows,
                rows,
                pl.BlockSpec((STEPS, 2 * STATE, BLOCK, 128), lambda b, at: (0, 0, b, 0)),
                pl.BlockSpec((STATE, CH), lambda b, at: (0, 0)),
            ],
            out_specs=(rows, pl.BlockSpec((BLOCK, STATE, CH), lambda b, at: (b, 0, 0))),
            scratch_shapes=[
                pltpu.VMEM((BLOCKS, BLOCK, STATE, CH), BF),
                pltpu.VMEM((CH // 128, BLOCK * STATE, 128), F32),
                pltpu.SemaphoreType.DMA((BLOCKS,)),
            ],
        ),
        compiler_params=pltpu.CompilerParams(vmem_limit_bytes=40 << 20),
    )(at, main, extra, dt, dx, sk, sg, bc, rate)


def shift(value, axis, size, k):
    return lax.ppermute(value, axis, [(i, (i + k) % size) for i in range(size)])


def reduce_mp(low, y, c):
    chunk = STEPS * ROWS // (NY * NC)
    halves = low.reshape(NC, NY * chunk, LOW)
    got = shift(lax.dynamic_index_in_dim(halves, 1 - c, 0, False), "c", NC, 1)
    mine = lax.dynamic_index_in_dim(halves, c, 0, False).astype(F32) + got.astype(F32)
    quarters = mine.reshape(NY, chunk, LOW)
    rounded = quarters.astype(BF)
    total = lax.dynamic_index_in_dim(quarters, y, 0, False)
    came = [
        shift(lax.dynamic_index_in_dim(rounded, lax.rem(y + k, NY), 0, False), "y", NY, k)
        for k in range(1, NY)
    ]
    total = (total + came[0].astype(F32) + came[1].astype(F32) + came[2].astype(F32)).astype(BF)
    own = jnp.stack([total] + [shift(total, "y", NY, NY - m) for m in range(1, NY)])
    return own, shift(own, "c", NC, 1)


def per_device(
    input_steps, gate_steps, conv_state, ssm_state, new_slot, remaining, conv_weight, conv_bias,
    coef_proj, delta_proj, delta_bias, decay_log, skip_gain, out_proj,
):
    z, x, y, c = (lax.axis_index(name) for name in ("z", "x", "y", "c"))
    group = z * NX + x
    me = jnp.stack([group, x, y, c]).astype(I32)
    out_whole = lax.all_gather(out_proj, ("z", "x"), axis=1, tiled=True)
    mine = lax.dynamic_slice_in_dim(new_slot, group * ROWS, ROWS)
    pick, at, rem, col, ext, buf, sec = plan(
        me,
        new_slot.reshape(1, -1),
        remaining.reshape(1, -1),
        mine.reshape(1, -1),
        conv_state.transpose(1, 0, 2),
        coef_proj.T,
    )
    moved = lax.all_to_all(
        buf.reshape(GROUPS, SLOT, CH), ("z", "x"), split_axis=0, concat_axis=0, tiled=True
    ).reshape(GROUPS * SLOT, CH)
    main, extra = pack(pick, ssm_state)
    gathered = lax.all_gather(
        jnp.concatenate([sec, delta_proj], axis=0), "z", axis=0, tiled=True
    )
    parts = [gathered] + [shift(gathered, "x", NX, k) for k in range(1, NX)]
    ssm_main = lax.all_to_all(main, ("z", "x"), split_axis=0, concat_axis=0, tiled=True)
    extras = lax.all_gather(extra.reshape(BASE * STATE, CH), "z", axis=0, tiled=True)
    extras = extras.reshape(NZ, BASE, STATE, CH)
    extras = [extras] + [shift(extras, "x", NX, k) for k in range(1, NX)]
    act, low, conv_final = conv_stage(
        me, moved, parts, col, ext, rem, input_steps, conv_weight, conv_bias.reshape(1, -1)
    )
    own, other = reduce_mp(low, y, c)
    dt, dx, sk, sg, bc, rate = step_stage(
        me, own, other, parts, delta_bias.reshape(1, -1), act, gate_steps, skip_gain.reshape(1, -1), rem, decay_log
    )
    spot = at[:1] - ROWS
    their = spot // BASE
    turned = (lax.rem(x - their % NX + NX, NX) * NZ + their // NX) * BASE + spot % BASE
    at = jnp.where(at[:1] < ROWS, at[:1], ROWS + turned)
    stepped, ssm_final = scan_stage(
        at, ssm_main, jnp.concatenate(extras, axis=0).reshape(ROWS, STATE, CH), dt, dx, sk, sg, bc, rate
    )
    partial_mix = bdot(stepped.reshape(STEPS * ROWS, CH), out_whole)
    summed = lax.psum_scatter(partial_mix.astype(BF), ("y", "c"), scatter_dimension=1, tiled=True)
    return summed.reshape(STEPS, ROWS, -1), conv_final.transpose(1, 0, 2), ssm_final


def solution(mesh):
    fine = Mesh(mesh.devices.reshape(NZ, NX, NY, NC), ("z", "x", "y", "c"))
    dp, mp = ("z", "x"), ("y", "c")
    return jax.shard_map(
        per_device,
        mesh=fine,
        in_specs=(
            P(None, dp, mp),
            P(None, dp, mp),
            P(dp, None, mp),
            P(dp, None, mp),
            P(),
            P(),
            P(None, mp),
            P(mp),
            P(mp, dp),
            P(dp, mp),
            P(mp),
            P(None, mp),
            P(mp),
            P(mp, dp),
        ),
        out_specs=(P(None, dp, mp), P(dp, None, mp), P(dp, None, mp)),
        check_vma=False,
    )
```

```python
import functools

import jax
import jax.numpy as jnp
from jax import lax
from jax.experimental import pallas as pl
from jax.experimental.pallas import tpu as pltpu
from jax.sharding import Mesh
from jax.sharding import PartitionSpec as P

BF = jnp.bfloat16
F32 = jnp.float32
I32 = jnp.int32
NZ, NX, NY, NC = 8, 4, 4, 2
GROUPS = NZ * NX
ROWS = 96
CH = 1024
STATE = 16
RANK = 512
STEPS = 4
LOW = RANK + 2 * STATE
COEF = LOW // GROUPS
DELTA = RANK // GROUPS
BASE = ROWS // GROUPS
SLOT = 16
SEC = 32
GATH = SEC + DELTA
LOG2E = 1.4426950408889634
VMEM = pl.BlockSpec(memory_space=pltpu.VMEM)
SMEM = pl.BlockSpec(memory_space=pltpu.SMEM)
ANY = pl.BlockSpec(memory_space=pl.ANY)


def iota(shape, dim):
    return lax.broadcasted_iota(I32, shape, dim)


def bdot(a, b):
    return jnp.dot(a, b, preferred_element_type=F32)


def bdot_t(a, b):
    return lax.dot_general(a, b, (((1,), (1,)), ((), ())), preferred_element_type=F32)


def onehot(cond):
    return cond.astype(F32).astype(BF)


def plan_kernel(
    me_ref, slots_ref, remaining_ref, table_ref, conv_ref, coef_ref, delta_ref, ssm_ref, proj_ref,
    gather_ref, relay_ref, rem_ref, col_ref, ext_ref, buf_ref, block_ref, main_ref, proj_out_ref,
    pick_ref, pick_smem, sems,
):
    me = me_ref[0]
    x = me_ref[1]
    passed = pltpu.make_async_copy(proj_ref, proj_out_ref, sems.at[3])
    passed.start()
    square = (ROWS, ROWS)
    eye = iota(square, 0) == iota(square, 1)
    to_row = table_ref[pl.ds(me, 1), :] // ROWS
    to = jnp.sum(jnp.where(eye, to_row, 0), axis=1, keepdims=True)
    same = to == to_row
    order_row = jnp.sum((same & (iota(square, 0) < iota(square, 1))).astype(I32), axis=0, keepdims=True)
    order = jnp.sum((same & (iota(square, 1) < iota(square, 0))).astype(I32), axis=1, keepdims=True)
    place = jnp.where(order < BASE, to * BASE + order, ROWS + order - BASE)
    lanes = (ROWS, 128)
    picked = jnp.sum(jnp.where(place == iota(lanes, 1), iota(lanes, 0), 0), axis=0, keepdims=True)
    pick_ref[...] = jnp.broadcast_to(picked, pick_ref.shape)
    picking = pltpu.make_async_copy(pick_ref, pick_smem, sems.at[0])
    picking.start()
    picking.wait()
    for p in range(BASE):
        pltpu.make_async_copy(
            ssm_ref.at[pick_smem[0, ROWS + p]], block_ref.at[pl.ds(GATH + p * STATE, STATE)], sems.at[2]
        ).start()

    def send(p, carry):
        pltpu.make_async_copy(ssm_ref.at[pick_smem[0, p]], main_ref.at[p], sems.at[1]).start()
        return carry

    lax.fori_loop(0, ROWS, send, 0)
    buf = jnp.zeros((GROUPS * SLOT, CH), F32)
    sec = bdot(onehot(iota((SEC, COEF), 0) == iota((SEC, COEF), 1)), coef_ref[...])
    for tap in range(3):
        dest = jnp.where(order_row < BASE, to_row * SLOT + order_row * 3 + tap, -1)
        buf += bdot(onehot(iota((GROUPS * SLOT, ROWS), 0) == dest), conv_ref[tap])
        dest = jnp.where(order_row < BASE, -1, COEF + (order_row - BASE) * 3 + tap)
        sec += bdot(onehot(iota((SEC, ROWS), 0) == dest), conv_ref[tap])
    buf_ref[...] = buf.astype(BF)
    block_ref[pl.ds(0, SEC), :] = sec.astype(BF)
    block_ref[pl.ds(SEC, DELTA), :] = delta_ref[...]
    match = (slots_ref[...] == me * ROWS + iota((ROWS, GROUPS * ROWS), 0)).astype(I32)
    inv = jnp.sum(match * iota(match.shape, 1), axis=1, keepdims=True)
    rem_ref[...] = jnp.sum(match * remaining_ref[...], axis=1, keepdims=True)
    inv_row = jnp.sum(jnp.where(eye, inv, 0), axis=0, keepdims=True)
    src = inv // ROWS
    src_row = inv_row // ROWS
    rank = jnp.sum(
        ((src == src_row) & (inv_row < inv)).astype(I32), axis=1, keepdims=True
    )
    rank_row = jnp.sum(
        ((src == src_row) & (inv < inv_row)).astype(I32), axis=0, keepdims=True
    )
    turn = lax.rem(x - lax.rem(src_row, NX) + NX, NX)
    where_row = jnp.where(rank_row < BASE, src_row * BASE + rank_row, ROWS + (turn - 1) * BASE + rank_row)
    gather_ref[...] = jnp.broadcast_to(where_row, gather_ref.shape)
    for tap in range(3):
        at = pl.ds(tap * ROWS, ROWS)
        col_ref[at, :] = jnp.where(rank < BASE, src * SLOT + rank * 3 + tap, -1)
        ext_ref[at, :] = jnp.where(
            rank < BASE, -1, src * SEC + COEF + (rank - BASE) * 3 + tap
        )
    target = table_ref[...] // ROWS
    groups = iota((GROUPS, 1), 0)
    for k in range(NX):
        dest = me - x + lax.rem(x + k, NX)
        count = jnp.sum((target == dest).astype(I32), axis=1, keepdims=True)
        holds = (count > BASE) & (lax.rem(groups, NX) == x)
        z = jnp.sum(jnp.where(holds, groups // NX, 0), axis=0, keepdims=True)
        relay_ref[pl.ds(k, 1), :] = jnp.broadcast_to(z, (1, 128))
    pltpu.make_async_copy(
        ssm_ref.at[pl.ds(0, BASE)].reshape(BASE * STATE, CH), block_ref.at[pl.ds(GATH, BASE * STATE)], sems.at[2]
    ).wait()
    pltpu.make_async_copy(ssm_ref, main_ref, sems.at[1]).wait()
    passed.wait()


def plan(me, slots, remaining, table, conv, coef, delta, ssm, proj):
    shape = jax.ShapeDtypeStruct
    return pl.pallas_call(
        plan_kernel,
        name="plan",
        out_shape=(
            shape((8, ROWS), I32),
            shape((NX, 128), I32),
            shape((ROWS, 1), I32),
            shape((3 * ROWS, 1), I32),
            shape((3 * ROWS, 1), I32),
            shape((GROUPS * SLOT, CH), BF),
            shape((GATH + BASE * STATE, CH), BF),
            shape((ROWS, STATE, CH), BF),
            shape(proj.shape, BF),
        ),
        in_specs=[SMEM] + [VMEM] * 6 + [ANY] * 2,
        out_specs=(VMEM,) * 7 + (ANY,) * 2,
        scratch_shapes=[
            pltpu.VMEM((8, 128), I32),
            pltpu.SMEM((8, 128), I32),
            pltpu.SemaphoreType.DMA((4,)),
        ],
        compiler_params=pltpu.CompilerParams(vmem_limit_bytes=60 << 20),
    )(me, slots, remaining, table, conv, coef, delta, ssm, proj)


def conv_kernel(
    me_ref, moved_ref, g0, g1, g2, g3, col_ref, ext_ref, rem_ref, inputs_ref, weight_ref, bias_ref,
    act_ref, low_ref, final_ref,
):
    x = me_ref[1]
    parts = (g0, g1, g2, g3)
    span = NZ * SEC
    window = bdot(onehot(col_ref[...] == iota((3 * ROWS, GROUPS * SLOT), 1)), moved_ref[...])
    coef = jnp.zeros((LOW, CH), F32)
    for k, part in enumerate(parts):
        at = iota((1, span), 1)
        z, q = at // SEC, at % SEC
        group = z * NX + lax.rem(x - k + NX, NX)
        ext = onehot(ext_ref[...] == group * SEC + q)
        window += bdot(ext, part[...])
        row = jnp.where(q < COEF, group * COEF + q, -1)
        coef += bdot(onehot(iota((LOW, span), 0) == row), part[...])
    coef = coef.astype(BF)
    taps = [window[tap * ROWS : (tap + 1) * ROWS] for tap in range(3)]
    taps += [inputs_ref[t].astype(F32) for t in range(STEPS)]
    weight = weight_ref[...]
    for t in range(STEPS):
        out = bias_ref[...] + sum(taps[t + k] * weight[k : k + 1] for k in range(4))
        act = out / (1.0 + jnp.exp(-out))
        act_ref[t] = act
        low_ref[pl.ds(t * ROWS, ROWS), :] = bdot_t(act.astype(BF), coef).astype(BF)
    rem = rem_ref[...]
    for k in range(3):
        kept = taps[k]
        for t in range(1, STEPS + 1):
            kept = jnp.where(rem >= t, taps[t + k], kept)
        final_ref[k] = kept.astype(BF)


def conv_stage(me, moved, parts, col, ext, rem, inputs, weight, bias):
    shape = jax.ShapeDtypeStruct
    return pl.pallas_call(
        conv_kernel,
        name="conv",
        out_shape=(
            shape((STEPS, ROWS, CH), F32),
            shape((STEPS * ROWS, LOW), BF),
            shape((3, ROWS, CH), BF),
        ),
        in_specs=[SMEM] + [VMEM] * 11,
        out_specs=(VMEM,) * 3,
        compiler_params=pltpu.CompilerParams(vmem_limit_bytes=60 << 20),
    )(me, moved, *parts, col, ext, rem, inputs, weight, bias)


def step_kernel(
    me_ref, own_ref, other_ref, g0, g1, g2, g3, bias_ref, act_ref, gate_ref, skip_ref, rem_ref, log_ref,
    dt_ref, dx_ref, sk_ref, sg_ref, bc_ref, rate_ref, low_ref,
):
    x, y, c = me_ref[1], me_ref[2], me_ref[3]
    rate_ref[...] = -jnp.exp(log_ref[...]) * LOG2E
    chunk = STEPS * ROWS // (NY * NC)
    for half, piece in ((c, own_ref), (1 - c, other_ref)):
        for m in range(NY):
            at = half * NY + lax.rem(y + m, NY)
            low_ref[pl.ds(pl.multiple_of(at * chunk, 16), chunk), :] = piece[m]
    span = NZ * DELTA
    delta = jnp.zeros((RANK, CH), F32)
    for k, part in enumerate((g0, g1, g2, g3)):
        at = iota((1, span), 1)
        z, q = at // DELTA, at % DELTA
        row = (z * NX + lax.rem(x - k + NX, NX)) * DELTA + q
        delta += bdot(onehot(iota((RANK, span), 0) == row), part[...])
    delta = delta.astype(BF)
    rem = rem_ref[...]
    for t in range(STEPS):
        low = low_ref[pl.ds(t * ROWS, ROWS), :]
        raw = bdot(low[:, :RANK], delta) + bias_ref[...]
        size = jnp.maximum(raw, 0.0) + jnp.log1p(jnp.exp(-jnp.abs(raw)))
        active = rem > t
        size = jnp.where(active, size, 0.0)
        act = act_ref[t]
        gate = gate_ref[t].astype(F32)
        dt_ref[t] = size
        dx_ref[t] = size * act
        sk_ref[t] = skip_ref[...] * act
        sg_ref[t] = jnp.where(active, gate / (1.0 + jnp.exp(-gate)), 0.0)
        coefs = low[:, RANK:].astype(F32)
        for n in range(2 * STATE):
            bc_ref[t, n] = jnp.broadcast_to(coefs[:, n : n + 1], (ROWS, 128))


def step_stage(me, own, other, parts, bias, act, gate, skip, rem, log):
    shape = jax.ShapeDtypeStruct
    rows = shape((STEPS, ROWS, CH), F32)
    return pl.pallas_call(
        step_kernel,
        name="sizes",
        out_shape=(rows, rows, rows, rows, shape((STEPS, 2 * STATE, ROWS, 128), F32), shape((STATE, CH), F32)),
        in_specs=[SMEM] + [VMEM] * 12,
        out_specs=(VMEM,) * 6,
        scratch_shapes=[pltpu.VMEM((STEPS * ROWS, LOW), BF)],
        compiler_params=pltpu.CompilerParams(vmem_limit_bytes=60 << 20),
    )(me, own, other, *parts, bias, act, gate, skip, rem, log)


BLOCK = 8
BLOCKS = ROWS // BLOCK


def scan_kernel(
    at_ref, main_ref, e0, e1, e2, e3, dt_ref, dx_ref, sk_ref, sg_ref, bc_ref, rate_ref,
    out_ref, final_ref, held, wide, sems,
):
    b = pl.program_id(0)

    def fetch(block):
        for i in range(BLOCK):
            at = at_ref[0, block * BLOCK + i]

            @pl.when(at < ROWS)
            def _():
                pltpu.make_async_copy(main_ref.at[at], held.at[block, i], sems.at[block]).start()

            for k, extra in enumerate((e0, e1, e2, e3)):
                row = at - ROWS - k * BASE

                @pl.when((row >= 0) & (row < BASE))
                def _(row=row, extra=extra):
                    pltpu.make_async_copy(extra.at[row], held.at[block, i], sems.at[block]).start()

    @pl.when(b == 0)
    def _():
        for block in range(3):
            fetch(block)

    @pl.when(b + 3 < BLOCKS)
    def _():
        fetch(b + 3)

    pltpu.make_async_copy(main_ref.at[pl.ds(0, BLOCK)], held.at[b], sems.at[b]).wait()
    for i in range(BLOCK):
        for l in range(CH // 128):
            wide[l, pl.ds(i * STATE, STATE), :] = held[b, i, :, pl.ds(l * 128, 128)].astype(F32)

    def lanes(l, carry):
        cols = pl.ds(pl.multiple_of(l * 128, 128), 128)
        dts = [dt_ref[t, :, cols] for t in range(STEPS)]
        dxs = [dx_ref[t, :, cols] for t in range(STEPS)]
        sums = [sk_ref[t, :, cols] for t in range(STEPS)]
        for n in range(STATE):
            here = pl.ds(n, BLOCK, stride=STATE)
            h = wide[l, here, :]
            rate = jnp.broadcast_to(rate_ref[pl.ds(n, 1), cols], (BLOCK, 128))
            for t in range(STEPS):
                h = jnp.exp2(dts[t] * rate) * h + dxs[t] * bc_ref[t, n]
                sums[t] += h * bc_ref[t, STATE + n]
            wide[l, here, :] = h
        for t in range(STEPS):
            out_ref[t, :, cols] = (sums[t] * sg_ref[t, :, cols]).astype(BF)
        return carry

    lax.fori_loop(0, CH // 128, lanes, 0)
    for i in range(BLOCK):
        for l in range(CH // 128):
            final_ref[i, :, pl.ds(l * 128, 128)] = wide[l, pl.ds(i * STATE, STATE), :].astype(BF)


def scan_stage(at, main, extras, dt, dx, sk, sg, bc, rate):
    shape = jax.ShapeDtypeStruct
    rows = pl.BlockSpec((STEPS, BLOCK, CH), lambda b, at: (0, b, 0))
    return pl.pallas_call(
        scan_kernel,
        name="scan",
        out_shape=(shape((STEPS, ROWS, CH), BF), shape((ROWS, STATE, CH), BF)),
        grid_spec=pltpu.PrefetchScalarGridSpec(
            num_scalar_prefetch=1,
            grid=(BLOCKS,),
            in_specs=[
                ANY,
                ANY,
                ANY,
                ANY,
                ANY,
                rows,
                rows,
                rows,
                rows,
                pl.BlockSpec((STEPS, 2 * STATE, BLOCK, 128), lambda b, at: (0, 0, b, 0)),
                pl.BlockSpec((STATE, CH), lambda b, at: (0, 0)),
            ],
            out_specs=(rows, pl.BlockSpec((BLOCK, STATE, CH), lambda b, at: (b, 0, 0))),
            scratch_shapes=[
                pltpu.VMEM((BLOCKS, BLOCK, STATE, CH), BF),
                pltpu.VMEM((CH // 128, BLOCK * STATE, 128), F32),
                pltpu.SemaphoreType.DMA((BLOCKS,)),
            ],
        ),
        compiler_params=pltpu.CompilerParams(vmem_limit_bytes=60 << 20),
    )(at, main, *extras, dt, dx, sk, sg, bc, rate)


def shift(value, axis, size, k):
    return lax.ppermute(value, axis, [(i, (i + k) % size) for i in range(size)])


def reduce_mp(low, y, c):
    chunk = STEPS * ROWS // (NY * NC)
    halves = low.reshape(NC, NY * chunk, LOW)
    got = shift(lax.dynamic_index_in_dim(halves, 1 - c, 0, False), "c", NC, 1)
    mine = lax.dynamic_index_in_dim(halves, c, 0, False).astype(F32) + got.astype(F32)
    quarters = mine.reshape(NY, chunk, LOW)
    rounded = quarters.astype(BF)
    total = lax.dynamic_index_in_dim(quarters, y, 0, False)
    came = [
        shift(lax.dynamic_index_in_dim(rounded, lax.rem(y + k, NY), 0, False), "y", NY, k)
        for k in range(1, NY)
    ]
    total = (total + came[0].astype(F32) + came[1].astype(F32) + came[2].astype(F32)).astype(BF)
    own = jnp.stack([total] + [shift(total, "y", NY, NY - m) for m in range(1, NY)])
    return own, shift(own, "c", NC, 1)


def per_device(
    input_steps, gate_steps, conv_state, ssm_state, new_slot, remaining, conv_weight, conv_bias,
    coef_proj, delta_proj, delta_bias, decay_log, skip_gain, out_proj,
):
    z, x, y, c = (lax.axis_index(name) for name in ("z", "x", "y", "c"))
    group = z * NX + x
    me = jnp.stack([group, x, y, c]).astype(I32)
    at, relay, rem, col, ext, buf, block, main, proj = plan(
        me,
        new_slot.reshape(1, -1),
        remaining.reshape(1, -1),
        new_slot.reshape(GROUPS, ROWS),
        conv_state.transpose(1, 0, 2),
        coef_proj.T,
        delta_proj,
        ssm_state,
        out_proj,
    )
    gathered = lax.all_gather(block, "z", axis=0)
    moved = lax.all_to_all(
        buf.reshape(GROUPS, SLOT, CH), ("z", "x"), split_axis=0, concat_axis=0, tiled=True
    ).reshape(GROUPS * SLOT, CH)
    out_whole = lax.all_gather(proj, ("z", "x"), axis=1, tiled=True)
    ssm_main = lax.all_to_all(main, ("z", "x"), split_axis=0, concat_axis=0, tiled=True)

    def turned(value):
        return [value] + [shift(value, "x", NX, k) for k in range(1, NX)]

    secs = turned(gathered[:, :SEC].reshape(NZ * SEC, CH))
    deltas = turned(gathered[:, SEC:GATH].reshape(NZ * DELTA, CH))
    extras = [
        lax.dynamic_slice(gathered, (relay[k, 0], GATH, 0), (1, BASE * STATE, CH)) for k in range(NX)
    ]
    extras = [extras[0]] + [shift(extras[k], "x", NX, k) for k in range(1, NX)]
    extras = [e.reshape(BASE, STATE, CH) for e in extras]
    act, low, conv_final = conv_stage(
        me, moved, secs, col, ext, rem, input_steps, conv_weight, conv_bias.reshape(1, -1)
    )
    own, other = reduce_mp(low, y, c)
    dt, dx, sk, sg, bc, rate = step_stage(
        me, own, other, deltas, delta_bias.reshape(1, -1), act, gate_steps, skip_gain.reshape(1, -1), rem, decay_log
    )
    stepped, ssm_final = scan_stage(at, ssm_main, extras, dt, dx, sk, sg, bc, rate)
    partial_mix = bdot(stepped.reshape(STEPS * ROWS, CH), out_whole)
    summed = lax.psum_scatter(partial_mix.astype(BF), ("y", "c"), scatter_dimension=1, tiled=True)
    return summed.reshape(STEPS, ROWS, -1), conv_final.transpose(1, 0, 2), ssm_final


def solution(mesh):
    fine = Mesh(mesh.devices.reshape(NZ, NX, NY, NC), ("z", "x", "y", "c"))
    dp, mp = ("z", "x"), ("y", "c")
    return jax.shard_map(
        per_device,
        mesh=fine,
        in_specs=(
            P(None, dp, mp),
            P(None, dp, mp),
            P(dp, None, mp),
            P(dp, None, mp),
            P(),
            P(),
            P(None, mp),
            P(mp),
            P(mp, dp),
            P(dp, mp),
            P(mp),
            P(None, mp),
            P(mp),
            P(mp, dp),
        ),
        out_specs=(P(None, dp, mp), P(dp, None, mp), P(dp, None, mp)),
        check_vma=False,
    )
```

```python
import functools

import jax
import jax.numpy as jnp
from jax import lax
from jax.experimental import pallas as pl
from jax.experimental.pallas import tpu as pltpu
from jax.sharding import Mesh
from jax.sharding import PartitionSpec as P

BF = jnp.bfloat16
F32 = jnp.float32
I32 = jnp.int32
NZ, NX, NY, NC = 8, 4, 4, 2
GROUPS = NZ * NX
ROWS = 96
CH = 1024
STATE = 16
RANK = 512
STEPS = 4
LOW = RANK + 2 * STATE
COEF = LOW // GROUPS
DELTA = RANK // GROUPS
BASE = ROWS // GROUPS
SLOT = 16
SEC = 32
GATH = SEC + DELTA
LOG2E = 1.4426950408889634
VMEM = pl.BlockSpec(memory_space=pltpu.VMEM)
SMEM = pl.BlockSpec(memory_space=pltpu.SMEM)
ANY = pl.BlockSpec(memory_space=pl.ANY)


def iota(shape, dim):
    return lax.broadcasted_iota(I32, shape, dim)


def bdot(a, b):
    return jnp.dot(a, b, preferred_element_type=F32)


def bdot_t(a, b):
    return lax.dot_general(a, b, (((1,), (1,)), ((), ())), preferred_element_type=F32)


def onehot(cond):
    return cond.astype(F32).astype(BF)


def plan_kernel(
    me_ref, slots_ref, remaining_ref, table_ref, conv_ref, coef_ref, delta_ref, ssm_ref, proj_ref,
    gather_ref, relay_ref, rem_ref, col_ref, ext_ref, buf_ref, block_ref, main_ref, proj_out_ref,
    pick_ref, pick_smem, sems,
):
    me = me_ref[0]
    x = me_ref[1]
    passed = pltpu.make_async_copy(proj_ref, proj_out_ref, sems.at[3])
    passed.start()
    square = (ROWS, ROWS)
    eye = iota(square, 0) == iota(square, 1)
    to_row = table_ref[pl.ds(me, 1), :] // ROWS
    to = jnp.sum(jnp.where(eye, to_row, 0), axis=1, keepdims=True)
    same = to == to_row
    order_row = jnp.sum((same & (iota(square, 0) < iota(square, 1))).astype(I32), axis=0, keepdims=True)
    order = jnp.sum((same & (iota(square, 1) < iota(square, 0))).astype(I32), axis=1, keepdims=True)
    place = jnp.where(order < BASE, to * BASE + order, ROWS + order - BASE)
    lanes = (ROWS, 128)
    picked = jnp.sum(jnp.where(place == iota(lanes, 1), iota(lanes, 0), 0), axis=0, keepdims=True)
    pick_ref[...] = jnp.broadcast_to(picked, pick_ref.shape)
    picking = pltpu.make_async_copy(pick_ref, pick_smem, sems.at[0])
    picking.start()
    picking.wait()
    for p in range(BASE):
        pltpu.make_async_copy(
            ssm_ref.at[pick_smem[0, ROWS + p]], block_ref.at[pl.ds(GATH + p * STATE, STATE)], sems.at[2]
        ).start()

    def send(p, carry):
        pltpu.make_async_copy(ssm_ref.at[pick_smem[0, p]], main_ref.at[p], sems.at[1]).start()
        return carry

    lax.fori_loop(0, ROWS, send, 0)
    buf = jnp.zeros((GROUPS * SLOT, CH), F32)
    sec = bdot(onehot(iota((SEC, COEF), 0) == iota((SEC, COEF), 1)), coef_ref[...])
    for tap in range(3):
        dest = jnp.where(order_row < BASE, to_row * SLOT + order_row * 3 + tap, -1)
        buf += bdot(onehot(iota((GROUPS * SLOT, ROWS), 0) == dest), conv_ref[tap])
        dest = jnp.where(order_row < BASE, -1, COEF + (order_row - BASE) * 3 + tap)
        sec += bdot(onehot(iota((SEC, ROWS), 0) == dest), conv_ref[tap])
    buf_ref[...] = buf.astype(BF)
    block_ref[pl.ds(0, SEC), :] = sec.astype(BF)
    block_ref[pl.ds(SEC, DELTA), :] = delta_ref[...]
    match = (slots_ref[...] == me * ROWS + iota((ROWS, GROUPS * ROWS), 0)).astype(I32)
    inv = jnp.sum(match * iota(match.shape, 1), axis=1, keepdims=True)
    rem_ref[...] = jnp.sum(match * remaining_ref[...], axis=1, keepdims=True)
    inv_row = jnp.sum(jnp.where(eye, inv, 0), axis=0, keepdims=True)
    src = inv // ROWS
    src_row = inv_row // ROWS
    rank = jnp.sum(
        ((src == src_row) & (inv_row < inv)).astype(I32), axis=1, keepdims=True
    )
    rank_row = jnp.sum(
        ((src == src_row) & (inv < inv_row)).astype(I32), axis=0, keepdims=True
    )
    turn = lax.rem(x - lax.rem(src_row, NX) + NX, NX)
    where_row = jnp.where(rank_row < BASE, src_row * BASE + rank_row, ROWS + (turn - 1) * BASE + rank_row)
    gather_ref[...] = jnp.broadcast_to(where_row, gather_ref.shape)
    for tap in range(3):
        at = pl.ds(tap * ROWS, ROWS)
        col_ref[at, :] = jnp.where(rank < BASE, src * SLOT + rank * 3 + tap, -1)
        ext_ref[at, :] = jnp.where(
            rank < BASE, -1, src * SEC + COEF + (rank - BASE) * 3 + tap
        )
    target = table_ref[...] // ROWS
    groups = iota((GROUPS, 1), 0)
    for k in range(NX):
        dest = me - x + lax.rem(x + k, NX)
        count = jnp.sum((target == dest).astype(I32), axis=1, keepdims=True)
        holds = (count > BASE) & (lax.rem(groups, NX) == x)
        z = jnp.sum(jnp.where(holds, groups // NX, 0), axis=0, keepdims=True)
        relay_ref[pl.ds(k, 1), :] = jnp.broadcast_to(z, (1, 128))
    pltpu.make_async_copy(
        ssm_ref.at[pl.ds(0, BASE)].reshape(BASE * STATE, CH), block_ref.at[pl.ds(GATH, BASE * STATE)], sems.at[2]
    ).wait()
    pltpu.make_async_copy(ssm_ref, main_ref, sems.at[1]).wait()
    passed.wait()


def plan(me, slots, remaining, table, conv, coef, delta, ssm, proj):
    shape = jax.ShapeDtypeStruct
    return pl.pallas_call(
        plan_kernel,
        name="plan",
        out_shape=(
            shape((8, ROWS), I32),
            shape((NX, 128), I32),
            shape((ROWS, 1), I32),
            shape((3 * ROWS, 1), I32),
            shape((3 * ROWS, 1), I32),
            shape((GROUPS * SLOT, CH), BF),
            shape((GATH + BASE * STATE, CH), BF),
            shape((ROWS, STATE, CH), BF),
            shape(proj.shape, BF),
        ),
        in_specs=[SMEM] + [VMEM] * 6 + [ANY] * 2,
        out_specs=(VMEM,) * 9,
        scratch_shapes=[
            pltpu.VMEM((8, 128), I32),
            pltpu.SMEM((8, 128), I32),
            pltpu.SemaphoreType.DMA((4,)),
        ],
        compiler_params=pltpu.CompilerParams(vmem_limit_bytes=60 << 20),
    )(me, slots, remaining, table, conv, coef, delta, ssm, proj)


def conv_kernel(
    me_ref, moved_ref, g0, g1, g2, g3, col_ref, ext_ref, rem_ref, inputs_ref, weight_ref, bias_ref,
    act_ref, low_ref, final_ref,
):
    x = me_ref[1]
    parts = (g0, g1, g2, g3)
    span = NZ * SEC
    window = bdot(onehot(col_ref[...] == iota((3 * ROWS, GROUPS * SLOT), 1)), moved_ref[...])
    coef = jnp.zeros((LOW, CH), F32)
    for k, part in enumerate(parts):
        at = iota((1, span), 1)
        z, q = at // SEC, at % SEC
        group = z * NX + lax.rem(x - k + NX, NX)
        ext = onehot(ext_ref[...] == group * SEC + q)
        window += bdot(ext, part[...])
        row = jnp.where(q < COEF, group * COEF + q, -1)
        coef += bdot(onehot(iota((LOW, span), 0) == row), part[...])
    coef = coef.astype(BF)
    taps = [window[tap * ROWS : (tap + 1) * ROWS] for tap in range(3)]
    taps += [inputs_ref[t].astype(F32) for t in range(STEPS)]
    weight = weight_ref[...]
    for t in range(STEPS):
        out = bias_ref[...] + sum(taps[t + k] * weight[k : k + 1] for k in range(4))
        act = out / (1.0 + jnp.exp(-out))
        act_ref[t] = act
        low_ref[pl.ds(t * ROWS, ROWS), :] = bdot_t(act.astype(BF), coef).astype(BF)
    rem = rem_ref[...]
    for k in range(3):
        kept = taps[k]
        for t in range(1, STEPS + 1):
            kept = jnp.where(rem >= t, taps[t + k], kept)
        final_ref[k] = kept.astype(BF)


def conv_stage(me, moved, parts, col, ext, rem, inputs, weight, bias):
    shape = jax.ShapeDtypeStruct
    return pl.pallas_call(
        conv_kernel,
        name="conv",
        out_shape=(
            shape((STEPS, ROWS, CH), F32),
            shape((STEPS * ROWS, LOW), BF),
            shape((3, ROWS, CH), BF),
        ),
        in_specs=[SMEM] + [VMEM] * 11,
        out_specs=(VMEM,) * 3,
        compiler_params=pltpu.CompilerParams(vmem_limit_bytes=60 << 20),
    )(me, moved, *parts, col, ext, rem, inputs, weight, bias)


def step_kernel(
    me_ref, own_ref, other_ref, g0, g1, g2, g3, bias_ref, act_ref, gate_ref, skip_ref, rem_ref, log_ref,
    dt_ref, dx_ref, sk_ref, sg_ref, bc_ref, rate_ref, low_ref,
):
    x, y, c = me_ref[1], me_ref[2], me_ref[3]
    rate_ref[...] = -jnp.exp(log_ref[...]) * LOG2E
    chunk = STEPS * ROWS // (NY * NC)
    for half, piece in ((c, own_ref), (1 - c, other_ref)):
        for m in range(NY):
            at = half * NY + lax.rem(y + m, NY)
            low_ref[pl.ds(pl.multiple_of(at * chunk, 16), chunk), :] = piece[m]
    span = NZ * DELTA
    delta = jnp.zeros((RANK, CH), F32)
    for k, part in enumerate((g0, g1, g2, g3)):
        at = iota((1, span), 1)
        z, q = at // DELTA, at % DELTA
        row = (z * NX + lax.rem(x - k + NX, NX)) * DELTA + q
        delta += bdot(onehot(iota((RANK, span), 0) == row), part[...])
    delta = delta.astype(BF)
    rem = rem_ref[...]
    for t in range(STEPS):
        low = low_ref[pl.ds(t * ROWS, ROWS), :]
        raw = bdot(low[:, :RANK], delta) + bias_ref[...]
        size = jnp.maximum(raw, 0.0) + jnp.log1p(jnp.exp(-jnp.abs(raw)))
        active = rem > t
        size = jnp.where(active, size, 0.0)
        act = act_ref[t]
        gate = gate_ref[t].astype(F32)
        dt_ref[t] = size
        dx_ref[t] = size * act
        sk_ref[t] = skip_ref[...] * act
        sg_ref[t] = jnp.where(active, gate / (1.0 + jnp.exp(-gate)), 0.0)
        coefs = low[:, RANK:].astype(F32)
        for n in range(2 * STATE):
            bc_ref[t, n] = jnp.broadcast_to(coefs[:, n : n + 1], (ROWS, 128))


def step_stage(me, own, other, parts, bias, act, gate, skip, rem, log):
    shape = jax.ShapeDtypeStruct
    rows = shape((STEPS, ROWS, CH), F32)
    return pl.pallas_call(
        step_kernel,
        name="sizes",
        out_shape=(rows, rows, rows, rows, shape((STEPS, 2 * STATE, ROWS, 128), F32), shape((STATE, CH), F32)),
        in_specs=[SMEM] + [VMEM] * 12,
        out_specs=(VMEM,) * 6,
        scratch_shapes=[pltpu.VMEM((STEPS * ROWS, LOW), BF)],
        compiler_params=pltpu.CompilerParams(vmem_limit_bytes=60 << 20),
    )(me, own, other, *parts, bias, act, gate, skip, rem, log)


BLOCK = 8
BLOCKS = ROWS // BLOCK


def scan_kernel(
    at_ref, main_ref, e0, e1, e2, e3, _ours, _theirs, dt_ref, dx_ref, sk_ref, sg_ref, bc_ref, rate_ref,
    out_ref, final_ref, held, wide, sems,
):
    b = pl.program_id(0)

    def fetch(block):
        for i in range(BLOCK):
            at = at_ref[0, block * BLOCK + i]

            @pl.when(at < ROWS)
            def _():
                pltpu.make_async_copy(main_ref.at[at], held.at[block, i], sems.at[block]).start()

            for k, extra in enumerate((e0, e1, e2, e3)):
                row = at - ROWS - k * BASE

                @pl.when((row >= 0) & (row < BASE))
                def _(row=row, extra=extra):
                    pltpu.make_async_copy(extra.at[row], held.at[block, i], sems.at[block]).start()

    @pl.when(b == 0)
    def _():
        for block in range(3):
            fetch(block)

    @pl.when(b + 3 < BLOCKS)
    def _():
        fetch(b + 3)

    pltpu.make_async_copy(main_ref.at[pl.ds(0, BLOCK)], held.at[b], sems.at[b]).wait()
    for i in range(BLOCK):
        for l in range(CH // 128):
            wide[l, pl.ds(i * STATE, STATE), :] = held[b, i, :, pl.ds(l * 128, 128)].astype(F32)

    def lanes(l, carry):
        cols = pl.ds(pl.multiple_of(l * 128, 128), 128)
        dts = [dt_ref[t, :, cols] for t in range(STEPS)]
        dxs = [dx_ref[t, :, cols] for t in range(STEPS)]
        sums = [sk_ref[t, :, cols] for t in range(STEPS)]
        for n in range(STATE):
            here = pl.ds(n, BLOCK, stride=STATE)
            h = wide[l, here, :]
            rate = jnp.broadcast_to(rate_ref[pl.ds(n, 1), cols], (BLOCK, 128))
            for t in range(STEPS):
                h = jnp.exp2(dts[t] * rate) * h + dxs[t] * bc_ref[t, n]
                sums[t] += h * bc_ref[t, STATE + n]
            wide[l, here, :] = h
        for t in range(STEPS):
            out_ref[t, :, cols] = (sums[t] * sg_ref[t, :, cols]).astype(BF)
        return carry

    lax.fori_loop(0, CH // 128, lanes, 0)
    for i in range(BLOCK):
        for l in range(CH // 128):
            final_ref[i, :, pl.ds(l * 128, 128)] = wide[l, pl.ds(i * STATE, STATE), :].astype(BF)


def scan_stage(at, main, extras, ahead, dt, dx, sk, sg, bc, rate):
    shape = jax.ShapeDtypeStruct
    rows = pl.BlockSpec((STEPS, BLOCK, CH), lambda b, at: (0, b, 0))
    return pl.pallas_call(
        scan_kernel,
        name="scan",
        out_shape=(shape((STEPS, ROWS, CH), BF), shape((ROWS, STATE, CH), BF)),
        grid_spec=pltpu.PrefetchScalarGridSpec(
            num_scalar_prefetch=1,
            grid=(BLOCKS,),
            in_specs=[ANY] * 7
            + [
                rows,
                rows,
                rows,
                rows,
                pl.BlockSpec((STEPS, 2 * STATE, BLOCK, 128), lambda b, at: (0, 0, b, 0)),
                pl.BlockSpec((STATE, CH), lambda b, at: (0, 0)),
            ],
            out_specs=(rows, pl.BlockSpec((BLOCK, STATE, CH), lambda b, at: (b, 0, 0))),
            scratch_shapes=[
                pltpu.VMEM((BLOCKS, BLOCK, STATE, CH), BF),
                pltpu.VMEM((CH // 128, BLOCK * STATE, 128), F32),
                pltpu.SemaphoreType.DMA((BLOCKS,)),
            ],
        ),
        compiler_params=pltpu.CompilerParams(vmem_limit_bytes=60 << 20),
    )(at, main, *extras, *ahead, dt, dx, sk, sg, bc, rate)


def shift(value, axis, size, k):
    return lax.ppermute(value, axis, [(i, (i + k) % size) for i in range(size)])


def reduce_mp(low, y, c):
    chunk = STEPS * ROWS // (NY * NC)
    halves = low.reshape(NC, NY * chunk, LOW)
    got = shift(lax.dynamic_index_in_dim(halves, 1 - c, 0, False), "c", NC, 1)
    mine = lax.dynamic_index_in_dim(halves, c, 0, False).astype(F32) + got.astype(F32)
    quarters = mine.reshape(NY, chunk, LOW)
    rounded = quarters.astype(BF)
    total = lax.dynamic_index_in_dim(quarters, y, 0, False)
    came = [
        shift(lax.dynamic_index_in_dim(rounded, lax.rem(y + k, NY), 0, False), "y", NY, k)
        for k in range(1, NY)
    ]
    total = (total + came[0].astype(F32) + came[1].astype(F32) + came[2].astype(F32)).astype(BF)
    own = jnp.stack([total] + [shift(total, "y", NY, NY - m) for m in range(1, NY)])
    return own, shift(own, "c", NC, 1)


def mix(rows, ours, theirs, x, y):
    width = ours.shape[1] // NY
    visits = [rows] + [shift(rows, "x", NX, k) for k in range(1, NX)]
    pieces = []
    for visit in visits:
        got = shift(bdot(visit, theirs).astype(BF), "c", NC, 1)
        pieces.append((bdot(visit, ours) + got.astype(F32)).astype(BF))

    def over_y(some):
        def block(s):
            at = lax.rem(y + s, NY) * width
            return [lax.dynamic_slice_in_dim(piece, at, width, 1) for piece in some]

        total = jnp.concatenate(block(0), axis=0).astype(F32)
        for s in range(1, NY):
            total += shift(jnp.concatenate(block(s), axis=0), "y", NY, s).astype(F32)
        return total.astype(BF).reshape(len(some), rows.shape[0], width)

    first, rest = over_y(pieces[:1]), over_y(pieces[1:])
    back = [first[0]] + [shift(rest[k - 1], "x", NX, NX - k) for k in range(1, NX)]
    twice = jnp.stack(back + back)
    ordered = lax.dynamic_slice_in_dim(twice, lax.rem(NX - x, NX), NX, 0)
    return ordered.transpose(1, 0, 2)


def per_device(
    input_steps, gate_steps, conv_state, ssm_state, new_slot, remaining, conv_weight, conv_bias,
    coef_proj, delta_proj, delta_bias, decay_log, skip_gain, out_proj,
):
    z, x, y, c = (lax.axis_index(name) for name in ("z", "x", "y", "c"))
    group = z * NX + x
    me = jnp.stack([group, x, y, c]).astype(I32)
    at, relay, rem, col, ext, buf, block, main, proj = plan(
        me,
        new_slot.reshape(1, -1),
        remaining.reshape(1, -1),
        new_slot.reshape(GROUPS, ROWS),
        conv_state.transpose(1, 0, 2),
        coef_proj.T,
        delta_proj,
        ssm_state,
        out_proj,
    )
    gathered = lax.all_gather(block, "z", axis=0)
    moved = lax.all_to_all(
        buf.reshape(GROUPS, SLOT, CH), ("z", "x"), split_axis=0, concat_axis=0, tiled=True
    ).reshape(GROUPS * SLOT, CH)
    columns = lax.all_gather(proj, "z", axis=1, tiled=True).reshape(CH, NY, NC, -1)
    halves = [lax.dynamic_index_in_dim(columns, core, 2, False).reshape(CH, -1) for core in (c, 1 - c)]
    ssm_main = lax.all_to_all(main, ("z", "x"), split_axis=0, concat_axis=0, tiled=True)

    def turned(value):
        return [value] + [shift(value, "x", NX, k) for k in range(1, NX)]

    secs = turned(gathered[:, :SEC].reshape(NZ * SEC, CH))
    deltas = turned(gathered[:, SEC:GATH].reshape(NZ * DELTA, CH))
    extras = [
        lax.dynamic_slice(gathered, (relay[k, 0], GATH, 0), (1, BASE * STATE, CH)) for k in range(NX)
    ]
    extras = [extras[0]] + [shift(extras[k], "x", NX, k) for k in range(1, NX)]
    extras = [e.reshape(BASE, STATE, CH) for e in extras]
    act, low, conv_final = conv_stage(
        me, moved, secs, col, ext, rem, input_steps, conv_weight, conv_bias.reshape(1, -1)
    )
    own, other = reduce_mp(low, y, c)
    dt, dx, sk, sg, bc, rate = step_stage(
        me, own, other, deltas, delta_bias.reshape(1, -1), act, gate_steps, skip_gain.reshape(1, -1), rem, decay_log
    )
    stepped, ssm_final = scan_stage(at, ssm_main, extras, halves, dt, dx, sk, sg, bc, rate)
    mixed = mix(stepped.reshape(STEPS * ROWS, CH), *halves, x, y)
    return mixed.reshape(STEPS, ROWS, -1), conv_final.transpose(1, 0, 2), ssm_final


def solution(mesh):
    fine = Mesh(mesh.devices.reshape(NZ, NX, NY, NC), ("z", "x", "y", "c"))
    dp, mp = ("z", "x"), ("y", "c")
    return jax.shard_map(
        per_device,
        mesh=fine,
        in_specs=(
            P(None, dp, mp),
            P(None, dp, mp),
            P(dp, None, mp),
            P(dp, None, mp),
            P(),
            P(),
            P(None, mp),
            P(mp),
            P(mp, dp),
            P(dp, mp),
            P(mp),
            P(None, mp),
            P(mp),
            P(mp, dp),
        ),
        out_specs=(P(None, dp, mp), P(dp, None, mp), P(dp, None, mp)),
        check_vma=False,
    )
```

```python
import functools

import jax
import jax.numpy as jnp
from jax import lax
from jax.experimental import pallas as pl
from jax.experimental.pallas import tpu as pltpu
from jax.sharding import Mesh
from jax.sharding import PartitionSpec as P

BF = jnp.bfloat16
F32 = jnp.float32
I32 = jnp.int32
NZ, NX, NY, NC = 8, 4, 4, 2
GROUPS = NZ * NX
ROWS = 96
CH = 1024
STATE = 16
RANK = 512
STEPS = 4
LOW = RANK + 2 * STATE
COEF = LOW // GROUPS
DELTA = RANK // GROUPS
BASE = ROWS // GROUPS
SLOT = 16
SEC = 32
LOG2E = 1.4426950408889634
VMEM = pl.BlockSpec(memory_space=pltpu.VMEM)
SMEM = pl.BlockSpec(memory_space=pltpu.SMEM)
ANY = pl.BlockSpec(memory_space=pl.ANY)


def iota(shape, dim):
    return lax.broadcasted_iota(I32, shape, dim)


def bdot(a, b):
    return jnp.dot(a, b, preferred_element_type=F32)


def bdot_t(a, b):
    return lax.dot_general(a, b, (((1,), (1,)), ((), ())), preferred_element_type=F32)


def onehot(cond):
    return cond.astype(F32).astype(BF)


def plan_kernel(
    me_ref, slots_ref, remaining_ref, table_ref, conv_ref, proj_ref, ssm_ref,
    gather_ref, relay_ref, rem_ref, col_ref, ext_ref, buf_ref, block_ref, main_ref, proj_out_ref,
    pick_ref, pick_smem, sems,
):
    me = me_ref[0]
    x = me_ref[1]
    square = (ROWS, ROWS)
    eye = iota(square, 0) == iota(square, 1)
    to_row = table_ref[pl.ds(me, 1), :] // ROWS
    to = jnp.sum(jnp.where(eye, to_row, 0), axis=1, keepdims=True)
    same = to == to_row
    order_row = jnp.sum((same & (iota(square, 0) < iota(square, 1))).astype(I32), axis=0, keepdims=True)
    order = jnp.sum((same & (iota(square, 1) < iota(square, 0))).astype(I32), axis=1, keepdims=True)
    place = jnp.where(order < BASE, to * BASE + order, ROWS + order - BASE)
    lanes = (ROWS, 128)
    picked = jnp.sum(jnp.where(place == iota(lanes, 1), iota(lanes, 0), 0), axis=0, keepdims=True)
    pick_ref[...] = jnp.broadcast_to(picked, pick_ref.shape)
    picking = pltpu.make_async_copy(pick_ref, pick_smem, sems.at[0])
    picking.start()
    picking.wait()
    for p in range(BASE):
        pltpu.make_async_copy(
            ssm_ref.at[pick_smem[0, ROWS + p]], block_ref.at[pl.ds(SLOT + p * STATE, STATE)], sems.at[2]
        ).start()

    def send(p, carry):
        pltpu.make_async_copy(ssm_ref.at[pick_smem[0, p]], main_ref.at[p], sems.at[1]).start()
        return carry

    lax.fori_loop(0, ROWS, send, 0)
    buf = jnp.zeros((GROUPS * SLOT, CH), F32)
    sec = jnp.zeros((SLOT, CH), F32)
    for tap in range(3):
        dest = jnp.where(order_row < BASE, to_row * SLOT + order_row * 3 + tap, -1)
        buf += bdot(onehot(iota((GROUPS * SLOT, ROWS), 0) == dest), conv_ref[tap])
        dest = jnp.where(order_row < BASE, -1, (order_row - BASE) * 3 + tap)
        sec += bdot(onehot(iota((SLOT, ROWS), 0) == dest), conv_ref[tap])
    buf_ref[...] = buf.astype(BF)
    block_ref[pl.ds(0, SLOT), :] = sec.astype(BF)
    match = (slots_ref[...] == me * ROWS + iota((ROWS, GROUPS * ROWS), 0)).astype(I32)
    inv = jnp.sum(match * iota(match.shape, 1), axis=1, keepdims=True)
    rem_ref[...] = jnp.sum(match * remaining_ref[...], axis=1, keepdims=True)
    inv_row = jnp.sum(jnp.where(eye, inv, 0), axis=0, keepdims=True)
    src = inv // ROWS
    src_row = inv_row // ROWS
    rank = jnp.sum(
        ((src == src_row) & (inv_row < inv)).astype(I32), axis=1, keepdims=True
    )
    rank_row = jnp.sum(
        ((src == src_row) & (inv < inv_row)).astype(I32), axis=0, keepdims=True
    )
    turn_row = lax.rem(x - lax.rem(src_row, NX) + NX, NX)
    turn = lax.rem(x - lax.rem(src, NX) + NX, NX)
    where_row = jnp.where(rank_row < BASE, src_row * BASE + rank_row, ROWS + (turn_row - 1) * BASE + rank_row)
    gather_ref[...] = jnp.broadcast_to(where_row, gather_ref.shape)
    for tap in range(3):
        at = pl.ds(tap * ROWS, ROWS)
        col_ref[at, :] = jnp.where(rank < BASE, src * SLOT + rank * 3 + tap, -1)
        ext_ref[at, :] = jnp.where(
            rank < BASE, -1, turn * SLOT + (rank - BASE) * 3 + tap
        )
    target = table_ref[...] // ROWS
    groups = iota((GROUPS, 1), 0)
    for k in range(NX):
        dest = me - x + lax.rem(x + k, NX)
        count = jnp.sum((target == dest).astype(I32), axis=1, keepdims=True)
        holds = (count > BASE) & (lax.rem(groups, NX) == x)
        z = jnp.sum(jnp.where(holds, groups // NX, 0), axis=0, keepdims=True)
        relay_ref[pl.ds(k, 1), :] = jnp.broadcast_to(z, (1, 128))
    pltpu.make_async_copy(
        ssm_ref.at[pl.ds(0, BASE)].reshape(BASE * STATE, CH), block_ref.at[pl.ds(SLOT, BASE * STATE)], sems.at[2]
    ).wait()
    pltpu.make_async_copy(ssm_ref, main_ref, sems.at[1]).wait()
    proj_out_ref[...] = proj_ref[...].T


def plan(me, slots, remaining, table, conv, proj, ssm):
    shape = jax.ShapeDtypeStruct
    return pl.pallas_call(
        plan_kernel,
        name="plan",
        out_shape=(
            shape((8, ROWS), I32),
            shape((NX, 128), I32),
            shape((ROWS, 1), I32),
            shape((3 * ROWS, 1), I32),
            shape((3 * ROWS, 1), I32),
            shape((GROUPS * SLOT, CH), BF),
            shape((SLOT + BASE * STATE, CH), BF),
            shape((ROWS, STATE, CH), BF),
            shape(proj.shape[::-1], BF),
        ),
        in_specs=[SMEM] + [VMEM] * 5 + [ANY],
        out_specs=(VMEM,) * 9,
        scratch_shapes=[
            pltpu.VMEM((8, 128), I32),
            pltpu.SMEM((8, 128), I32),
            pltpu.SemaphoreType.DMA((3,)),
        ],
        compiler_params=pltpu.CompilerParams(vmem_limit_bytes=60 << 20),
    )(me, slots, remaining, table, conv, proj, ssm)


def conv_kernel(
    me_ref, moved_ref, g0, g1, g2, g3, e0, e1, e2, e3, col_ref, ext_ref, rem_ref, inputs_ref, weight_ref, bias_ref,
    act_ref, low_ref, final_ref,
):
    x = me_ref[1]
    parts = (g0, g1, g2, g3)
    span = NZ * SEC
    window = bdot(onehot(col_ref[...] == iota((3 * ROWS, GROUPS * SLOT), 1)), moved_ref[...])
    for k, part in enumerate((e0, e1, e2, e3)):
        ext = onehot(ext_ref[...] == k * SLOT + iota((3 * ROWS, SLOT), 1))
        window += bdot(ext, part[pl.ds(0, SLOT), :])
    coef = jnp.zeros((LOW, CH), F32)
    for k, part in enumerate(parts):
        at = iota((1, span), 1)
        z, q = at // SEC, at % SEC
        group = z * NX + lax.rem(x - k + NX, NX)
        row = jnp.where(q < COEF, group * COEF + q, -1)
        coef += bdot(onehot(iota((LOW, span), 0) == row), part[...])
    coef = coef.astype(BF)
    taps = [window[tap * ROWS : (tap + 1) * ROWS] for tap in range(3)]
    taps += [inputs_ref[t].astype(F32) for t in range(STEPS)]
    weight = weight_ref[...]
    for t in range(STEPS):
        out = bias_ref[...] + sum(taps[t + k] * weight[k : k + 1] for k in range(4))
        act = out / (1.0 + jnp.exp(-out))
        act_ref[t] = act
        low_ref[pl.ds(t * ROWS, ROWS), :] = bdot_t(act.astype(BF), coef).astype(BF)
    rem = rem_ref[...]
    for k in range(3):
        kept = taps[k]
        for t in range(1, STEPS + 1):
            kept = jnp.where(rem >= t, taps[t + k], kept)
        final_ref[k] = kept.astype(BF)


def conv_stage(me, moved, parts, extras, col, ext, rem, inputs, weight, bias):
    shape = jax.ShapeDtypeStruct
    return pl.pallas_call(
        conv_kernel,
        name="conv",
        out_shape=(
            shape((STEPS, ROWS, CH), F32),
            shape((STEPS * ROWS, LOW), BF),
            shape((3, ROWS, CH), BF),
        ),
        in_specs=[SMEM] + [VMEM] * 15,
        out_specs=(VMEM,) * 3,
        compiler_params=pltpu.CompilerParams(vmem_limit_bytes=60 << 20),
    )(me, moved, *parts, *extras, col, ext, rem, inputs, weight, bias)


def step_kernel(
    me_ref, own_ref, other_ref, g0, g1, g2, g3, bias_ref, act_ref, gate_ref, skip_ref, rem_ref, log_ref,
    dt_ref, dx_ref, sk_ref, sg_ref, bc_ref, rate_ref, low_ref,
):
    x, y, c = me_ref[1], me_ref[2], me_ref[3]
    rate_ref[...] = -jnp.exp(log_ref[...]) * LOG2E
    chunk = STEPS * ROWS // (NY * NC)
    for half, piece in ((c, own_ref), (1 - c, other_ref)):
        for m in range(NY):
            at = half * NY + lax.rem(y + m, NY)
            low_ref[pl.ds(pl.multiple_of(at * chunk, 16), chunk), :] = piece[m]
    span = NZ * DELTA
    delta = jnp.zeros((RANK, CH), F32)
    for k, part in enumerate((g0, g1, g2, g3)):
        at = iota((1, span), 1)
        z, q = at // DELTA, at % DELTA
        row = (z * NX + lax.rem(x - k + NX, NX)) * DELTA + q
        delta += bdot(onehot(iota((RANK, span), 0) == row), part[...])
    delta = delta.astype(BF)
    rem = rem_ref[...]
    for t in range(STEPS):
        low = low_ref[pl.ds(t * ROWS, ROWS), :]
        raw = bdot(low[:, :RANK], delta) + bias_ref[...]
        size = jnp.maximum(raw, 0.0) + jnp.log1p(jnp.exp(-jnp.abs(raw)))
        active = rem > t
        size = jnp.where(active, size, 0.0)
        act = act_ref[t]
        gate = gate_ref[t].astype(F32)
        dt_ref[t] = size
        dx_ref[t] = size * act
        sk_ref[t] = skip_ref[...] * act
        sg_ref[t] = jnp.where(active, gate / (1.0 + jnp.exp(-gate)), 0.0)
        coefs = low[:, RANK:].astype(F32)
        for n in range(2 * STATE):
            bc_ref[t, n] = jnp.broadcast_to(coefs[:, n : n + 1], (ROWS, 128))


def step_stage(me, own, other, parts, bias, act, gate, skip, rem, log):
    shape = jax.ShapeDtypeStruct
    rows = shape((STEPS, ROWS, CH), F32)
    return pl.pallas_call(
        step_kernel,
        name="sizes",
        out_shape=(rows, rows, rows, rows, shape((STEPS, 2 * STATE, ROWS, 128), F32), shape((STATE, CH), F32)),
        in_specs=[SMEM] + [VMEM] * 12,
        out_specs=(VMEM,) * 6,
        scratch_shapes=[pltpu.VMEM((STEPS * ROWS, LOW), BF)],
        compiler_params=pltpu.CompilerParams(vmem_limit_bytes=60 << 20),
    )(me, own, other, *parts, bias, act, gate, skip, rem, log)


BLOCK = 8
BLOCKS = ROWS // BLOCK


def scan_kernel(
    at_ref, main_ref, e0, e1, e2, e3, _ours, _theirs, dt_ref, dx_ref, sk_ref, sg_ref, bc_ref, rate_ref,
    out_ref, final_ref, held, wide, sems,
):
    b = pl.program_id(0)

    def fetch(block):
        for i in range(BLOCK):
            at = at_ref[0, block * BLOCK + i]

            @pl.when(at < ROWS)
            def _():
                pltpu.make_async_copy(main_ref.at[at], held.at[block, i], sems.at[block]).start()

            for k, extra in enumerate((e0, e1, e2, e3)):
                row = at - ROWS - k * BASE

                @pl.when((row >= 0) & (row < BASE))
                def _(row=row, extra=extra):
                    pltpu.make_async_copy(extra.at[pl.ds(SLOT + row * STATE, STATE)], held.at[block, i], sems.at[block]).start()

    @pl.when(b == 0)
    def _():
        for block in range(3):
            fetch(block)

    @pl.when(b + 3 < BLOCKS)
    def _():
        fetch(b + 3)

    pltpu.make_async_copy(main_ref.at[pl.ds(0, BLOCK)], held.at[b], sems.at[b]).wait()
    for i in range(BLOCK):
        for l in range(CH // 128):
            wide[l, pl.ds(i * STATE, STATE), :] = held[b, i, :, pl.ds(l * 128, 128)].astype(F32)

    def lanes(l, carry):
        cols = pl.ds(pl.multiple_of(l * 128, 128), 128)
        dts = [dt_ref[t, :, cols] for t in range(STEPS)]
        dxs = [dx_ref[t, :, cols] for t in range(STEPS)]
        sums = [sk_ref[t, :, cols] for t in range(STEPS)]
        for n in range(STATE):
            here = pl.ds(n, BLOCK, stride=STATE)
            h = wide[l, here, :]
            rate = jnp.broadcast_to(rate_ref[pl.ds(n, 1), cols], (BLOCK, 128))
            for t in range(STEPS):
                h = jnp.exp2(dts[t] * rate) * h + dxs[t] * bc_ref[t, n]
                sums[t] += h * bc_ref[t, STATE + n]
            wide[l, here, :] = h
        for t in range(STEPS):
            out_ref[t, :, cols] = (sums[t] * sg_ref[t, :, cols]).astype(BF)
        return carry

    lax.fori_loop(0, CH // 128, lanes, 0)
    for i in range(BLOCK):
        for l in range(CH // 128):
            final_ref[i, :, pl.ds(l * 128, 128)] = wide[l, pl.ds(i * STATE, STATE), :].astype(BF)


def scan_stage(at, main, extras, ahead, dt, dx, sk, sg, bc, rate):
    shape = jax.ShapeDtypeStruct
    rows = pl.BlockSpec((STEPS, BLOCK, CH), lambda b, at: (0, b, 0))
    return pl.pallas_call(
        scan_kernel,
        name="scan",
        out_shape=(shape((STEPS, ROWS, CH), BF), shape((ROWS, STATE, CH), BF)),
        grid_spec=pltpu.PrefetchScalarGridSpec(
            num_scalar_prefetch=1,
            grid=(BLOCKS,),
            in_specs=[ANY] * 7
            + [
                rows,
                rows,
                rows,
                rows,
                pl.BlockSpec((STEPS, 2 * STATE, BLOCK, 128), lambda b, at: (0, 0, b, 0)),
                pl.BlockSpec((STATE, CH), lambda b, at: (0, 0)),
            ],
            out_specs=(rows, pl.BlockSpec((BLOCK, STATE, CH), lambda b, at: (b, 0, 0))),
            scratch_shapes=[
                pltpu.VMEM((BLOCKS, BLOCK, STATE, CH), BF),
                pltpu.VMEM((CH // 128, BLOCK * STATE, 128), F32),
                pltpu.SemaphoreType.DMA((BLOCKS,)),
            ],
        ),
        compiler_params=pltpu.CompilerParams(vmem_limit_bytes=60 << 20),
    )(at, main, *extras, *ahead, dt, dx, sk, sg, bc, rate)


def shift(value, axis, size, k):
    return lax.ppermute(value, axis, [(i, (i + k) % size) for i in range(size)])


def reduce_mp(low, y, c):
    chunk = STEPS * ROWS // (NY * NC)
    halves = low.reshape(NC, NY * chunk, LOW)
    got = shift(lax.dynamic_index_in_dim(halves, 1 - c, 0, False), "c", NC, 1)
    mine = lax.dynamic_index_in_dim(halves, c, 0, False).astype(F32) + got.astype(F32)
    quarters = mine.reshape(NY, chunk, LOW)
    rounded = quarters.astype(BF)
    total = lax.dynamic_index_in_dim(quarters, y, 0, False)
    came = [
        shift(lax.dynamic_index_in_dim(rounded, lax.rem(y + k, NY), 0, False), "y", NY, k)
        for k in range(1, NY)
    ]
    total = (total + came[0].astype(F32) + came[1].astype(F32) + came[2].astype(F32)).astype(BF)
    own = jnp.stack([total] + [shift(total, "y", NY, NY - m) for m in range(1, NY)])
    return own, shift(own, "c", NC, 1)


def mix(rows, ours, theirs, x, y):
    width = ours.shape[0] // NY
    visits = [rows] + [shift(rows, "x", NX, k) for k in range(1, NX)]
    pieces = []
    for visit in visits:
        got = shift(bdot_t(visit, theirs).astype(BF), "c", NC, 1)
        pieces.append((bdot_t(visit, ours) + got.astype(F32)).astype(BF))

    def over_y(some):
        def block(s):
            at = lax.rem(y + s, NY) * width
            return [lax.dynamic_slice_in_dim(piece, at, width, 1) for piece in some]

        total = jnp.concatenate(block(0), axis=0).astype(F32)
        for s in range(1, NY):
            total += shift(jnp.concatenate(block(s), axis=0), "y", NY, s).astype(F32)
        return total.astype(BF).reshape(len(some), rows.shape[0], width)

    first, rest = over_y(pieces[:1]), over_y(pieces[1:])
    back = [first[0]] + [shift(rest[k - 1], "x", NX, NX - k) for k in range(1, NX)]
    twice = jnp.stack(back + back)
    ordered = lax.dynamic_slice_in_dim(twice, lax.rem(NX - x, NX), NX, 0)
    return ordered.transpose(1, 0, 2)


def per_device(
    input_steps, gate_steps, conv_state, ssm_state, new_slot, remaining, conv_weight, conv_bias,
    coef_proj, delta_proj, delta_bias, decay_log, skip_gain, out_proj,
):
    z, x, y, c = (lax.axis_index(name) for name in ("z", "x", "y", "c"))
    group = z * NX + x
    me = jnp.stack([group, x, y, c]).astype(I32)
    first = jnp.concatenate([delta_proj, coef_proj.T, jnp.zeros((2 * SEC - COEF - DELTA, CH), BF)], axis=0)
    gathered = lax.all_gather(first, "z", axis=0)
    at, relay, rem, col, ext, buf, block, main, proj = plan(
        me,
        new_slot.reshape(1, -1),
        remaining.reshape(1, -1),
        new_slot.reshape(GROUPS, ROWS),
        conv_state.transpose(1, 0, 2),
        out_proj,
        ssm_state,
    )
    moved = lax.all_to_all(
        buf.reshape(GROUPS, SLOT, CH), ("z", "x"), split_axis=0, concat_axis=0, tiled=True
    ).reshape(GROUPS * SLOT, CH)
    blocks = lax.all_gather(block, "z", axis=0)
    columns = lax.all_gather(proj, "z", axis=0).reshape(NY, NC, -1, CH)
    halves = [lax.dynamic_index_in_dim(columns, core, 1, False).reshape(-1, CH) for core in (c, 1 - c)]
    ssm_main = lax.all_to_all(main, ("z", "x"), split_axis=0, concat_axis=0, tiled=True)

    def turned(value):
        return [value] + [shift(value, "x", NX, k) for k in range(1, NX)]

    secs = turned(gathered[:, DELTA : DELTA + SEC].reshape(NZ * SEC, CH))
    deltas = turned(gathered[:, :DELTA].reshape(NZ * DELTA, CH))
    extras = [lax.dynamic_index_in_dim(blocks, relay[k, 0], 0, False) for k in range(NX)]
    extras = [extras[0]] + [shift(extras[k], "x", NX, k) for k in range(1, NX)]
    act, low, conv_final = conv_stage(
        me, moved, secs, extras, col, ext, rem, input_steps, conv_weight, conv_bias.reshape(1, -1)
    )
    own, other = reduce_mp(low, y, c)
    dt, dx, sk, sg, bc, rate = step_stage(
        me, own, other, deltas, delta_bias.reshape(1, -1), act, gate_steps, skip_gain.reshape(1, -1), rem, decay_log
    )
    stepped, ssm_final = scan_stage(at, ssm_main, extras, halves, dt, dx, sk, sg, bc, rate)
    mixed = mix(stepped.reshape(STEPS * ROWS, CH), *halves, x, y)
    return mixed.reshape(STEPS, ROWS, -1), conv_final.transpose(1, 0, 2), ssm_final


def solution(mesh):
    fine = Mesh(mesh.devices.reshape(NZ, NX, NY, NC), ("z", "x", "y", "c"))
    dp, mp = ("z", "x"), ("y", "c")
    return jax.shard_map(
        per_device,
        mesh=fine,
        in_specs=(
            P(None, dp, mp),
            P(None, dp, mp),
            P(dp, None, mp),
            P(dp, None, mp),
            P(),
            P(),
            P(None, mp),
            P(mp),
            P(mp, dp),
            P(dp, mp),
            P(mp),
            P(None, mp),
            P(mp),
            P(mp, dp),
        ),
        out_specs=(P(None, dp, mp), P(dp, None, mp), P(dp, None, mp)),
        check_vma=False,
    )
```

```python
import functools

import jax
import jax.numpy as jnp
from jax import lax
from jax.experimental import pallas as pl
from jax.experimental.pallas import tpu as pltpu
from jax.sharding import Mesh
from jax.sharding import PartitionSpec as P

BF = jnp.bfloat16
F32 = jnp.float32
I32 = jnp.int32
NZ, NX, NY, NC = 8, 4, 4, 2
GROUPS = NZ * NX
ROWS = 96
CH = 1024
STATE = 16
RANK = 512
STEPS = 4
LOW = RANK + 2 * STATE
COEF = LOW // GROUPS
DELTA = RANK // GROUPS
BASE = ROWS // GROUPS
SLOT = 16
SEC = 32
GATH = SEC + DELTA
LOG2E = 1.4426950408889634
VMEM = pl.BlockSpec(memory_space=pltpu.VMEM)
SMEM = pl.BlockSpec(memory_space=pltpu.SMEM)
ANY = pl.BlockSpec(memory_space=pl.ANY)


def iota(shape, dim):
    return lax.broadcasted_iota(I32, shape, dim)


def bdot(a, b):
    return jnp.dot(a, b, preferred_element_type=F32)


def bdot_t(a, b):
    return lax.dot_general(a, b, (((1,), (1,)), ((), ())), preferred_element_type=F32)


def onehot(cond):
    return cond.astype(F32).astype(BF)


def plan_kernel(
    me_ref, slots_ref, remaining_ref, table_ref, conv_ref, coef_ref, delta_ref, proj_ref, ssm_ref,
    gather_ref, relay_ref, rem_ref, col_ref, ext_ref, buf_ref, block_ref, main_ref, proj_out_ref,
    pick_ref, pick_smem, sems,
):
    me = me_ref[0]
    x = me_ref[1]
    square = (ROWS, ROWS)
    eye = iota(square, 0) == iota(square, 1)
    to_row = table_ref[pl.ds(me, 1), :] // ROWS
    to = jnp.sum(jnp.where(eye, to_row, 0), axis=1, keepdims=True)
    same = to == to_row
    order_row = jnp.sum((same & (iota(square, 0) < iota(square, 1))).astype(I32), axis=0, keepdims=True)
    order = jnp.sum((same & (iota(square, 1) < iota(square, 0))).astype(I32), axis=1, keepdims=True)
    place = jnp.where(order < BASE, to * BASE + order, ROWS + order - BASE)
    lanes = (ROWS, 128)
    picked = jnp.sum(jnp.where(place == iota(lanes, 1), iota(lanes, 0), 0), axis=0, keepdims=True)
    pick_ref[...] = jnp.broadcast_to(picked, pick_ref.shape)
    picking = pltpu.make_async_copy(pick_ref, pick_smem, sems.at[0])
    picking.start()
    picking.wait()
    for p in range(BASE):
        pltpu.make_async_copy(
            ssm_ref.at[pick_smem[0, ROWS + p]], block_ref.at[pl.ds(GATH + p * STATE, STATE)], sems.at[2]
        ).start()

    def send(p, carry):
        pltpu.make_async_copy(ssm_ref.at[pick_smem[0, p]], main_ref.at[p], sems.at[1]).start()
        return carry

    lax.fori_loop(0, ROWS, send, 0)
    buf = jnp.zeros((GROUPS * SLOT, CH), F32)
    sec = bdot(onehot(iota((SEC, COEF), 0) == iota((SEC, COEF), 1)), coef_ref[...])
    for tap in range(3):
        dest = jnp.where(order_row < BASE, to_row * SLOT + order_row * 3 + tap, -1)
        buf += bdot(onehot(iota((GROUPS * SLOT, ROWS), 0) == dest), conv_ref[tap])
        dest = jnp.where(order_row < BASE, -1, COEF + (order_row - BASE) * 3 + tap)
        sec += bdot(onehot(iota((SEC, ROWS), 0) == dest), conv_ref[tap])
    buf_ref[...] = buf.astype(BF)
    block_ref[pl.ds(0, SEC), :] = sec.astype(BF)
    block_ref[pl.ds(SEC, DELTA), :] = delta_ref[...]
    match = (slots_ref[...] == me * ROWS + iota((ROWS, GROUPS * ROWS), 0)).astype(I32)
    inv = jnp.sum(match * iota(match.shape, 1), axis=1, keepdims=True)
    rem_ref[...] = jnp.sum(match * remaining_ref[...], axis=1, keepdims=True)
    inv_row = jnp.sum(jnp.where(eye, inv, 0), axis=0, keepdims=True)
    src = inv // ROWS
    src_row = inv_row // ROWS
    rank = jnp.sum(
        ((src == src_row) & (inv_row < inv)).astype(I32), axis=1, keepdims=True
    )
    rank_row = jnp.sum(
        ((src == src_row) & (inv < inv_row)).astype(I32), axis=0, keepdims=True
    )
    turn = lax.rem(x - lax.rem(src_row, NX) + NX, NX)
    where_row = jnp.where(rank_row < BASE, src_row * BASE + rank_row, ROWS + (turn - 1) * BASE + rank_row)
    gather_ref[...] = jnp.broadcast_to(where_row, gather_ref.shape)
    for tap in range(3):
        at = pl.ds(tap * ROWS, ROWS)
        col_ref[at, :] = jnp.where(rank < BASE, src * SLOT + rank * 3 + tap, -1)
        ext_ref[at, :] = jnp.where(
            rank < BASE, -1, src * GATH + COEF + (rank - BASE) * 3 + tap
        )
    target = table_ref[...] // ROWS
    groups = iota((GROUPS, 1), 0)
    for k in range(NX):
        dest = me - x + lax.rem(x + k, NX)
        count = jnp.sum((target == dest).astype(I32), axis=1, keepdims=True)
        holds = (count > BASE) & (lax.rem(groups, NX) == x)
        z = jnp.sum(jnp.where(holds, groups // NX, 0), axis=0, keepdims=True)
        relay_ref[pl.ds(k, 1), :] = jnp.broadcast_to(z, (1, 128))
    pltpu.make_async_copy(
        ssm_ref.at[pl.ds(0, BASE)].reshape(BASE * STATE, CH), block_ref.at[pl.ds(GATH, BASE * STATE)], sems.at[2]
    ).wait()
    pltpu.make_async_copy(ssm_ref, main_ref, sems.at[1]).wait()
    proj_out_ref[...] = proj_ref[...].T


def plan(me, slots, remaining, table, conv, coef, delta, proj, ssm):
    shape = jax.ShapeDtypeStruct
    return pl.pallas_call(
        plan_kernel,
        name="plan",
        out_shape=(
            shape((8, ROWS), I32),
            shape((NX, 128), I32),
            shape((ROWS, 1), I32),
            shape((3 * ROWS, 1), I32),
            shape((3 * ROWS, 1), I32),
            shape((GROUPS * SLOT, CH), BF),
            shape((GATH + BASE * STATE, CH), BF),
            shape((ROWS, STATE, CH), BF),
            shape(proj.shape[::-1], BF),
        ),
        in_specs=[SMEM] + [VMEM] * 7 + [ANY],
        out_specs=(VMEM,) * 9,
        scratch_shapes=[
            pltpu.VMEM((8, 128), I32),
            pltpu.SMEM((8, 128), I32),
            pltpu.SemaphoreType.DMA((3,)),
        ],
        compiler_params=pltpu.CompilerParams(vmem_limit_bytes=60 << 20),
    )(me, slots, remaining, table, conv, coef, delta, proj, ssm)


def conv_kernel(
    me_ref, moved_ref, g0, g1, g2, g3, col_ref, ext_ref, rem_ref, inputs_ref, weight_ref, bias_ref, proj_ref,
    act_ref, low_ref, final_ref, proj_out_ref,
):
    x = me_ref[1]
    proj_out_ref[...] = proj_ref[...]
    parts = (g0, g1, g2, g3)
    span = NZ * GATH
    window = bdot(onehot(col_ref[...] == iota((3 * ROWS, GROUPS * SLOT), 1)), moved_ref[...])
    coef = jnp.zeros((LOW, CH), F32)
    for k, part in enumerate(parts):
        at = iota((1, span), 1)
        z, q = at // GATH, at % GATH
        group = z * NX + lax.rem(x - k + NX, NX)
        ext = onehot(ext_ref[...] == group * GATH + q)
        window += bdot(ext, part[...])
        row = jnp.where(q < COEF, group * COEF + q, -1)
        coef += bdot(onehot(iota((LOW, span), 0) == row), part[...])
    coef = coef.astype(BF)
    taps = [window[tap * ROWS : (tap + 1) * ROWS] for tap in range(3)]
    taps += [inputs_ref[t].astype(F32) for t in range(STEPS)]
    weight = weight_ref[...]
    for t in range(STEPS):
        out = bias_ref[...] + sum(taps[t + k] * weight[k : k + 1] for k in range(4))
        act = out / (1.0 + jnp.exp(-out))
        act_ref[t] = act
        low_ref[pl.ds(t * ROWS, ROWS), :] = bdot_t(act.astype(BF), coef).astype(BF)
    rem = rem_ref[...]
    for k in range(3):
        kept = taps[k]
        for t in range(1, STEPS + 1):
            kept = jnp.where(rem >= t, taps[t + k], kept)
        final_ref[k] = kept.astype(BF)


def conv_stage(me, moved, parts, col, ext, rem, inputs, weight, bias, proj):
    shape = jax.ShapeDtypeStruct
    return pl.pallas_call(
        conv_kernel,
        name="conv",
        out_shape=(
            shape((STEPS, ROWS, CH), F32),
            shape((STEPS * ROWS, LOW), BF),
            shape((3, ROWS, CH), BF),
            shape(proj.shape, BF),
        ),
        in_specs=[SMEM] + [VMEM] * 12,
        out_specs=(VMEM,) * 4,
        compiler_params=pltpu.CompilerParams(vmem_limit_bytes=60 << 20),
    )(me, moved, *parts, col, ext, rem, inputs, weight, bias, proj)


def step_kernel(
    me_ref, own_ref, other_ref, g0, g1, g2, g3, bias_ref, act_ref, gate_ref, skip_ref, rem_ref, log_ref,
    dt_ref, dx_ref, sk_ref, sg_ref, bc_ref, rate_ref, low_ref,
):
    x, y, c = me_ref[1], me_ref[2], me_ref[3]
    rate_ref[...] = -jnp.exp(log_ref[...]) * LOG2E
    chunk = STEPS * ROWS // (NY * NC)
    for half, piece in ((c, own_ref), (1 - c, other_ref)):
        for m in range(NY):
            at = half * NY + lax.rem(y + m, NY)
            low_ref[pl.ds(pl.multiple_of(at * chunk, 16), chunk), :] = piece[m]
    span = NZ * GATH
    delta = jnp.zeros((RANK, CH), F32)
    for k, part in enumerate((g0, g1, g2, g3)):
        at = iota((1, span), 1)
        z, q = at // GATH, at % GATH
        group = z * NX + lax.rem(x - k + NX, NX)
        row = jnp.where(q >= SEC, group * DELTA + q - SEC, -1)
        delta += bdot(onehot(iota((RANK, span), 0) == row), part[...])
    delta = delta.astype(BF)
    rem = rem_ref[...]
    for t in range(STEPS):
        low = low_ref[pl.ds(t * ROWS, ROWS), :]
        raw = bdot(low[:, :RANK], delta) + bias_ref[...]
        size = jnp.maximum(raw, 0.0) + jnp.log1p(jnp.exp(-jnp.abs(raw)))
        active = rem > t
        size = jnp.where(active, size, 0.0)
        act = act_ref[t]
        gate = gate_ref[t].astype(F32)
        dt_ref[t] = size
        dx_ref[t] = size * act
        sk_ref[t] = skip_ref[...] * act
        sg_ref[t] = jnp.where(active, gate / (1.0 + jnp.exp(-gate)), 0.0)
        coefs = low[:, RANK:].astype(F32)
        for n in range(2 * STATE):
            bc_ref[t, n] = jnp.broadcast_to(coefs[:, n : n + 1], (ROWS, 128))


def step_stage(me, own, other, parts, bias, act, gate, skip, rem, log):
    shape = jax.ShapeDtypeStruct
    rows = shape((STEPS, ROWS, CH), F32)
    return pl.pallas_call(
        step_kernel,
        name="sizes",
        out_shape=(rows, rows, rows, rows, shape((STEPS, 2 * STATE, ROWS, 128), F32), shape((STATE, CH), F32)),
        in_specs=[SMEM] + [VMEM] * 12,
        out_specs=(VMEM,) * 6,
        scratch_shapes=[pltpu.VMEM((STEPS * ROWS, LOW), BF)],
        compiler_params=pltpu.CompilerParams(vmem_limit_bytes=60 << 20),
    )(me, own, other, *parts, bias, act, gate, skip, rem, log)


BLOCK = 8
HALF = ROWS // 2
BLOCKS = HALF // BLOCK


def scan_kernel(
    start, at_ref, main_ref, e0, e1, e2, e3, _before, dt_ref, dx_ref, sk_ref, sg_ref, bc_ref, rate_ref,
    out_ref, final_ref, held, wide, sems,
):
    b = pl.program_id(0)

    def fetch(block):
        for i in range(BLOCK):
            at = at_ref[0, (start + block) * BLOCK + i]

            @pl.when(at < ROWS)
            def _():
                pltpu.make_async_copy(main_ref.at[at], held.at[block, i], sems.at[block]).start()

            for k, extra in enumerate((e0, e1, e2, e3)):
                row = at - ROWS - k * BASE

                @pl.when((row >= 0) & (row < BASE))
                def _(row=row, extra=extra):
                    pltpu.make_async_copy(extra.at[row], held.at[block, i], sems.at[block]).start()

    @pl.when(b == 0)
    def _():
        for block in range(3):
            fetch(block)

    @pl.when(b + 3 < BLOCKS)
    def _():
        fetch(b + 3)

    pltpu.make_async_copy(main_ref.at[pl.ds(0, BLOCK)], held.at[b], sems.at[b]).wait()
    for i in range(BLOCK):
        for l in range(CH // 128):
            wide[l, pl.ds(i * STATE, STATE), :] = held[b, i, :, pl.ds(l * 128, 128)].astype(F32)

    def lanes(l, carry):
        cols = pl.ds(pl.multiple_of(l * 128, 128), 128)
        dts = [dt_ref[t, :, cols] for t in range(STEPS)]
        dxs = [dx_ref[t, :, cols] for t in range(STEPS)]
        sums = [sk_ref[t, :, cols] for t in range(STEPS)]
        for n in range(STATE):
            here = pl.ds(n, BLOCK, stride=STATE)
            h = wide[l, here, :]
            rate = jnp.broadcast_to(rate_ref[pl.ds(n, 1), cols], (BLOCK, 128))
            for t in range(STEPS):
                h = jnp.exp2(dts[t] * rate) * h + dxs[t] * bc_ref[t, n]
                sums[t] += h * bc_ref[t, STATE + n]
            wide[l, here, :] = h
        for t in range(STEPS):
            out_ref[t, :, cols] = (sums[t] * sg_ref[t, :, cols]).astype(BF)
        return carry

    lax.fori_loop(0, CH // 128, lanes, 0)
    for i in range(BLOCK):
        for l in range(CH // 128):
            final_ref[i, :, pl.ds(l * 128, 128)] = wide[l, pl.ds(i * STATE, STATE), :].astype(BF)


def scan_stage(start, at, main, extras, before, dt, dx, sk, sg, bc, rate):
    shape = jax.ShapeDtypeStruct
    rows = pl.BlockSpec((STEPS, BLOCK, CH), lambda b, at: (0, start + b, 0))
    final = shape((ROWS, STATE, CH), BF)
    held = [] if before is None else [before]
    kernel = functools.partial(scan_kernel, start)
    if before is None:
        kernel = lambda *refs: scan_kernel(start, *refs[:6], None, *refs[6:])
    return pl.pallas_call(
        kernel,
        name="scan",
        out_shape=(shape((STEPS, HALF, CH), BF), final),
        grid_spec=pltpu.PrefetchScalarGridSpec(
            num_scalar_prefetch=1,
            grid=(BLOCKS,),
            in_specs=[ANY] * (5 + len(held))
            + [
                rows,
                rows,
                rows,
                rows,
                pl.BlockSpec((STEPS, 2 * STATE, BLOCK, 128), lambda b, at: (0, 0, start + b, 0)),
                pl.BlockSpec((STATE, CH), lambda b, at: (0, 0)),
            ],
            out_specs=(
                pl.BlockSpec((STEPS, BLOCK, CH), lambda b, at: (0, b, 0)),
                pl.BlockSpec((BLOCK, STATE, CH), lambda b, at: (start + b, 0, 0)),
            ),
            scratch_shapes=[
                pltpu.VMEM((BLOCKS, BLOCK, STATE, CH), BF),
                pltpu.VMEM((CH // 128, BLOCK * STATE, 128), F32),
                pltpu.SemaphoreType.DMA((BLOCKS,)),
            ],
        ),
        input_output_aliases={6: 1} if held else {},
        cost_estimate=pl.CostEstimate(flops=1 << 33, bytes_accessed=16 << 20, transcendentals=3 << 20),
        compiler_params=pltpu.CompilerParams(vmem_limit_bytes=60 << 20),
    )(at, main, *extras, *held, dt, dx, sk, sg, bc, rate)


def after_kernel(value_ref, other_ref, out_ref):
    pass


def after(value, other):
    return pl.pallas_call(
        after_kernel,
        name="after",
        out_shape=jax.ShapeDtypeStruct(value.shape, value.dtype),
        in_specs=[ANY, ANY],
        out_specs=ANY,
        input_output_aliases={0: 0},
    )(value, other)


VISIT = STEPS * HALF
PIECE = CH // (NZ * NX) * NX


def theirs_kernel(me_ref, v0, v1, v2, v3, columns_ref, _before, out_ref):
    c = me_ref[3]
    for b in range(NY):
        part = columns_ref[b * NC + 1 - c]
        for k, visit in enumerate((v0, v1, v2, v3)):
            out_ref[k, :, pl.ds(b * PIECE, PIECE)] = bdot_t(visit[...], part).astype(BF)


def ours_kernel(me_ref, v0, v1, v2, v3, columns_ref, got_ref, o0, o1, o2, o3):
    y, c = me_ref[2], me_ref[3]
    for s, out in enumerate((o0, o1, o2, o3)):
        b = lax.rem(y + s, NY)
        part = columns_ref[b * NC + c]
        for k, visit in enumerate((v0, v1, v2, v3)):
            got = got_ref[k, :, pl.ds(pl.multiple_of(b * PIECE, 128), PIECE)]
            out[k] = (bdot_t(visit[...], part) + got.astype(F32)).astype(BF)


def mix(me, half, columns, before):
    shape = jax.ShapeDtypeStruct
    params = pltpu.CompilerParams(vmem_limit_bytes=60 << 20)
    rows = half.reshape(VISIT, CH)
    visits = [rows] + [shift(rows, "x", NX, k) for k in range(1, NX)]
    given = pl.pallas_call(
        theirs_kernel,
        name="theirs",
        out_shape=shape((NX, VISIT, NY * PIECE), BF),
        in_specs=[SMEM] + [VMEM] * 5 + [ANY],
        out_specs=VMEM,
        compiler_params=params,
    )(me, *visits, columns, before)
    got = shift(given, "c", NC, 1)
    parts = pl.pallas_call(
        ours_kernel,
        name="ours",
        out_shape=(shape((NX, VISIT, PIECE), BF),) * NY,
        in_specs=[SMEM] + [VMEM] * 6,
        out_specs=(VMEM,) * NY,
        compiler_params=params,
    )(me, *visits, columns, got)
    total = parts[0].astype(F32)
    for s in range(1, NY):
        total += shift(parts[s], "y", NY, s).astype(F32)
    total = total.astype(BF)
    return [total[0]] + [shift(total[k], "x", NX, NX - k) for k in range(1, NX)], given


def join_kernel(me_ref, *refs):
    x, out_ref = me_ref[1], refs[-1]
    for h in range(2):
        for k in range(NX):
            at = pl.multiple_of(lax.rem(x + k, NX) * PIECE, 128)
            for t in range(STEPS):
                out_ref[t, pl.ds(h * HALF, HALF), pl.ds(at, PIECE)] = refs[h * NX + k][pl.ds(t * HALF, HALF), :]


def join(me, pieces):
    return pl.pallas_call(
        join_kernel,
        name="join",
        out_shape=jax.ShapeDtypeStruct((STEPS, ROWS, NX * PIECE), BF),
        in_specs=[SMEM] + [VMEM] * len(pieces),
        out_specs=VMEM,
        compiler_params=pltpu.CompilerParams(vmem_limit_bytes=60 << 20),
    )(me, *pieces)


def shift(value, axis, size, k):
    return lax.ppermute(value, axis, [(i, (i + k) % size) for i in range(size)])


def reduce_mp(low, y, c):
    chunk = STEPS * ROWS // (NY * NC)
    halves = low.reshape(NC, NY * chunk, LOW)
    got = shift(lax.dynamic_index_in_dim(halves, 1 - c, 0, False), "c", NC, 1)
    mine = lax.dynamic_index_in_dim(halves, c, 0, False).astype(F32) + got.astype(F32)
    quarters = mine.reshape(NY, chunk, LOW)
    rounded = quarters.astype(BF)
    total = lax.dynamic_index_in_dim(quarters, y, 0, False)
    came = [
        shift(lax.dynamic_index_in_dim(rounded, lax.rem(y + k, NY), 0, False), "y", NY, k)
        for k in range(1, NY)
    ]
    total = (total + came[0].astype(F32) + came[1].astype(F32) + came[2].astype(F32)).astype(BF)
    own = jnp.stack([total] + [shift(total, "y", NY, NY - m) for m in range(1, NY)])
    return own, shift(own, "c", NC, 1)


def per_device(
    input_steps, gate_steps, conv_state, ssm_state, new_slot, remaining, conv_weight, conv_bias,
    coef_proj, delta_proj, delta_bias, decay_log, skip_gain, out_proj,
):
    z, x, y, c = (lax.axis_index(name) for name in ("z", "x", "y", "c"))
    group = z * NX + x
    me = jnp.stack([group, x, y, c]).astype(I32)
    at, relay, rem, col, ext, buf, block, main, proj = plan(
        me,
        new_slot.reshape(1, -1),
        remaining.reshape(1, -1),
        new_slot.reshape(GROUPS, ROWS),
        conv_state.transpose(1, 0, 2),
        coef_proj.T,
        delta_proj,
        out_proj,
        ssm_state,
    )
    gathered = lax.all_gather(block, "z", axis=0)
    moved = lax.all_to_all(
        buf.reshape(GROUPS, SLOT, CH), ("z", "x"), split_axis=0, concat_axis=0, tiled=True
    ).reshape(GROUPS * SLOT, CH)
    ssm_main = lax.all_to_all(
        after(main, gathered), ("z", "x"), split_axis=0, concat_axis=0, tiled=True
    )

    def turned(value):
        return [value] + [shift(value, "x", NX, k) for k in range(1, NX)]

    parts = turned(gathered[:, :GATH].reshape(NZ * GATH, CH))
    extras = [
        lax.dynamic_slice(gathered, (relay[k, 0], GATH, 0), (1, BASE * STATE, CH)) for k in range(NX)
    ]
    extras = [extras[0]] + [shift(extras[k], "x", NX, k) for k in range(1, NX)]
    extras = [e.reshape(BASE, STATE, CH) for e in extras]
    act, low, conv_final, proj = conv_stage(
        me, moved, parts, col, ext, rem, input_steps, conv_weight, conv_bias.reshape(1, -1), proj
    )
    columns = lax.all_gather(proj, "z", axis=0)
    own, other = reduce_mp(low, y, c)
    sized = step_stage(
        me, own, other, parts, delta_bias.reshape(1, -1), act, gate_steps, skip_gain.reshape(1, -1), rem, decay_log
    )
    early, ssm_final = scan_stage(0, at, ssm_main, extras, None, *sized)
    late, ssm_final = scan_stage(BLOCKS, at, ssm_main, extras, ssm_final, *sized)
    early, done = mix(me, early, columns, rem)
    late, _ = mix(me, late, columns, done)
    mixed = join(me, early + late)
    return mixed, conv_final.transpose(1, 0, 2), ssm_final


def solution(mesh):
    fine = Mesh(mesh.devices.reshape(NZ, NX, NY, NC), ("z", "x", "y", "c"))
    dp, mp = ("z", "x"), ("y", "c")
    return jax.shard_map(
        per_device,
        mesh=fine,
        in_specs=(
            P(None, dp, mp),
            P(None, dp, mp),
            P(dp, None, mp),
            P(dp, None, mp),
            P(),
            P(),
            P(None, mp),
            P(mp),
            P(mp, dp),
            P(dp, mp),
            P(mp),
            P(None, mp),
            P(mp),
            P(mp, dp),
        ),
        out_specs=(P(None, dp, mp), P(dp, None, mp), P(dp, None, mp)),
        check_vma=False,
    )
```

```python
import functools

import jax
import jax.numpy as jnp
from jax import lax
from jax.experimental import pallas as pl
from jax.experimental.pallas import tpu as pltpu
from jax.sharding import Mesh
from jax.sharding import PartitionSpec as P

BF = jnp.bfloat16
F32 = jnp.float32
I32 = jnp.int32
NZ, NX, NY, NC = 8, 4, 4, 2
GROUPS = NZ * NX
ROWS = 96
CH = 1024
STATE = 16
RANK = 512
STEPS = 4
LOW = RANK + 2 * STATE
COEF = LOW // GROUPS
DELTA = RANK // GROUPS
BASE = ROWS // GROUPS
SLOT = 24
GATH = 40
LOG2E = 1.4426950408889634
VMEM = pl.BlockSpec(memory_space=pltpu.VMEM)
SMEM = pl.BlockSpec(memory_space=pltpu.SMEM)
ANY = pl.BlockSpec(memory_space=pl.ANY)


def iota(shape, dim):
    return lax.broadcasted_iota(I32, shape, dim)


def bdot(a, b):
    return jnp.dot(a, b, preferred_element_type=F32)


def bdot_t(a, b):
    return lax.dot_general(a, b, (((1,), (1,)), ((), ())), preferred_element_type=F32)


def onehot(cond):
    return cond.astype(F32).astype(BF)


def plan_kernel(
    me_ref, slots_ref, remaining_ref, table_ref, conv_ref, ssm_ref,
    gather_ref, relay_ref, rem_ref, col_ref, buf_ref, extra_ref, main_ref,
    pick_ref, pick_smem, sems,
):
    me = me_ref[0]
    x = me_ref[1]
    z = me // NX
    square = (ROWS, ROWS)
    eye = iota(square, 0) == iota(square, 1)
    to_row = table_ref[pl.ds(me, 1), :] // ROWS
    to = jnp.sum(jnp.where(eye, to_row, 0), axis=1, keepdims=True)
    same = to == to_row
    order_row = jnp.sum((same & (iota(square, 0) < iota(square, 1))).astype(I32), axis=0, keepdims=True)
    order = jnp.sum((same & (iota(square, 1) < iota(square, 0))).astype(I32), axis=1, keepdims=True)
    place = jnp.where(order < BASE, to * BASE + order, ROWS + order - BASE)
    lanes = (ROWS, 128)
    picked = jnp.sum(jnp.where(place == iota(lanes, 1), iota(lanes, 0), 0), axis=0, keepdims=True)
    pick_ref[...] = jnp.broadcast_to(picked, pick_ref.shape)
    picking = pltpu.make_async_copy(pick_ref, pick_smem, sems.at[0])
    picking.start()
    picking.wait()
    for p in range(BASE):
        pltpu.make_async_copy(
            ssm_ref.at[pick_smem[0, ROWS + p]], extra_ref.at[pl.ds(p * STATE, STATE)], sems.at[2]
        ).start()

    def send(p, carry):
        pltpu.make_async_copy(ssm_ref.at[pick_smem[0, p]], main_ref.at[p], sems.at[1]).start()
        return carry

    lax.fori_loop(0, ROWS, send, 0)
    buf = jnp.zeros((GROUPS * SLOT, CH), F32)
    for tap in range(3):
        dest = to_row * SLOT + order_row * 3 + tap
        buf += bdot(onehot(iota((GROUPS * SLOT, ROWS), 0) == dest), conv_ref[tap])
    buf_ref[...] = buf.astype(BF)
    match = (slots_ref[...] == me * ROWS + iota((ROWS, GROUPS * ROWS), 0)).astype(I32)
    inv = jnp.sum(match * iota(match.shape, 1), axis=1, keepdims=True)
    rem_ref[...] = jnp.sum(match * remaining_ref[...], axis=1, keepdims=True)
    inv_row = jnp.sum(jnp.where(eye, inv, 0), axis=0, keepdims=True)
    src = inv // ROWS
    src_row = inv_row // ROWS
    rank = jnp.sum(
        ((src == src_row) & (inv_row < inv)).astype(I32), axis=1, keepdims=True
    )
    rank_row = jnp.sum(
        ((src == src_row) & (inv < inv_row)).astype(I32), axis=0, keepdims=True
    )
    turn = lax.rem(z - src_row // NX + NZ, NZ)
    where_row = jnp.where(rank_row < BASE, src_row * BASE + rank_row, ROWS + (turn - 1) * BASE + rank_row)
    gather_ref[...] = jnp.broadcast_to(where_row, gather_ref.shape)
    for tap in range(3):
        col_ref[pl.ds(tap * ROWS, ROWS), :] = src * SLOT + rank * 3 + tap
    target = table_ref[...] // ROWS
    groups = iota((GROUPS, 1), 0)
    for k in range(NZ):
        dest = lax.rem(z + k, NZ) * NX + x
        count = jnp.sum((target == dest).astype(I32), axis=1, keepdims=True)
        holds = (count > BASE) & (groups // NX == z)
        spot = jnp.sum(jnp.where(holds, lax.rem(x - lax.rem(groups, NX) + NX, NX), 0), axis=0, keepdims=True)
        relay_ref[pl.ds(k, 1), :] = jnp.broadcast_to(spot, (1, 128))
    pltpu.make_async_copy(
        ssm_ref.at[pl.ds(0, BASE)].reshape(BASE * STATE, CH), extra_ref, sems.at[2]
    ).wait()
    pltpu.make_async_copy(ssm_ref, main_ref, sems.at[1]).wait()


def plan(me, slots, remaining, table, conv, ssm):
    shape = jax.ShapeDtypeStruct
    return pl.pallas_call(
        plan_kernel,
        name="plan",
        out_shape=(
            shape((8, ROWS), I32),
            shape((NZ, 128), I32),
            shape((ROWS, 1), I32),
            shape((3 * ROWS, 1), I32),
            shape((GROUPS * SLOT, CH), BF),
            shape((BASE * STATE, CH), BF),
            shape((ROWS, STATE, CH), BF),
        ),
        in_specs=[SMEM] + [VMEM] * 4 + [ANY],
        out_specs=(VMEM,) * 7,
        scratch_shapes=[
            pltpu.VMEM((8, 128), I32),
            pltpu.SMEM((8, 128), I32),
            pltpu.SemaphoreType.DMA((3,)),
        ],
        cost_estimate=pl.CostEstimate(flops=1 << 33, bytes_accessed=12 << 20, transcendentals=0),
        compiler_params=pltpu.CompilerParams(vmem_limit_bytes=60 << 20),
    )(me, slots, remaining, table, conv, ssm)


def conv_kernel(
    me_ref, moved_ref, g0, g1, g2, g3, col_ref, rem_ref, inputs_ref, weight_ref, bias_ref,
    act_ref, low_ref, final_ref,
):
    x = me_ref[1]
    parts = (g0, g1, g2, g3)
    span = NZ * GATH
    window = bdot(onehot(col_ref[...] == iota((3 * ROWS, GROUPS * SLOT), 1)), moved_ref[...])
    coef = jnp.zeros((LOW, CH), F32)
    for k, part in enumerate(parts):
        at = iota((1, span), 1)
        z, q = at // GATH, at % GATH
        group = z * NX + lax.rem(x - k + NX, NX)
        row = jnp.where((q >= DELTA) & (q < DELTA + COEF), group * COEF + q - DELTA, -1)
        coef += bdot(onehot(iota((LOW, span), 0) == row), part[...])
    coef = coef.astype(BF)
    taps = [window[tap * ROWS : (tap + 1) * ROWS] for tap in range(3)]
    taps += [inputs_ref[t].astype(F32) for t in range(STEPS)]
    weight = weight_ref[...]
    for t in range(STEPS):
        out = bias_ref[...] + sum(taps[t + k] * weight[k : k + 1] for k in range(4))
        act = out / (1.0 + jnp.exp(-out))
        act_ref[t] = act
        low_ref[pl.ds(t * ROWS, ROWS), :] = bdot_t(act.astype(BF), coef).astype(BF)
    rem = rem_ref[...]
    for k in range(3):
        kept = taps[k]
        for t in range(1, STEPS + 1):
            kept = jnp.where(rem >= t, taps[t + k], kept)
        final_ref[k] = kept.astype(BF)


def conv_stage(me, moved, parts, col, rem, inputs, weight, bias):
    shape = jax.ShapeDtypeStruct
    return pl.pallas_call(
        conv_kernel,
        name="conv",
        out_shape=(
            shape((STEPS, ROWS, CH), F32),
            shape((STEPS * ROWS, LOW), BF),
            shape((3, ROWS, CH), BF),
        ),
        in_specs=[SMEM] + [VMEM] * 10,
        out_specs=(VMEM,) * 3,
        compiler_params=pltpu.CompilerParams(vmem_limit_bytes=60 << 20),
    )(me, moved, *parts, col, rem, inputs, weight, bias)


def step_kernel(
    me_ref, own_ref, other_ref, g0, g1, g2, g3, bias_ref, act_ref, gate_ref, skip_ref, rem_ref, log_ref,
    dt_ref, dx_ref, sk_ref, sg_ref, bc_ref, rate_ref, low_ref,
):
    x, y, c = me_ref[1], me_ref[2], me_ref[3]
    rate_ref[...] = -jnp.exp(log_ref[...]) * LOG2E
    chunk = STEPS * ROWS // (NY * NC)
    for half, piece in ((c, own_ref), (1 - c, other_ref)):
        for m in range(NY):
            at = half * NY + lax.rem(y + m, NY)
            low_ref[pl.ds(pl.multiple_of(at * chunk, 16), chunk), :] = piece[m]
    span = NZ * GATH
    delta = jnp.zeros((RANK, CH), F32)
    for k, part in enumerate((g0, g1, g2, g3)):
        at = iota((1, span), 1)
        z, q = at // GATH, at % GATH
        group = z * NX + lax.rem(x - k + NX, NX)
        row = jnp.where(q < DELTA, group * DELTA + q, -1)
        delta += bdot(onehot(iota((RANK, span), 0) == row), part[...])
    delta = delta.astype(BF)
    rem = rem_ref[...]
    for t in range(STEPS):
        low = low_ref[pl.ds(t * ROWS, ROWS), :]
        raw = bdot(low[:, :RANK], delta) + bias_ref[...]
        size = jnp.maximum(raw, 0.0) + jnp.log1p(jnp.exp(-jnp.abs(raw)))
        active = rem > t
        size = jnp.where(active, size, 0.0)
        act = act_ref[t]
        gate = gate_ref[t].astype(F32)
        dt_ref[t] = size
        dx_ref[t] = size * act
        sk_ref[t] = skip_ref[...] * act
        sg_ref[t] = jnp.where(active, gate / (1.0 + jnp.exp(-gate)), 0.0)
        coefs = low[:, RANK:].astype(F32)
        for n in range(2 * STATE):
            bc_ref[t, n] = jnp.broadcast_to(coefs[:, n : n + 1], (ROWS, 128))


def step_stage(me, own, other, parts, bias, act, gate, skip, rem, log):
    shape = jax.ShapeDtypeStruct
    rows = shape((STEPS, ROWS, CH), F32)
    return pl.pallas_call(
        step_kernel,
        name="sizes",
        out_shape=(rows, rows, rows, rows, shape((STEPS, 2 * STATE, ROWS, 128), F32), shape((STATE, CH), F32)),
        in_specs=[SMEM] + [VMEM] * 12,
        out_specs=(VMEM,) * 6,
        scratch_shapes=[pltpu.VMEM((STEPS * ROWS, LOW), BF)],
        compiler_params=pltpu.CompilerParams(vmem_limit_bytes=60 << 20),
    )(me, own, other, *parts, bias, act, gate, skip, rem, log)


BLOCK = 8
BLOCKS = ROWS // BLOCK


def scan_kernel(
    at_ref, main_ref, extra_ref, dt_ref, dx_ref, sk_ref, sg_ref, bc_ref, rate_ref,
    out_ref, final_ref, held, wide, sems,
):
    b = pl.program_id(0)

    def fetch(block):
        for i in range(BLOCK):
            at = at_ref[0, block * BLOCK + i]

            @pl.when(at < ROWS)
            def _():
                pltpu.make_async_copy(main_ref.at[at], held.at[block, i], sems.at[block]).start()

            @pl.when(at >= ROWS)
            def _():
                rows = pl.ds(pl.multiple_of((at - ROWS) * STATE, STATE), STATE)
                pltpu.make_async_copy(extra_ref.at[rows], held.at[block, i], sems.at[block]).start()

    @pl.when(b == 0)
    def _():
        for block in range(3):
            fetch(block)

    @pl.when(b + 3 < BLOCKS)
    def _():
        fetch(b + 3)

    pltpu.make_async_copy(main_ref.at[pl.ds(0, BLOCK)], held.at[b], sems.at[b]).wait()
    for i in range(BLOCK):
        for l in range(CH // 128):
            wide[l, pl.ds(i * STATE, STATE), :] = held[b, i, :, pl.ds(l * 128, 128)].astype(F32)

    def lanes(l, carry):
        cols = pl.ds(pl.multiple_of(l * 128, 128), 128)
        dts = [dt_ref[t, :, cols] for t in range(STEPS)]
        dxs = [dx_ref[t, :, cols] for t in range(STEPS)]
        sums = [sk_ref[t, :, cols] for t in range(STEPS)]
        for n in range(STATE):
            here = pl.ds(n, BLOCK, stride=STATE)
            h = wide[l, here, :]
            rate = jnp.broadcast_to(rate_ref[pl.ds(n, 1), cols], (BLOCK, 128))
            for t in range(STEPS):
                h = jnp.exp2(dts[t] * rate) * h + dxs[t] * bc_ref[t, n]
                sums[t] += h * bc_ref[t, STATE + n]
            wide[l, here, :] = h
        for t in range(STEPS):
            out_ref[t, :, cols] = (sums[t] * sg_ref[t, :, cols]).astype(BF)
        return carry

    lax.fori_loop(0, CH // 128, lanes, 0)
    for i in range(BLOCK):
        for l in range(CH // 128):
            final_ref[i, :, pl.ds(l * 128, 128)] = wide[l, pl.ds(i * STATE, STATE), :].astype(BF)


def scan_stage(at, main, extra, dt, dx, sk, sg, bc, rate):
    shape = jax.ShapeDtypeStruct
    rows = pl.BlockSpec((STEPS, BLOCK, CH), lambda b, at: (0, b, 0))
    return pl.pallas_call(
        scan_kernel,
        name="scan",
        out_shape=(shape((STEPS, ROWS, CH), BF), shape((ROWS, STATE, CH), BF)),
        grid_spec=pltpu.PrefetchScalarGridSpec(
            num_scalar_prefetch=1,
            grid=(BLOCKS,),
            in_specs=[
                ANY,
                ANY,
                rows,
                rows,
                rows,
                rows,
                pl.BlockSpec((STEPS, 2 * STATE, BLOCK, 128), lambda b, at: (0, 0, b, 0)),
                pl.BlockSpec((STATE, CH), lambda b, at: (0, 0)),
            ],
            out_specs=(rows, pl.BlockSpec((BLOCK, STATE, CH), lambda b, at: (b, 0, 0))),
            scratch_shapes=[
                pltpu.VMEM((BLOCKS, BLOCK, STATE, CH), BF),
                pltpu.VMEM((CH // 128, BLOCK * STATE, 128), F32),
                pltpu.SemaphoreType.DMA((BLOCKS,)),
            ],
        ),
        compiler_params=pltpu.CompilerParams(vmem_limit_bytes=60 << 20),
    )(at, main, extra, dt, dx, sk, sg, bc, rate)


def after_kernel(*refs):
    pass


def after(value, *others):
    return pl.pallas_call(
        after_kernel,
        name="after",
        out_shape=jax.ShapeDtypeStruct(value.shape, value.dtype),
        in_specs=[ANY] * (1 + len(others)),
        out_specs=ANY,
        input_output_aliases={0: 0},
    )(value, *others)


def theirs_kernel(me_ref, rows_ref, proj_ref, out_ref):
    out_ref[0] = bdot(rows_ref[...], proj_ref[...]).astype(BF)


def ours_kernel(me_ref, rows_ref, proj_ref, got_ref, out_ref):
    out_ref[0] = (bdot(rows_ref[...], proj_ref[...]) + got_ref[0].astype(F32)).astype(BF)


def mix(me, rows, proj):
    shape = jax.ShapeDtypeStruct
    count, width = rows.shape[0], proj.shape[1] // (NY * NC)
    params = pltpu.CompilerParams(vmem_limit_bytes=60 << 20)
    whole = pl.BlockSpec((count, CH), lambda i, me: (0, 0))
    sums = shape((NY, count, width), BF)

    def block(index):
        return pl.BlockSpec((1, count, width), lambda i, me: (index(i, me), 0, 0))

    def columns(index):
        return pl.BlockSpec((CH, width), lambda i, me: (0, index(i, me)))

    given = pl.pallas_call(
        theirs_kernel,
        name="theirs",
        out_shape=sums,
        grid_spec=pltpu.PrefetchScalarGridSpec(
            num_scalar_prefetch=1,
            grid=(NY,),
            in_specs=[whole, columns(lambda i, me: i * NC + 1 - me[3])],
            out_specs=block(lambda i, me: i),
        ),
        compiler_params=params,
    )(me, rows, proj)
    got = shift(given, "c", NC, 1)
    parts = pl.pallas_call(
        ours_kernel,
        name="ours",
        out_shape=sums,
        grid_spec=pltpu.PrefetchScalarGridSpec(
            num_scalar_prefetch=1,
            grid=(NY,),
            in_specs=[
                whole,
                columns(lambda i, me: lax.rem(me[2] + i, NY) * NC + me[3]),
                block(lambda i, me: lax.rem(me[2] + i, NY)),
            ],
            out_specs=block(lambda i, me: i),
        ),
        compiler_params=params,
    )(me, rows, proj, got)
    total = parts[0].astype(F32)
    for s in range(1, NY):
        total += shift(parts[s], "y", NY, s).astype(F32)
    return total.astype(BF)


def shift(value, axis, size, k):
    return lax.ppermute(value, axis, [(i, (i + k) % size) for i in range(size)])


def reduce_mp(low, y, c):
    chunk = STEPS * ROWS // (NY * NC)
    halves = low.reshape(NC, NY * chunk, LOW)
    got = shift(lax.dynamic_index_in_dim(halves, 1 - c, 0, False), "c", NC, 1)
    mine = lax.dynamic_index_in_dim(halves, c, 0, False).astype(F32) + got.astype(F32)
    quarters = mine.reshape(NY, chunk, LOW)
    rounded = quarters.astype(BF)
    total = lax.dynamic_index_in_dim(quarters, y, 0, False)
    came = [
        shift(lax.dynamic_index_in_dim(rounded, lax.rem(y + k, NY), 0, False), "y", NY, k)
        for k in range(1, NY)
    ]
    total = (total + came[0].astype(F32) + came[1].astype(F32) + came[2].astype(F32)).astype(BF)
    own = jnp.stack([total] + [shift(total, "y", NY, NY - m) for m in range(1, NY)])
    return own, shift(own, "c", NC, 1)


def per_device(
    input_steps, gate_steps, conv_state, ssm_state, new_slot, remaining, conv_weight, conv_bias,
    coef_proj, delta_proj, delta_bias, decay_log, skip_gain, out_proj,
):
    z, x, y, c = (lax.axis_index(name) for name in ("z", "x", "y", "c"))
    group = z * NX + x
    me = jnp.stack([group, x, y, c]).astype(I32)
    proj = lax.all_gather(out_proj, ("z", "x"), axis=1, tiled=True)

    def exchange(value, axes):
        return lax.all_to_all(value, axes, split_axis=0, concat_axis=0, tiled=True)

    def turned(value):
        return [value] + [shift(value, "x", NX, k) for k in range(1, NX)]

    first = jnp.concatenate([delta_proj, coef_proj.T, jnp.zeros((GATH - COEF - DELTA, CH), BF)], axis=0)
    gathered = exchange(jnp.broadcast_to(first[None], (NZ, GATH, CH)), "z")
    parts = turned(gathered.reshape(NZ * GATH, CH))
    at, relay, rem, col, buf, extra, main = plan(
        me,
        new_slot.reshape(1, -1),
        remaining.reshape(1, -1),
        new_slot.reshape(GROUPS, ROWS),
        conv_state.transpose(1, 0, 2),
        ssm_state,
    )
    moved = exchange(after(buf, gathered).reshape(GROUPS, SLOT, CH), ("z", "x")).reshape(GROUPS * SLOT, CH)
    ssm_main = exchange(after(main, moved, *parts[1:]), ("z", "x"))
    beside = jnp.stack(turned(extra))
    extras = [lax.dynamic_index_in_dim(beside, relay[k, 0], 0, False) for k in range(NZ)]
    extras = [extras[0]] + [shift(extras[k], "z", NZ, k) for k in range(1, NZ)]
    act, low, conv_final = conv_stage(
        me, moved, parts, col, rem, input_steps, conv_weight, conv_bias.reshape(1, -1)
    )
    own, other = reduce_mp(low, y, c)
    sized = step_stage(
        me, own, other, parts, delta_bias.reshape(1, -1), act, gate_steps, skip_gain.reshape(1, -1), rem, decay_log
    )
    stepped, ssm_final = scan_stage(at, ssm_main, jnp.concatenate(extras, axis=0), *sized)
    mixed = mix(me, stepped.reshape(STEPS * ROWS, CH), proj)
    return mixed.reshape(STEPS, ROWS, -1), conv_final.transpose(1, 0, 2), ssm_final


def solution(mesh):
    fine = Mesh(mesh.devices.reshape(NZ, NX, NY, NC), ("z", "x", "y", "c"))
    dp, mp = ("z", "x"), ("y", "c")
    return jax.shard_map(
        per_device,
        mesh=fine,
        in_specs=(
            P(None, dp, mp),
            P(None, dp, mp),
            P(dp, None, mp),
            P(dp, None, mp),
            P(),
            P(),
            P(None, mp),
            P(mp),
            P(mp, dp),
            P(dp, mp),
            P(mp),
            P(None, mp),
            P(mp),
            P(mp, dp),
        ),
        out_specs=(P(None, dp, mp), P(dp, None, mp), P(dp, None, mp)),
        check_vma=False,
    )
```

```python
import functools

import jax
import jax.numpy as jnp
from jax import lax
from jax.experimental import pallas as pl
from jax.experimental.pallas import tpu as pltpu
from jax.sharding import Mesh
from jax.sharding import PartitionSpec as P

BF = jnp.bfloat16
F32 = jnp.float32
I32 = jnp.int32
NZ, NX, NY, NC = 8, 4, 4, 2
GROUPS = NZ * NX
ROWS = 96
CH = 1024
STATE = 16
RANK = 512
STEPS = 4
LOW = RANK + 2 * STATE
COEF = LOW // GROUPS
DELTA = RANK // GROUPS
BASE = ROWS // GROUPS
SLOT = 16
SEC = 32
GATH = SEC + DELTA
LOG2E = 1.4426950408889634
VMEM = pl.BlockSpec(memory_space=pltpu.VMEM)
SMEM = pl.BlockSpec(memory_space=pltpu.SMEM)
ANY = pl.BlockSpec(memory_space=pl.ANY)


def iota(shape, dim):
    return lax.broadcasted_iota(I32, shape, dim)


def bdot(a, b):
    return jnp.dot(a, b, preferred_element_type=F32)


def bdot_t(a, b):
    return lax.dot_general(a, b, (((1,), (1,)), ((), ())), preferred_element_type=F32)


def onehot(cond):
    return cond.astype(F32).astype(BF)


def plan_kernel(
    me_ref, slots_ref, remaining_ref, table_ref, conv_ref, coef_ref, delta_ref, proj_ref, ssm_ref,
    gather_ref, relay_ref, rem_ref, col_ref, ext_ref, buf_ref, block_ref, main_ref, proj_out_ref,
    pick_ref, pick_smem, sems,
):
    me = me_ref[0]
    x = me_ref[1]
    square = (ROWS, ROWS)
    eye = iota(square, 0) == iota(square, 1)
    to_row = table_ref[pl.ds(me, 1), :] // ROWS
    to = jnp.sum(jnp.where(eye, to_row, 0), axis=1, keepdims=True)
    same = to == to_row
    order_row = jnp.sum((same & (iota(square, 0) < iota(square, 1))).astype(I32), axis=0, keepdims=True)
    order = jnp.sum((same & (iota(square, 1) < iota(square, 0))).astype(I32), axis=1, keepdims=True)
    place = jnp.where(order < BASE, to * BASE + order, ROWS + order - BASE)
    lanes = (ROWS, 128)
    picked = jnp.sum(jnp.where(place == iota(lanes, 1), iota(lanes, 0), 0), axis=0, keepdims=True)
    pick_ref[...] = jnp.broadcast_to(picked, pick_ref.shape)
    picking = pltpu.make_async_copy(pick_ref, pick_smem, sems.at[0])
    picking.start()
    picking.wait()
    for p in range(BASE):
        pltpu.make_async_copy(
            ssm_ref.at[pick_smem[0, ROWS + p]], block_ref.at[pl.ds(GATH + p * STATE, STATE)], sems.at[2]
        ).start()

    def send(p, carry):
        pltpu.make_async_copy(ssm_ref.at[pick_smem[0, p]], main_ref.at[p], sems.at[1]).start()
        return carry

    lax.fori_loop(0, ROWS, send, 0)
    buf = jnp.zeros((GROUPS * SLOT, CH), F32)
    sec = bdot(onehot(iota((SEC, COEF), 0) == iota((SEC, COEF), 1)), coef_ref[...])
    for tap in range(3):
        dest = jnp.where(order_row < BASE, to_row * SLOT + order_row * 3 + tap, -1)
        buf += bdot(onehot(iota((GROUPS * SLOT, ROWS), 0) == dest), conv_ref[tap])
        dest = jnp.where(order_row < BASE, -1, COEF + (order_row - BASE) * 3 + tap)
        sec += bdot(onehot(iota((SEC, ROWS), 0) == dest), conv_ref[tap])
    buf_ref[...] = buf.astype(BF)
    block_ref[pl.ds(0, SEC), :] = sec.astype(BF)
    block_ref[pl.ds(SEC, DELTA), :] = delta_ref[...]
    match = (slots_ref[...] == me * ROWS + iota((ROWS, GROUPS * ROWS), 0)).astype(I32)
    inv = jnp.sum(match * iota(match.shape, 1), axis=1, keepdims=True)
    rem_ref[...] = jnp.sum(match * remaining_ref[...], axis=1, keepdims=True)
    inv_row = jnp.sum(jnp.where(eye, inv, 0), axis=0, keepdims=True)
    src = inv // ROWS
    src_row = inv_row // ROWS
    rank = jnp.sum(
        ((src == src_row) & (inv_row < inv)).astype(I32), axis=1, keepdims=True
    )
    rank_row = jnp.sum(
        ((src == src_row) & (inv < inv_row)).astype(I32), axis=0, keepdims=True
    )
    turn = lax.rem(x - lax.rem(src_row, NX) + NX, NX)
    where_row = jnp.where(rank_row < BASE, src_row * BASE + rank_row, ROWS + (turn - 1) * BASE + rank_row)
    gather_ref[...] = jnp.broadcast_to(where_row, gather_ref.shape)
    for tap in range(3):
        at = pl.ds(tap * ROWS, ROWS)
        col_ref[at, :] = jnp.where(rank < BASE, src * SLOT + rank * 3 + tap, -1)
        ext_ref[at, :] = jnp.where(
            rank < BASE, -1, src * SEC + COEF + (rank - BASE) * 3 + tap
        )
    target = table_ref[...] // ROWS
    groups = iota((GROUPS, 1), 0)
    for k in range(NX):
        dest = me - x + lax.rem(x + k, NX)
        count = jnp.sum((target == dest).astype(I32), axis=1, keepdims=True)
        holds = (count > BASE) & (lax.rem(groups, NX) == x)
        z = jnp.sum(jnp.where(holds, groups // NX, 0), axis=0, keepdims=True)
        relay_ref[pl.ds(k, 1), :] = jnp.broadcast_to(z, (1, 128))
    pltpu.make_async_copy(
        ssm_ref.at[pl.ds(0, BASE)].reshape(BASE * STATE, CH), block_ref.at[pl.ds(GATH, BASE * STATE)], sems.at[2]
    ).wait()
    pltpu.make_async_copy(ssm_ref, main_ref, sems.at[1]).wait()
    proj_out_ref[...] = proj_ref[...].T


def plan(me, slots, remaining, table, conv, coef, delta, proj, ssm):
    shape = jax.ShapeDtypeStruct
    return pl.pallas_call(
        plan_kernel,
        name="plan",
        out_shape=(
            shape((8, ROWS), I32),
            shape((NX, 128), I32),
            shape((ROWS, 1), I32),
            shape((3 * ROWS, 1), I32),
            shape((3 * ROWS, 1), I32),
            shape((GROUPS * SLOT, CH), BF),
            shape((GATH + BASE * STATE, CH), BF),
            shape((ROWS, STATE, CH), BF),
            shape(proj.shape[::-1], BF),
        ),
        in_specs=[SMEM] + [VMEM] * 7 + [ANY],
        out_specs=(VMEM,) * 9,
        scratch_shapes=[
            pltpu.VMEM((8, 128), I32),
            pltpu.SMEM((8, 128), I32),
            pltpu.SemaphoreType.DMA((3,)),
        ],
        compiler_params=pltpu.CompilerParams(vmem_limit_bytes=60 << 20),
    )(me, slots, remaining, table, conv, coef, delta, proj, ssm)


def conv_kernel(
    me_ref, moved_ref, g0, g1, g2, g3, col_ref, ext_ref, rem_ref, inputs_ref, weight_ref, bias_ref, proj_ref,
    act_ref, low_ref, final_ref, proj_out_ref,
):
    x = me_ref[1]
    proj_out_ref[...] = proj_ref[...]
    parts = (g0, g1, g2, g3)
    span = NZ * SEC
    window = bdot(onehot(col_ref[...] == iota((3 * ROWS, GROUPS * SLOT), 1)), moved_ref[...])
    coef = jnp.zeros((LOW, CH), F32)
    for k, part in enumerate(parts):
        at = iota((1, span), 1)
        z, q = at // SEC, at % SEC
        group = z * NX + lax.rem(x - k + NX, NX)
        ext = onehot(ext_ref[...] == group * SEC + q)
        window += bdot(ext, part[...])
        row = jnp.where(q < COEF, group * COEF + q, -1)
        coef += bdot(onehot(iota((LOW, span), 0) == row), part[...])
    coef = coef.astype(BF)
    taps = [window[tap * ROWS : (tap + 1) * ROWS] for tap in range(3)]
    taps += [inputs_ref[t].astype(F32) for t in range(STEPS)]
    weight = weight_ref[...]
    for t in range(STEPS):
        out = bias_ref[...] + sum(taps[t + k] * weight[k : k + 1] for k in range(4))
        act = out / (1.0 + jnp.exp(-out))
        act_ref[t] = act
        low_ref[pl.ds(t * ROWS, ROWS), :] = bdot_t(act.astype(BF), coef).astype(BF)
    rem = rem_ref[...]
    for k in range(3):
        kept = taps[k]
        for t in range(1, STEPS + 1):
            kept = jnp.where(rem >= t, taps[t + k], kept)
        final_ref[k] = kept.astype(BF)


def conv_stage(me, moved, parts, col, ext, rem, inputs, weight, bias, proj):
    shape = jax.ShapeDtypeStruct
    return pl.pallas_call(
        conv_kernel,
        name="conv",
        out_shape=(
            shape((STEPS, ROWS, CH), F32),
            shape((STEPS * ROWS, LOW), BF),
            shape((3, ROWS, CH), BF),
            shape(proj.shape, BF),
        ),
        in_specs=[SMEM] + [VMEM] * 12,
        out_specs=(VMEM,) * 4,
        compiler_params=pltpu.CompilerParams(vmem_limit_bytes=60 << 20),
    )(me, moved, *parts, col, ext, rem, inputs, weight, bias, proj)


def step_kernel(
    me_ref, own_ref, other_ref, g0, g1, g2, g3, bias_ref, act_ref, gate_ref, skip_ref, rem_ref, log_ref,
    dt_ref, dx_ref, sk_ref, sg_ref, bc_ref, rate_ref, low_ref,
):
    x, y, c = me_ref[1], me_ref[2], me_ref[3]
    rate_ref[...] = -jnp.exp(log_ref[...]) * LOG2E
    chunk = STEPS * ROWS // (NY * NC)
    for half, piece in ((c, own_ref), (1 - c, other_ref)):
        for m in range(NY):
            at = half * NY + lax.rem(y + m, NY)
            low_ref[pl.ds(pl.multiple_of(at * chunk, 16), chunk), :] = piece[m]
    span = NZ * DELTA
    delta = jnp.zeros((RANK, CH), F32)
    for k, part in enumerate((g0, g1, g2, g3)):
        at = iota((1, span), 1)
        z, q = at // DELTA, at % DELTA
        row = (z * NX + lax.rem(x - k + NX, NX)) * DELTA + q
        delta += bdot(onehot(iota((RANK, span), 0) == row), part[...])
    delta = delta.astype(BF)
    rem = rem_ref[...]
    for t in range(STEPS):
        low = low_ref[pl.ds(t * ROWS, ROWS), :]
        raw = bdot(low[:, :RANK], delta) + bias_ref[...]
        size = jnp.maximum(raw, 0.0) + jnp.log1p(jnp.exp(-jnp.abs(raw)))
        active = rem > t
        size = jnp.where(active, size, 0.0)
        act = act_ref[t]
        gate = gate_ref[t].astype(F32)
        dt_ref[t] = size
        dx_ref[t] = size * act
        sk_ref[t] = skip_ref[...] * act
        sg_ref[t] = jnp.where(active, gate / (1.0 + jnp.exp(-gate)), 0.0)
        coefs = low[:, RANK:].astype(F32)
        for n in range(2 * STATE):
            bc_ref[t, n] = jnp.broadcast_to(coefs[:, n : n + 1], (ROWS, 128))


def step_stage(me, own, other, parts, bias, act, gate, skip, rem, log):
    shape = jax.ShapeDtypeStruct
    rows = shape((STEPS, ROWS, CH), F32)
    return pl.pallas_call(
        step_kernel,
        name="sizes",
        out_shape=(rows, rows, rows, rows, shape((STEPS, 2 * STATE, ROWS, 128), F32), shape((STATE, CH), F32)),
        in_specs=[SMEM] + [VMEM] * 12,
        out_specs=(VMEM,) * 6,
        scratch_shapes=[pltpu.VMEM((STEPS * ROWS, LOW), BF)],
        compiler_params=pltpu.CompilerParams(vmem_limit_bytes=60 << 20),
    )(me, own, other, *parts, bias, act, gate, skip, rem, log)


BLOCK = 8
BLOCKS = ROWS // BLOCK


def scan_kernel(
    at_ref, main_ref, e0, e1, e2, e3, _ours, _theirs, dt_ref, dx_ref, sk_ref, sg_ref, bc_ref, rate_ref,
    out_ref, final_ref, held, wide, sems,
):
    b = pl.program_id(0)

    def fetch(block):
        for i in range(BLOCK):
            at = at_ref[0, block * BLOCK + i]

            @pl.when(at < ROWS)
            def _():
                pltpu.make_async_copy(main_ref.at[at], held.at[block, i], sems.at[block]).start()

            for k, extra in enumerate((e0, e1, e2, e3)):
                row = at - ROWS - k * BASE

                @pl.when((row >= 0) & (row < BASE))
                def _(row=row, extra=extra):
                    pltpu.make_async_copy(extra.at[row], held.at[block, i], sems.at[block]).start()

    @pl.when(b == 0)
    def _():
        for block in range(3):
            fetch(block)

    @pl.when(b + 3 < BLOCKS)
    def _():
        fetch(b + 3)

    pltpu.make_async_copy(main_ref.at[pl.ds(0, BLOCK)], held.at[b], sems.at[b]).wait()
    for i in range(BLOCK):
        for l in range(CH // 128):
            wide[l, pl.ds(i * STATE, STATE), :] = held[b, i, :, pl.ds(l * 128, 128)].astype(F32)

    def lanes(l, carry):
        cols = pl.ds(pl.multiple_of(l * 128, 128), 128)
        dts = [dt_ref[t, :, cols] for t in range(STEPS)]
        dxs = [dx_ref[t, :, cols] for t in range(STEPS)]
        sums = [sk_ref[t, :, cols] for t in range(STEPS)]
        for n in range(STATE):
            here = pl.ds(n, BLOCK, stride=STATE)
            h = wide[l, here, :]
            rate = jnp.broadcast_to(rate_ref[pl.ds(n, 1), cols], (BLOCK, 128))
            for t in range(STEPS):
                h = jnp.exp2(dts[t] * rate) * h + dxs[t] * bc_ref[t, n]
                sums[t] += h * bc_ref[t, STATE + n]
            wide[l, here, :] = h
        for t in range(STEPS):
            out_ref[t, :, cols] = (sums[t] * sg_ref[t, :, cols]).astype(BF)
        return carry

    lax.fori_loop(0, CH // 128, lanes, 0)
    for i in range(BLOCK):
        for l in range(CH // 128):
            final_ref[i, :, pl.ds(l * 128, 128)] = wide[l, pl.ds(i * STATE, STATE), :].astype(BF)


def scan_stage(at, main, extras, ahead, dt, dx, sk, sg, bc, rate):
    shape = jax.ShapeDtypeStruct
    rows = pl.BlockSpec((STEPS, BLOCK, CH), lambda b, at: (0, b, 0))
    return pl.pallas_call(
        scan_kernel,
        name="scan",
        out_shape=(shape((STEPS, ROWS, CH), BF), shape((ROWS, STATE, CH), BF)),
        grid_spec=pltpu.PrefetchScalarGridSpec(
            num_scalar_prefetch=1,
            grid=(BLOCKS,),
            in_specs=[ANY] * 7
            + [
                rows,
                rows,
                rows,
                rows,
                pl.BlockSpec((STEPS, 2 * STATE, BLOCK, 128), lambda b, at: (0, 0, b, 0)),
                pl.BlockSpec((STATE, CH), lambda b, at: (0, 0)),
            ],
            out_specs=(rows, pl.BlockSpec((BLOCK, STATE, CH), lambda b, at: (b, 0, 0))),
            scratch_shapes=[
                pltpu.VMEM((BLOCKS, BLOCK, STATE, CH), BF),
                pltpu.VMEM((CH // 128, BLOCK * STATE, 128), F32),
                pltpu.SemaphoreType.DMA((BLOCKS,)),
            ],
        ),
        compiler_params=pltpu.CompilerParams(vmem_limit_bytes=60 << 20),
    )(at, main, *extras, *ahead, dt, dx, sk, sg, bc, rate)


def after_kernel(*refs):
    pass


def after(value, *others):
    return pl.pallas_call(
        after_kernel,
        name="after",
        out_shape=jax.ShapeDtypeStruct(value.shape, value.dtype),
        in_specs=[ANY] * (1 + len(others)),
        out_specs=ANY,
        input_output_aliases={0: 0},
    )(value, *others)


def shift(value, axis, size, k):
    return lax.ppermute(value, axis, [(i, (i + k) % size) for i in range(size)])


def reduce_mp(low, y, c):
    chunk = STEPS * ROWS // (NY * NC)
    halves = low.reshape(NC, NY * chunk, LOW)
    got = shift(lax.dynamic_index_in_dim(halves, 1 - c, 0, False), "c", NC, 1)
    mine = lax.dynamic_index_in_dim(halves, c, 0, False).astype(F32) + got.astype(F32)
    quarters = mine.reshape(NY, chunk, LOW)
    rounded = quarters.astype(BF)
    total = lax.dynamic_index_in_dim(quarters, y, 0, False)
    came = [
        shift(lax.dynamic_index_in_dim(rounded, lax.rem(y + k, NY), 0, False), "y", NY, k)
        for k in range(1, NY)
    ]
    total = (total + came[0].astype(F32) + came[1].astype(F32) + came[2].astype(F32)).astype(BF)
    own = jnp.stack([total] + [shift(total, "y", NY, NY - m) for m in range(1, NY)])
    return own, shift(own, "c", NC, 1)


def mix(rows, ours, theirs, x, y):
    width = ours.shape[0] // NY
    visits = [rows] + [shift(rows, "x", NX, k) for k in range(1, NX)]
    pieces = []
    for visit in visits:
        got = shift(bdot_t(visit, theirs).astype(BF), "c", NC, 1)
        pieces.append((bdot_t(visit, ours) + got.astype(F32)).astype(BF))

    def over_y(some):
        def block(s):
            at = lax.rem(y + s, NY) * width
            return [lax.dynamic_slice_in_dim(piece, at, width, 1) for piece in some]

        total = jnp.concatenate(block(0), axis=0).astype(F32)
        for s in range(1, NY):
            total += shift(jnp.concatenate(block(s), axis=0), "y", NY, s).astype(F32)
        return total.astype(BF).reshape(len(some), rows.shape[0], width)

    total = over_y(pieces)
    back = [total[0]] + [shift(total[k], "x", NX, NX - k) for k in range(1, NX)]
    twice = jnp.stack(back + back)
    ordered = lax.dynamic_slice_in_dim(twice, lax.rem(NX - x, NX), NX, 0)
    return ordered.transpose(1, 0, 2)


def per_device(
    input_steps, gate_steps, conv_state, ssm_state, new_slot, remaining, conv_weight, conv_bias,
    coef_proj, delta_proj, delta_bias, decay_log, skip_gain, out_proj,
):
    z, x, y, c = (lax.axis_index(name) for name in ("z", "x", "y", "c"))
    group = z * NX + x
    me = jnp.stack([group, x, y, c]).astype(I32)
    at, relay, rem, col, ext, buf, block, main, proj = plan(
        me,
        new_slot.reshape(1, -1),
        remaining.reshape(1, -1),
        new_slot.reshape(GROUPS, ROWS),
        conv_state.transpose(1, 0, 2),
        coef_proj.T,
        delta_proj,
        out_proj,
        ssm_state,
    )
    gathered = lax.all_gather(block, "z", axis=0)
    moved = lax.all_to_all(
        buf.reshape(GROUPS, SLOT, CH), ("z", "x"), split_axis=0, concat_axis=0, tiled=True
    ).reshape(GROUPS * SLOT, CH)
    ssm_main = lax.all_to_all(after(main, gathered), ("z", "x"), split_axis=0, concat_axis=0, tiled=True)

    def turned(value):
        return [value] + [shift(value, "x", NX, k) for k in range(1, NX)]

    secs = turned(gathered[:, :SEC].reshape(NZ * SEC, CH))
    deltas = turned(gathered[:, SEC:GATH].reshape(NZ * DELTA, CH))
    extras = [
        lax.dynamic_slice(gathered, (relay[k, 0], GATH, 0), (1, BASE * STATE, CH)) for k in range(NX)
    ]
    extras = [extras[0]] + [shift(extras[k], "x", NX, k) for k in range(1, NX)]
    extras = [e.reshape(BASE, STATE, CH) for e in extras]
    act, low, conv_final, proj = conv_stage(
        me, moved, secs, col, ext, rem, input_steps, conv_weight, conv_bias.reshape(1, -1), proj
    )
    columns = lax.all_gather(proj, "z", axis=0).reshape(NY, NC, -1, CH)
    halves = [lax.dynamic_index_in_dim(columns, core, 1, False).reshape(-1, CH) for core in (c, 1 - c)]
    own, other = reduce_mp(low, y, c)
    dt, dx, sk, sg, bc, rate = step_stage(
        me, own, other, deltas, delta_bias.reshape(1, -1), act, gate_steps, skip_gain.reshape(1, -1), rem, decay_log
    )
    stepped, ssm_final = scan_stage(at, ssm_main, extras, halves, dt, dx, sk, sg, bc, rate)
    mixed = mix(stepped.reshape(STEPS * ROWS, CH), *halves, x, y)
    return mixed.reshape(STEPS, ROWS, -1), conv_final.transpose(1, 0, 2), ssm_final


def solution(mesh):
    fine = Mesh(mesh.devices.reshape(NZ, NX, NY, NC), ("z", "x", "y", "c"))
    dp, mp = ("z", "x"), ("y", "c")
    return jax.shard_map(
        per_device,
        mesh=fine,
        in_specs=(
            P(None, dp, mp),
            P(None, dp, mp),
            P(dp, None, mp),
            P(dp, None, mp),
            P(),
            P(),
            P(None, mp),
            P(mp),
            P(mp, dp),
            P(dp, mp),
            P(mp),
            P(None, mp),
            P(mp),
            P(mp, dp),
        ),
        out_specs=(P(None, dp, mp), P(dp, None, mp), P(dp, None, mp)),
        check_vma=False,
    )
```

```python
import functools

import jax
import jax.numpy as jnp
from jax import lax
from jax.experimental import pallas as pl
from jax.experimental.pallas import tpu as pltpu
from jax.sharding import Mesh
from jax.sharding import PartitionSpec as P

BF = jnp.bfloat16
F32 = jnp.float32
I32 = jnp.int32
NZ, NX, NY, NC = 8, 4, 4, 2
GROUPS = NZ * NX
ROWS = 96
CH = 1024
STATE = 16
RANK = 512
STEPS = 4
LOW = RANK + 2 * STATE
COEF = LOW // GROUPS
DELTA = RANK // GROUPS
BASE = ROWS // GROUPS
SLOT = 16
SEC = 32
GATH = SEC + DELTA
LOG2E = 1.4426950408889634
VMEM = pl.BlockSpec(memory_space=pltpu.VMEM)
SMEM = pl.BlockSpec(memory_space=pltpu.SMEM)
ANY = pl.BlockSpec(memory_space=pl.ANY)


def iota(shape, dim):
    return lax.broadcasted_iota(I32, shape, dim)


def bdot(a, b):
    return jnp.dot(a, b, preferred_element_type=F32)


def bdot_t(a, b):
    return lax.dot_general(a, b, (((1,), (1,)), ((), ())), preferred_element_type=F32)


def onehot(cond):
    return cond.astype(F32).astype(BF)


def plan_kernel(
    me_ref, slots_ref, remaining_ref, table_ref, conv_ref, coef_ref, delta_ref, proj_ref, ssm_ref,
    gather_ref, relay_ref, rem_ref, col_ref, ext_ref, buf_ref, block_ref, main_ref, proj_out_ref,
    pick_ref, pick_smem, sems,
):
    me = me_ref[0]
    x = me_ref[1]
    square = (ROWS, ROWS)
    eye = iota(square, 0) == iota(square, 1)
    to_row = table_ref[pl.ds(me, 1), :] // ROWS
    to = jnp.sum(jnp.where(eye, to_row, 0), axis=1, keepdims=True)
    same = to == to_row
    order_row = jnp.sum((same & (iota(square, 0) < iota(square, 1))).astype(I32), axis=0, keepdims=True)
    order = jnp.sum((same & (iota(square, 1) < iota(square, 0))).astype(I32), axis=1, keepdims=True)
    place = jnp.where(order < BASE, to * BASE + order, ROWS + order - BASE)
    lanes = (ROWS, 128)
    picked = jnp.sum(jnp.where(place == iota(lanes, 1), iota(lanes, 0), 0), axis=0, keepdims=True)
    pick_ref[...] = jnp.broadcast_to(picked, pick_ref.shape)
    picking = pltpu.make_async_copy(pick_ref, pick_smem, sems.at[0])
    picking.start()
    picking.wait()
    for p in range(BASE):
        pltpu.make_async_copy(
            ssm_ref.at[pick_smem[0, ROWS + p]], block_ref.at[pl.ds(GATH + p * STATE, STATE)], sems.at[2]
        ).start()

    def send(p, carry):
        pltpu.make_async_copy(ssm_ref.at[pick_smem[0, p]], main_ref.at[p], sems.at[1]).start()
        return carry

    lax.fori_loop(0, ROWS, send, 0)
    buf = jnp.zeros((GROUPS * SLOT, CH), F32)
    sec = bdot(onehot(iota((SEC, COEF), 0) == iota((SEC, COEF), 1)), coef_ref[...])
    for tap in range(3):
        dest = jnp.where(order_row < BASE, to_row * SLOT + order_row * 3 + tap, -1)
        buf += bdot(onehot(iota((GROUPS * SLOT, ROWS), 0) == dest), conv_ref[tap])
        dest = jnp.where(order_row < BASE, -1, COEF + (order_row - BASE) * 3 + tap)
        sec += bdot(onehot(iota((SEC, ROWS), 0) == dest), conv_ref[tap])
    buf_ref[...] = buf.astype(BF)
    block_ref[pl.ds(0, SEC), :] = sec.astype(BF)
    block_ref[pl.ds(SEC, DELTA), :] = delta_ref[...]
    match = (slots_ref[...] == me * ROWS + iota((ROWS, GROUPS * ROWS), 0)).astype(I32)
    inv = jnp.sum(match * iota(match.shape, 1), axis=1, keepdims=True)
    rem_ref[...] = jnp.sum(match * remaining_ref[...], axis=1, keepdims=True)
    inv_row = jnp.sum(jnp.where(eye, inv, 0), axis=0, keepdims=True)
    src = inv // ROWS
    src_row = inv_row // ROWS
    rank = jnp.sum(
        ((src == src_row) & (inv_row < inv)).astype(I32), axis=1, keepdims=True
    )
    rank_row = jnp.sum(
        ((src == src_row) & (inv < inv_row)).astype(I32), axis=0, keepdims=True
    )
    turn = lax.rem(x - lax.rem(src_row, NX) + NX, NX)
    where_row = jnp.where(rank_row < BASE, src_row * BASE + rank_row, ROWS + (turn - 1) * BASE + rank_row)
    gather_ref[...] = jnp.broadcast_to(where_row, gather_ref.shape)
    for tap in range(3):
        at = pl.ds(tap * ROWS, ROWS)
        col_ref[at, :] = jnp.where(rank < BASE, src * SLOT + rank * 3 + tap, -1)
        ext_ref[at, :] = jnp.where(
            rank < BASE, -1, src * SEC + COEF + (rank - BASE) * 3 + tap
        )
    target = table_ref[...] // ROWS
    groups = iota((GROUPS, 1), 0)
    for k in range(NX):
        dest = me - x + lax.rem(x + k, NX)
        count = jnp.sum((target == dest).astype(I32), axis=1, keepdims=True)
        holds = (count > BASE) & (lax.rem(groups, NX) == x)
        z = jnp.sum(jnp.where(holds, groups // NX, 0), axis=0, keepdims=True)
        relay_ref[pl.ds(k, 1), :] = jnp.broadcast_to(z, (1, 128))
    pltpu.make_async_copy(
        ssm_ref.at[pl.ds(0, BASE)].reshape(BASE * STATE, CH), block_ref.at[pl.ds(GATH, BASE * STATE)], sems.at[2]
    ).wait()
    pltpu.make_async_copy(ssm_ref, main_ref, sems.at[1]).wait()
    proj_out_ref[...] = proj_ref[...].T


def plan(me, slots, remaining, table, conv, coef, delta, proj, ssm):
    shape = jax.ShapeDtypeStruct
    return pl.pallas_call(
        plan_kernel,
        name="plan",
        out_shape=(
            shape((8, ROWS), I32),
            shape((NX, 128), I32),
            shape((ROWS, 1), I32),
            shape((3 * ROWS, 1), I32),
            shape((3 * ROWS, 1), I32),
            shape((GROUPS * SLOT, CH), BF),
            shape((GATH + BASE * STATE, CH), BF),
            shape((ROWS, STATE, CH), BF),
            shape(proj.shape[::-1], BF),
        ),
        in_specs=[SMEM] + [VMEM] * 7 + [ANY],
        out_specs=(VMEM,) * 9,
        scratch_shapes=[
            pltpu.VMEM((8, 128), I32),
            pltpu.SMEM((8, 128), I32),
            pltpu.SemaphoreType.DMA((3,)),
        ],
        compiler_params=pltpu.CompilerParams(vmem_limit_bytes=60 << 20),
    )(me, slots, remaining, table, conv, coef, delta, proj, ssm)


def conv_kernel(
    me_ref, moved_ref, g0, g1, g2, g3, col_ref, ext_ref, rem_ref, inputs_ref, weight_ref, bias_ref,
    act_ref, low_ref, final_ref,
):
    x = me_ref[1]
    parts = (g0, g1, g2, g3)
    span = NZ * SEC
    window = bdot(onehot(col_ref[...] == iota((3 * ROWS, GROUPS * SLOT), 1)), moved_ref[...])
    coef = jnp.zeros((LOW, CH), F32)
    for k, part in enumerate(parts):
        at = iota((1, span), 1)
        z, q = at // SEC, at % SEC
        group = z * NX + lax.rem(x - k + NX, NX)
        ext = onehot(ext_ref[...] == group * SEC + q)
        window += bdot(ext, part[...])
        row = jnp.where(q < COEF, group * COEF + q, -1)
        coef += bdot(onehot(iota((LOW, span), 0) == row), part[...])
    coef = coef.astype(BF)
    taps = [window[tap * ROWS : (tap + 1) * ROWS] for tap in range(3)]
    taps += [inputs_ref[t].astype(F32) for t in range(STEPS)]
    weight = weight_ref[...]
    for t in range(STEPS):
        out = bias_ref[...] + sum(taps[t + k] * weight[k : k + 1] for k in range(4))
        act = out / (1.0 + jnp.exp(-out))
        act_ref[t] = act
        low_ref[pl.ds(t * ROWS, ROWS), :] = bdot_t(act.astype(BF), coef).astype(BF)
    rem = rem_ref[...]
    for k in range(3):
        kept = taps[k]
        for t in range(1, STEPS + 1):
            kept = jnp.where(rem >= t, taps[t + k], kept)
        final_ref[k] = kept.astype(BF)


def conv_stage(me, moved, parts, col, ext, rem, inputs, weight, bias):
    shape = jax.ShapeDtypeStruct
    return pl.pallas_call(
        conv_kernel,
        name="conv",
        out_shape=(
            shape((STEPS, ROWS, CH), F32),
            shape((STEPS * ROWS, LOW), BF),
            shape((3, ROWS, CH), BF),
        ),
        in_specs=[SMEM] + [VMEM] * 11,
        out_specs=(VMEM,) * 3,
        compiler_params=pltpu.CompilerParams(vmem_limit_bytes=60 << 20),
    )(me, moved, *parts, col, ext, rem, inputs, weight, bias)


def step_kernel(
    me_ref, own_ref, other_ref, g0, g1, g2, g3, bias_ref, act_ref, gate_ref, skip_ref, rem_ref, log_ref,
    dt_ref, dx_ref, sk_ref, sg_ref, bc_ref, rate_ref, low_ref,
):
    x, y, c = me_ref[1], me_ref[2], me_ref[3]
    rate_ref[...] = -jnp.exp(log_ref[...]) * LOG2E
    chunk = STEPS * ROWS // (NY * NC)
    for half, piece in ((c, own_ref), (1 - c, other_ref)):
        for m in range(NY):
            at = half * NY + lax.rem(y + m, NY)
            low_ref[pl.ds(pl.multiple_of(at * chunk, 16), chunk), :] = piece[m]
    span = NZ * DELTA
    delta = jnp.zeros((RANK, CH), F32)
    for k, part in enumerate((g0, g1, g2, g3)):
        at = iota((1, span), 1)
        z, q = at // DELTA, at % DELTA
        row = (z * NX + lax.rem(x - k + NX, NX)) * DELTA + q
        delta += bdot(onehot(iota((RANK, span), 0) == row), part[...])
    delta = delta.astype(BF)
    rem = rem_ref[...]
    for t in range(STEPS):
        low = low_ref[pl.ds(t * ROWS, ROWS), :]
        raw = bdot(low[:, :RANK], delta) + bias_ref[...]
        size = jnp.maximum(raw, 0.0) + jnp.log1p(jnp.exp(-jnp.abs(raw)))
        active = rem > t
        size = jnp.where(active, size, 0.0)
        act = act_ref[t]
        gate = gate_ref[t].astype(F32)
        dt_ref[t] = size
        dx_ref[t] = size * act
        sk_ref[t] = skip_ref[...] * act
        sg_ref[t] = jnp.where(active, gate / (1.0 + jnp.exp(-gate)), 0.0)
        coefs = low[:, RANK:].astype(F32)
        for n in range(2 * STATE):
            bc_ref[t, n] = jnp.broadcast_to(coefs[:, n : n + 1], (ROWS, 128))


def step_stage(me, own, other, parts, bias, act, gate, skip, rem, log):
    shape = jax.ShapeDtypeStruct
    rows = shape((STEPS, ROWS, CH), F32)
    return pl.pallas_call(
        step_kernel,
        name="sizes",
        out_shape=(rows, rows, rows, rows, shape((STEPS, 2 * STATE, ROWS, 128), F32), shape((STATE, CH), F32)),
        in_specs=[SMEM] + [VMEM] * 12,
        out_specs=(VMEM,) * 6,
        scratch_shapes=[pltpu.VMEM((STEPS * ROWS, LOW), BF)],
        compiler_params=pltpu.CompilerParams(vmem_limit_bytes=60 << 20),
    )(me, own, other, *parts, bias, act, gate, skip, rem, log)


BLOCK = 8
BLOCKS = ROWS // BLOCK


def scan_kernel(
    at_ref, main_ref, e0, e1, e2, e3, _ours, _theirs, dt_ref, dx_ref, sk_ref, sg_ref, bc_ref, rate_ref,
    out_ref, final_ref, held, wide, sems,
):
    b = pl.program_id(0)

    def fetch(block):
        for i in range(BLOCK):
            at = at_ref[0, block * BLOCK + i]

            @pl.when(at < ROWS)
            def _():
                pltpu.make_async_copy(main_ref.at[at], held.at[block, i], sems.at[block]).start()

            for k, extra in enumerate((e0, e1, e2, e3)):
                row = at - ROWS - k * BASE

                @pl.when((row >= 0) & (row < BASE))
                def _(row=row, extra=extra):
                    pltpu.make_async_copy(extra.at[row], held.at[block, i], sems.at[block]).start()

    @pl.when(b == 0)
    def _():
        for block in range(3):
            fetch(block)

    @pl.when(b + 3 < BLOCKS)
    def _():
        fetch(b + 3)

    pltpu.make_async_copy(main_ref.at[pl.ds(0, BLOCK)], held.at[b], sems.at[b]).wait()
    for i in range(BLOCK):
        for l in range(CH // 128):
            wide[l, pl.ds(i * STATE, STATE), :] = held[b, i, :, pl.ds(l * 128, 128)].astype(F32)

    def lanes(l, carry):
        cols = pl.ds(pl.multiple_of(l * 128, 128), 128)
        dts = [dt_ref[t, :, cols] for t in range(STEPS)]
        dxs = [dx_ref[t, :, cols] for t in range(STEPS)]
        sums = [sk_ref[t, :, cols] for t in range(STEPS)]
        for n in range(STATE):
            here = pl.ds(n, BLOCK, stride=STATE)
            h = wide[l, here, :]
            rate = jnp.broadcast_to(rate_ref[pl.ds(n, 1), cols], (BLOCK, 128))
            for t in range(STEPS):
                h = jnp.exp2(dts[t] * rate) * h + dxs[t] * bc_ref[t, n]
                sums[t] += h * bc_ref[t, STATE + n]
            wide[l, here, :] = h
        for t in range(STEPS):
            out_ref[t, :, cols] = (sums[t] * sg_ref[t, :, cols]).astype(BF)
        return carry

    lax.fori_loop(0, CH // 128, lanes, 0)
    for i in range(BLOCK):
        for l in range(CH // 128):
            final_ref[i, :, pl.ds(l * 128, 128)] = wide[l, pl.ds(i * STATE, STATE), :].astype(BF)


def scan_stage(at, main, extras, ahead, dt, dx, sk, sg, bc, rate):
    shape = jax.ShapeDtypeStruct
    rows = pl.BlockSpec((STEPS, BLOCK, CH), lambda b, at: (0, b, 0))
    return pl.pallas_call(
        scan_kernel,
        name="scan",
        out_shape=(shape((STEPS, ROWS, CH), BF), shape((ROWS, STATE, CH), BF)),
        grid_spec=pltpu.PrefetchScalarGridSpec(
            num_scalar_prefetch=1,
            grid=(BLOCKS,),
            in_specs=[ANY] * 7
            + [
                rows,
                rows,
                rows,
                rows,
                pl.BlockSpec((STEPS, 2 * STATE, BLOCK, 128), lambda b, at: (0, 0, b, 0)),
                pl.BlockSpec((STATE, CH), lambda b, at: (0, 0)),
            ],
            out_specs=(rows, pl.BlockSpec((BLOCK, STATE, CH), lambda b, at: (b, 0, 0))),
            scratch_shapes=[
                pltpu.VMEM((BLOCKS, BLOCK, STATE, CH), BF),
                pltpu.VMEM((CH // 128, BLOCK * STATE, 128), F32),
                pltpu.SemaphoreType.DMA((BLOCKS,)),
            ],
        ),
        compiler_params=pltpu.CompilerParams(vmem_limit_bytes=60 << 20),
    )(at, main, *extras, *ahead, dt, dx, sk, sg, bc, rate)


def after_kernel(*refs):
    pass


def after(value, *others):
    return pl.pallas_call(
        after_kernel,
        name="after",
        out_shape=jax.ShapeDtypeStruct(value.shape, value.dtype),
        in_specs=[ANY] * (1 + len(others)),
        out_specs=ANY,
        input_output_aliases={0: 0},
    )(value, *others)


def shift(value, axis, size, k):
    return lax.ppermute(value, axis, [(i, (i + k) % size) for i in range(size)])


def reduce_mp(low, y, c):
    chunk = STEPS * ROWS // (NY * NC)
    halves = low.reshape(NC, NY * chunk, LOW)
    got = shift(lax.dynamic_index_in_dim(halves, 1 - c, 0, False), "c", NC, 1)
    mine = lax.dynamic_index_in_dim(halves, c, 0, False).astype(F32) + got.astype(F32)
    quarters = mine.reshape(NY, chunk, LOW)
    rounded = quarters.astype(BF)
    total = lax.dynamic_index_in_dim(quarters, y, 0, False)
    came = [
        shift(lax.dynamic_index_in_dim(rounded, lax.rem(y + k, NY), 0, False), "y", NY, k)
        for k in range(1, NY)
    ]
    total = (total + came[0].astype(F32) + came[1].astype(F32) + came[2].astype(F32)).astype(BF)
    own = jnp.stack([total] + [shift(total, "y", NY, NY - m) for m in range(1, NY)])
    return own, shift(own, "c", NC, 1)


def mix(rows, ours, theirs, x, y):
    width = ours.shape[0] // NY
    visits = [rows] + [shift(rows, "x", NX, k) for k in range(1, NX)]
    pieces = []
    for visit in visits:
        got = shift(bdot_t(visit, theirs).astype(BF), "c", NC, 1)
        pieces.append((bdot_t(visit, ours) + got.astype(F32)).astype(BF))

    def over_y(some):
        def block(s):
            at = lax.rem(y + s, NY) * width
            return [lax.dynamic_slice_in_dim(piece, at, width, 1) for piece in some]

        total = jnp.concatenate(block(0), axis=0).astype(F32)
        for s in range(1, NY):
            total += shift(jnp.concatenate(block(s), axis=0), "y", NY, s).astype(F32)
        return total.astype(BF).reshape(len(some), rows.shape[0], width)

    first, rest = over_y(pieces[:1]), over_y(pieces[1:])
    back = [first[0]] + [shift(rest[k - 1], "x", NX, NX - k) for k in range(1, NX)]
    twice = jnp.stack(back + back)
    ordered = lax.dynamic_slice_in_dim(twice, lax.rem(NX - x, NX), NX, 0)
    return ordered.transpose(1, 0, 2)


def per_device(
    input_steps, gate_steps, conv_state, ssm_state, new_slot, remaining, conv_weight, conv_bias,
    coef_proj, delta_proj, delta_bias, decay_log, skip_gain, out_proj,
):
    z, x, y, c = (lax.axis_index(name) for name in ("z", "x", "y", "c"))
    group = z * NX + x
    me = jnp.stack([group, x, y, c]).astype(I32)
    at, relay, rem, col, ext, buf, block, main, proj = plan(
        me,
        new_slot.reshape(1, -1),
        remaining.reshape(1, -1),
        new_slot.reshape(GROUPS, ROWS),
        conv_state.transpose(1, 0, 2),
        coef_proj.T,
        delta_proj,
        out_proj,
        ssm_state,
    )
    gathered = lax.all_gather(block, "z", axis=0)
    moved = lax.all_to_all(
        buf.reshape(GROUPS, SLOT, CH), ("z", "x"), split_axis=0, concat_axis=0, tiled=True
    ).reshape(GROUPS * SLOT, CH)
    def turned(value):
        return [value] + [shift(value, "x", NX, k) for k in range(1, NX)]

    secs = turned(gathered[:, :SEC].reshape(NZ * SEC, CH))
    ssm_main = lax.all_to_all(
        after(main, moved, *secs[1:]), ("z", "x"), split_axis=0, concat_axis=0, tiled=True
    )
    deltas = turned(gathered[:, SEC:GATH].reshape(NZ * DELTA, CH))
    extras = [
        lax.dynamic_slice(gathered, (relay[k, 0], GATH, 0), (1, BASE * STATE, CH)) for k in range(NX)
    ]
    extras = [extras[0]] + [shift(extras[k], "x", NX, k) for k in range(1, NX)]
    extras = [e.reshape(BASE, STATE, CH) for e in extras]
    act, low, conv_final = conv_stage(
        me, moved, secs, col, ext, rem, input_steps, conv_weight, conv_bias.reshape(1, -1)
    )
    columns = lax.all_gather(after(proj, gathered), "z", axis=0).reshape(NY, NC, -1, CH)
    halves = [lax.dynamic_index_in_dim(columns, core, 1, False).reshape(-1, CH) for core in (c, 1 - c)]
    own, other = reduce_mp(low, y, c)
    dt, dx, sk, sg, bc, rate = step_stage(
        me, own, other, deltas, delta_bias.reshape(1, -1), act, gate_steps, skip_gain.reshape(1, -1), rem, decay_log
    )
    stepped, ssm_final = scan_stage(at, ssm_main, extras, halves, dt, dx, sk, sg, bc, rate)
    mixed = mix(stepped.reshape(STEPS * ROWS, CH), *halves, x, y)
    return mixed.reshape(STEPS, ROWS, -1), conv_final.transpose(1, 0, 2), ssm_final


def solution(mesh):
    fine = Mesh(mesh.devices.reshape(NZ, NX, NY, NC), ("z", "x", "y", "c"))
    dp, mp = ("z", "x"), ("y", "c")
    return jax.shard_map(
        per_device,
        mesh=fine,
        in_specs=(
            P(None, dp, mp),
            P(None, dp, mp),
            P(dp, None, mp),
            P(dp, None, mp),
            P(),
            P(),
            P(None, mp),
            P(mp),
            P(mp, dp),
            P(dp, mp),
            P(mp),
            P(None, mp),
            P(mp),
            P(mp, dp),
        ),
        out_specs=(P(None, dp, mp), P(dp, None, mp), P(dp, None, mp)),
        check_vma=False,
    )
```

```python
import functools

import jax
import jax.numpy as jnp
from jax import lax
from jax.experimental import pallas as pl
from jax.experimental.pallas import tpu as pltpu
from jax.sharding import Mesh
from jax.sharding import PartitionSpec as P

BF = jnp.bfloat16
F32 = jnp.float32
I32 = jnp.int32
NZ, NX, NY, NC = 8, 4, 4, 2
GROUPS = NZ * NX
ROWS = 96
CH = 1024
STATE = 16
RANK = 512
STEPS = 4
LOW = RANK + 2 * STATE
COEF = LOW // GROUPS
DELTA = RANK // GROUPS
BASE = ROWS // GROUPS
SLOT = 16
SEC = 32
GATH = SEC + DELTA
LOG2E = 1.4426950408889634
VMEM = pl.BlockSpec(memory_space=pltpu.VMEM)
SMEM = pl.BlockSpec(memory_space=pltpu.SMEM)
ANY = pl.BlockSpec(memory_space=pl.ANY)


def iota(shape, dim):
    return lax.broadcasted_iota(I32, shape, dim)


def bdot(a, b):
    return jnp.dot(a, b, preferred_element_type=F32)


def bdot_t(a, b):
    return lax.dot_general(a, b, (((1,), (1,)), ((), ())), preferred_element_type=F32)


def onehot(cond):
    return cond.astype(F32).astype(BF)


def plan_kernel(
    me_ref, slots_ref, remaining_ref, table_ref, conv_ref, coef_ref, delta_ref, proj_ref, ssm_ref,
    gather_ref, relay_ref, rem_ref, col_ref, ext_ref, buf_ref, block_ref, main_ref, proj_out_ref,
    pick_ref, pick_smem, sems,
):
    me = me_ref[0]
    x = me_ref[1]
    square = (ROWS, ROWS)
    eye = iota(square, 0) == iota(square, 1)
    to_row = table_ref[pl.ds(me, 1), :] // ROWS
    to = jnp.sum(jnp.where(eye, to_row, 0), axis=1, keepdims=True)
    same = to == to_row
    order_row = jnp.sum((same & (iota(square, 0) < iota(square, 1))).astype(I32), axis=0, keepdims=True)
    order = jnp.sum((same & (iota(square, 1) < iota(square, 0))).astype(I32), axis=1, keepdims=True)
    place = jnp.where(order < BASE, to * BASE + order, ROWS + order - BASE)
    lanes = (ROWS, 128)
    picked = jnp.sum(jnp.where(place == iota(lanes, 1), iota(lanes, 0), 0), axis=0, keepdims=True)
    pick_ref[...] = jnp.broadcast_to(picked, pick_ref.shape)
    picking = pltpu.make_async_copy(pick_ref, pick_smem, sems.at[0])
    picking.start()
    picking.wait()
    for p in range(BASE):
        pltpu.make_async_copy(
            ssm_ref.at[pick_smem[0, ROWS + p]], block_ref.at[pl.ds(GATH + p * STATE, STATE)], sems.at[2]
        ).start()

    def send(p, carry):
        pltpu.make_async_copy(ssm_ref.at[pick_smem[0, p]], main_ref.at[p], sems.at[1]).start()
        return carry

    lax.fori_loop(0, ROWS, send, 0)
    buf = jnp.zeros((GROUPS * SLOT, CH), F32)
    sec = bdot(onehot(iota((SEC, COEF), 0) == iota((SEC, COEF), 1)), coef_ref[...])
    for tap in range(3):
        dest = jnp.where(order_row < BASE, to_row * SLOT + order_row * 3 + tap, -1)
        buf += bdot(onehot(iota((GROUPS * SLOT, ROWS), 0) == dest), conv_ref[tap])
        dest = jnp.where(order_row < BASE, -1, COEF + (order_row - BASE) * 3 + tap)
        sec += bdot(onehot(iota((SEC, ROWS), 0) == dest), conv_ref[tap])
    buf_ref[...] = buf.astype(BF)
    block_ref[pl.ds(0, SEC), :] = sec.astype(BF)
    block_ref[pl.ds(SEC, DELTA), :] = delta_ref[...]
    match = (slots_ref[...] == me * ROWS + iota((ROWS, GROUPS * ROWS), 0)).astype(I32)
    inv = jnp.sum(match * iota(match.shape, 1), axis=1, keepdims=True)
    rem_ref[...] = jnp.sum(match * remaining_ref[...], axis=1, keepdims=True)
    inv_row = jnp.sum(jnp.where(eye, inv, 0), axis=0, keepdims=True)
    src = inv // ROWS
    src_row = inv_row // ROWS
    rank = jnp.sum(
        ((src == src_row) & (inv_row < inv)).astype(I32), axis=1, keepdims=True
    )
    rank_row = jnp.sum(
        ((src == src_row) & (inv < inv_row)).astype(I32), axis=0, keepdims=True
    )
    turn = lax.rem(x - lax.rem(src_row, NX) + NX, NX)
    where_row = jnp.where(rank_row < BASE, src_row * BASE + rank_row, ROWS + (turn - 1) * BASE + rank_row)
    gather_ref[...] = jnp.broadcast_to(where_row, gather_ref.shape)
    for tap in range(3):
        at = pl.ds(tap * ROWS, ROWS)
        col_ref[at, :] = jnp.where(rank < BASE, src * SLOT + rank * 3 + tap, -1)
        ext_ref[at, :] = jnp.where(
            rank < BASE, -1, src * SEC + COEF + (rank - BASE) * 3 + tap
        )
    target = table_ref[...] // ROWS
    groups = iota((GROUPS, 1), 0)
    for k in range(NX):
        dest = me - x + lax.rem(x + k, NX)
        count = jnp.sum((target == dest).astype(I32), axis=1, keepdims=True)
        holds = (count > BASE) & (lax.rem(groups, NX) == x)
        z = jnp.sum(jnp.where(holds, groups // NX, 0), axis=0, keepdims=True)
        relay_ref[pl.ds(k, 1), :] = jnp.broadcast_to(z, (1, 128))
    pltpu.make_async_copy(
        ssm_ref.at[pl.ds(0, BASE)].reshape(BASE * STATE, CH), block_ref.at[pl.ds(GATH, BASE * STATE)], sems.at[2]
    ).wait()
    pltpu.make_async_copy(ssm_ref, main_ref, sems.at[1]).wait()
    proj_out_ref[...] = proj_ref[...].T


def plan(me, slots, remaining, table, conv, coef, delta, proj, ssm):
    shape = jax.ShapeDtypeStruct
    return pl.pallas_call(
        plan_kernel,
        name="plan",
        out_shape=(
            shape((8, ROWS), I32),
            shape((NX, 128), I32),
            shape((ROWS, 1), I32),
            shape((3 * ROWS, 1), I32),
            shape((3 * ROWS, 1), I32),
            shape((GROUPS * SLOT, CH), BF),
            shape((GATH + BASE * STATE, CH), BF),
            shape((ROWS, STATE, CH), BF),
            shape(proj.shape[::-1], BF),
        ),
        in_specs=[SMEM] + [VMEM] * 7 + [ANY],
        out_specs=(VMEM,) * 9,
        scratch_shapes=[
            pltpu.VMEM((8, 128), I32),
            pltpu.SMEM((8, 128), I32),
            pltpu.SemaphoreType.DMA((3,)),
        ],
        compiler_params=pltpu.CompilerParams(vmem_limit_bytes=60 << 20),
    )(me, slots, remaining, table, conv, coef, delta, proj, ssm)


def conv_kernel(
    me_ref, moved_ref, g0, g1, g2, g3, col_ref, ext_ref, rem_ref, inputs_ref, weight_ref, bias_ref,
    act_ref, low_ref, final_ref,
):
    x = me_ref[1]
    parts = (g0, g1, g2, g3)
    span = NZ * SEC
    window = bdot(onehot(col_ref[...] == iota((3 * ROWS, GROUPS * SLOT), 1)), moved_ref[...])
    coef = jnp.zeros((LOW, CH), F32)
    for k, part in enumerate(parts):
        at = iota((1, span), 1)
        z, q = at // SEC, at % SEC
        group = z * NX + lax.rem(x - k + NX, NX)
        ext = onehot(ext_ref[...] == group * SEC + q)
        window += bdot(ext, part[...])
        row = jnp.where(q < COEF, group * COEF + q, -1)
        coef += bdot(onehot(iota((LOW, span), 0) == row), part[...])
    coef = coef.astype(BF)
    taps = [window[tap * ROWS : (tap + 1) * ROWS] for tap in range(3)]
    taps += [inputs_ref[t].astype(F32) for t in range(STEPS)]
    weight = weight_ref[...]
    for t in range(STEPS):
        out = bias_ref[...] + sum(taps[t + k] * weight[k : k + 1] for k in range(4))
        act = out / (1.0 + jnp.exp(-out))
        act_ref[t] = act
        low_ref[pl.ds(t * ROWS, ROWS), :] = bdot_t(act.astype(BF), coef).astype(BF)
    rem = rem_ref[...]
    for k in range(3):
        kept = taps[k]
        for t in range(1, STEPS + 1):
            kept = jnp.where(rem >= t, taps[t + k], kept)
        final_ref[k] = kept.astype(BF)


def conv_stage(me, moved, parts, col, ext, rem, inputs, weight, bias):
    shape = jax.ShapeDtypeStruct
    return pl.pallas_call(
        conv_kernel,
        name="conv",
        out_shape=(
            shape((STEPS, ROWS, CH), F32),
            shape((STEPS * ROWS, LOW), BF),
            shape((3, ROWS, CH), BF),
        ),
        in_specs=[SMEM] + [VMEM] * 11,
        out_specs=(VMEM,) * 3,
        compiler_params=pltpu.CompilerParams(vmem_limit_bytes=60 << 20),
    )(me, moved, *parts, col, ext, rem, inputs, weight, bias)


def step_kernel(
    me_ref, own_ref, other_ref, g0, g1, g2, g3, bias_ref, act_ref, gate_ref, skip_ref, rem_ref, log_ref,
    dt_ref, dx_ref, sk_ref, sg_ref, bc_ref, rate_ref, low_ref,
):
    x, y, c = me_ref[1], me_ref[2], me_ref[3]
    rate_ref[...] = -jnp.exp(log_ref[...]) * LOG2E
    chunk = STEPS * ROWS // (NY * NC)
    for half, piece in ((c, own_ref), (1 - c, other_ref)):
        for m in range(NY):
            at = half * NY + lax.rem(y + m, NY)
            low_ref[pl.ds(pl.multiple_of(at * chunk, 16), chunk), :] = piece[m]
    span = NZ * DELTA
    delta = jnp.zeros((RANK, CH), F32)
    for k, part in enumerate((g0, g1, g2, g3)):
        at = iota((1, span), 1)
        z, q = at // DELTA, at % DELTA
        row = (z * NX + lax.rem(x - k + NX, NX)) * DELTA + q
        delta += bdot(onehot(iota((RANK, span), 0) == row), part[...])
    delta = delta.astype(BF)
    rem = rem_ref[...]
    for t in range(STEPS):
        low = low_ref[pl.ds(t * ROWS, ROWS), :]
        raw = bdot(low[:, :RANK], delta) + bias_ref[...]
        size = jnp.maximum(raw, 0.0) + jnp.log1p(jnp.exp(-jnp.abs(raw)))
        active = rem > t
        size = jnp.where(active, size, 0.0)
        act = act_ref[t]
        gate = gate_ref[t].astype(F32)
        dt_ref[t] = size
        dx_ref[t] = size * act
        sk_ref[t] = skip_ref[...] * act
        sg_ref[t] = jnp.where(active, gate / (1.0 + jnp.exp(-gate)), 0.0)
        coefs = low[:, RANK:].astype(F32)
        for n in range(2 * STATE):
            bc_ref[t, n] = jnp.broadcast_to(coefs[:, n : n + 1], (ROWS, 128))


def step_stage(me, own, other, parts, bias, act, gate, skip, rem, log):
    shape = jax.ShapeDtypeStruct
    rows = shape((STEPS, ROWS, CH), F32)
    return pl.pallas_call(
        step_kernel,
        name="sizes",
        out_shape=(rows, rows, rows, rows, shape((STEPS, 2 * STATE, ROWS, 128), F32), shape((STATE, CH), F32)),
        in_specs=[SMEM] + [VMEM] * 12,
        out_specs=(VMEM,) * 6,
        scratch_shapes=[pltpu.VMEM((STEPS * ROWS, LOW), BF)],
        compiler_params=pltpu.CompilerParams(vmem_limit_bytes=60 << 20),
    )(me, own, other, *parts, bias, act, gate, skip, rem, log)


BLOCK = 8
BLOCKS = ROWS // BLOCK


def scan_kernel(
    at_ref, main_ref, e0, e1, e2, e3, dt_ref, dx_ref, sk_ref, sg_ref, bc_ref, rate_ref,
    out_ref, final_ref, held, wide, sems,
):
    b = pl.program_id(0)

    def fetch(block):
        for i in range(BLOCK):
            at = at_ref[0, block * BLOCK + i]

            @pl.when(at < ROWS)
            def _():
                pltpu.make_async_copy(main_ref.at[at], held.at[block, i], sems.at[block]).start()

            for k, extra in enumerate((e0, e1, e2, e3)):
                row = at - ROWS - k * BASE

                @pl.when((row >= 0) & (row < BASE))
                def _(row=row, extra=extra):
                    pltpu.make_async_copy(extra.at[row], held.at[block, i], sems.at[block]).start()

    @pl.when(b == 0)
    def _():
        for block in range(3):
            fetch(block)

    @pl.when(b + 3 < BLOCKS)
    def _():
        fetch(b + 3)

    pltpu.make_async_copy(main_ref.at[pl.ds(0, BLOCK)], held.at[b], sems.at[b]).wait()
    for i in range(BLOCK):
        for l in range(CH // 128):
            wide[l, pl.ds(i * STATE, STATE), :] = held[b, i, :, pl.ds(l * 128, 128)].astype(F32)

    def lanes(l, carry):
        cols = pl.ds(pl.multiple_of(l * 128, 128), 128)
        dts = [dt_ref[t, :, cols] for t in range(STEPS)]
        dxs = [dx_ref[t, :, cols] for t in range(STEPS)]
        sums = [sk_ref[t, :, cols] for t in range(STEPS)]
        for n in range(STATE):
            here = pl.ds(n, BLOCK, stride=STATE)
            h = wide[l, here, :]
            rate = jnp.broadcast_to(rate_ref[pl.ds(n, 1), cols], (BLOCK, 128))
            for t in range(STEPS):
                h = jnp.exp2(dts[t] * rate) * h + dxs[t] * bc_ref[t, n]
                sums[t] += h * bc_ref[t, STATE + n]
            wide[l, here, :] = h
        for t in range(STEPS):
            out_ref[t, :, cols] = (sums[t] * sg_ref[t, :, cols]).astype(BF)
        return carry

    lax.fori_loop(0, CH // 128, lanes, 0)
    for i in range(BLOCK):
        for l in range(CH // 128):
            final_ref[i, :, pl.ds(l * 128, 128)] = wide[l, pl.ds(i * STATE, STATE), :].astype(BF)


def scan_stage(at, main, extras, dt, dx, sk, sg, bc, rate):
    shape = jax.ShapeDtypeStruct
    rows = pl.BlockSpec((STEPS, BLOCK, CH), lambda b, at: (0, b, 0))
    return pl.pallas_call(
        scan_kernel,
        name="scan",
        out_shape=(shape((STEPS, ROWS, CH), BF), shape((ROWS, STATE, CH), BF)),
        grid_spec=pltpu.PrefetchScalarGridSpec(
            num_scalar_prefetch=1,
            grid=(BLOCKS,),
            in_specs=[ANY] * 5
            + [
                rows,
                rows,
                rows,
                rows,
                pl.BlockSpec((STEPS, 2 * STATE, BLOCK, 128), lambda b, at: (0, 0, b, 0)),
                pl.BlockSpec((STATE, CH), lambda b, at: (0, 0)),
            ],
            out_specs=(rows, pl.BlockSpec((BLOCK, STATE, CH), lambda b, at: (b, 0, 0))),
            scratch_shapes=[
                pltpu.VMEM((BLOCKS, BLOCK, STATE, CH), BF),
                pltpu.VMEM((CH // 128, BLOCK * STATE, 128), F32),
                pltpu.SemaphoreType.DMA((BLOCKS,)),
            ],
        ),
        compiler_params=pltpu.CompilerParams(vmem_limit_bytes=60 << 20),
    )(at, main, *extras, dt, dx, sk, sg, bc, rate)


def after_kernel(*refs):
    pass


def after(value, *others):
    return pl.pallas_call(
        after_kernel,
        name="after",
        out_shape=jax.ShapeDtypeStruct(value.shape, value.dtype),
        in_specs=[ANY] * (1 + len(others)),
        out_specs=ANY,
        input_output_aliases={0: 0},
    )(value, *others)


def shift(value, axis, size, k):
    return lax.ppermute(value, axis, [(i, (i + k) % size) for i in range(size)])


def reduce_mp(low, y, c):
    chunk = STEPS * ROWS // (NY * NC)
    halves = low.reshape(NC, NY * chunk, LOW)
    got = shift(lax.dynamic_index_in_dim(halves, 1 - c, 0, False), "c", NC, 1)
    mine = lax.dynamic_index_in_dim(halves, c, 0, False).astype(F32) + got.astype(F32)
    quarters = mine.reshape(NY, chunk, LOW)
    rounded = quarters.astype(BF)
    total = lax.dynamic_index_in_dim(quarters, y, 0, False)
    came = [
        shift(lax.dynamic_index_in_dim(rounded, lax.rem(y + k, NY), 0, False), "y", NY, k)
        for k in range(1, NY)
    ]
    total = (total + came[0].astype(F32) + came[1].astype(F32) + came[2].astype(F32)).astype(BF)
    own = jnp.stack([total] + [shift(total, "y", NY, NY - m) for m in range(1, NY)])
    return own, shift(own, "c", NC, 1)


def mix(rows, columns, x, y, c):
    width = columns.shape[1]
    visits = [rows] + [shift(rows, "x", NX, k) for k in range(1, NX)]
    blocks = after(columns, *visits[1:]).reshape(NY, NC, width, CH)
    ours, theirs = (lax.dynamic_index_in_dim(blocks, core, 1, False).reshape(-1, CH) for core in (c, 1 - c))
    pieces = []
    for visit in visits:
        got = shift(bdot_t(visit, theirs).astype(BF), "c", NC, 1)
        pieces.append((bdot_t(visit, ours) + got.astype(F32)).astype(BF))

    def over_y(some):
        def block(s):
            at = lax.rem(y + s, NY) * width
            return [lax.dynamic_slice_in_dim(piece, at, width, 1) for piece in some]

        total = jnp.concatenate(block(0), axis=0).astype(F32)
        for s in range(1, NY):
            total += shift(jnp.concatenate(block(s), axis=0), "y", NY, s).astype(F32)
        return total.astype(BF).reshape(len(some), rows.shape[0], width)

    first, rest = over_y(pieces[:1]), over_y(pieces[1:])
    back = [first[0]] + [shift(rest[k - 1], "x", NX, NX - k) for k in range(1, NX)]
    twice = jnp.stack(back + back)
    ordered = lax.dynamic_slice_in_dim(twice, lax.rem(NX - x, NX), NX, 0)
    return ordered.transpose(1, 0, 2)


def per_device(
    input_steps, gate_steps, conv_state, ssm_state, new_slot, remaining, conv_weight, conv_bias,
    coef_proj, delta_proj, delta_bias, decay_log, skip_gain, out_proj,
):
    z, x, y, c = (lax.axis_index(name) for name in ("z", "x", "y", "c"))
    group = z * NX + x
    me = jnp.stack([group, x, y, c]).astype(I32)
    at, relay, rem, col, ext, buf, block, main, proj = plan(
        me,
        new_slot.reshape(1, -1),
        remaining.reshape(1, -1),
        new_slot.reshape(GROUPS, ROWS),
        conv_state.transpose(1, 0, 2),
        coef_proj.T,
        delta_proj,
        out_proj,
        ssm_state,
    )
    gathered = lax.all_gather(block, "z", axis=0)
    moved = lax.all_to_all(
        buf.reshape(GROUPS, SLOT, CH), ("z", "x"), split_axis=0, concat_axis=0, tiled=True
    ).reshape(GROUPS * SLOT, CH)
    def turned(value):
        return [value] + [shift(value, "x", NX, k) for k in range(1, NX)]

    secs = turned(gathered[:, :SEC].reshape(NZ * SEC, CH))
    ssm_main = lax.all_to_all(
        after(main, moved, *secs[1:]), ("z", "x"), split_axis=0, concat_axis=0, tiled=True
    )
    deltas = turned(gathered[:, SEC:GATH].reshape(NZ * DELTA, CH))
    extras = [
        lax.dynamic_slice(gathered, (relay[k, 0], GATH, 0), (1, BASE * STATE, CH)) for k in range(NX)
    ]
    extras = [extras[0]] + [shift(extras[k], "x", NX, k) for k in range(1, NX)]
    extras = [e.reshape(BASE, STATE, CH) for e in extras]
    act, low, conv_final = conv_stage(
        me, moved, secs, col, ext, rem, input_steps, conv_weight, conv_bias.reshape(1, -1)
    )
    own, other = reduce_mp(low, y, c)
    dt, dx, sk, sg, bc, rate = step_stage(
        me, own, other, deltas, delta_bias.reshape(1, -1), act, gate_steps, skip_gain.reshape(1, -1), rem, decay_log
    )
    columns = lax.all_gather(after(proj, ssm_main, rate), "z", axis=0)
    stepped, ssm_final = scan_stage(at, ssm_main, extras, dt, dx, sk, sg, bc, rate)
    mixed = mix(stepped.reshape(STEPS * ROWS, CH), columns, x, y, c)
    return mixed.reshape(STEPS, ROWS, -1), conv_final.transpose(1, 0, 2), ssm_final


def solution(mesh):
    fine = Mesh(mesh.devices.reshape(NZ, NX, NY, NC), ("z", "x", "y", "c"))
    dp, mp = ("z", "x"), ("y", "c")
    return jax.shard_map(
        per_device,
        mesh=fine,
        in_specs=(
            P(None, dp, mp),
            P(None, dp, mp),
            P(dp, None, mp),
            P(dp, None, mp),
            P(),
            P(),
            P(None, mp),
            P(mp),
            P(mp, dp),
            P(dp, mp),
            P(mp),
            P(None, mp),
            P(mp),
            P(mp, dp),
        ),
        out_specs=(P(None, dp, mp), P(dp, None, mp), P(dp, None, mp)),
        check_vma=False,
    )
```
